256 devices in a mesh: wide: 64 (over z_hi, x, y, core), narrow: 4 (over z_lo).
Axes of the slice: x: 4, y: 4, z: 8 (z_hi: 2, z_lo: 4; z = z_hi * 4 + z_lo), core: 2. Of those that a mesh axis runs over, the one named last changes fastest.
Arguments:
- factor_rows: float32 [1, 4, 4, 64, 16, 1024], P(None, 'narrow', None, 'wide'), may hold values from -0.09375 to 0.09375
- load_vectors: float32 [1, 4, 1024, 128], P(None, 'narrow', 'wide'), may hold values from -6 to 6
- child_updates: float32 [4, 1, 4, 1024, 128], P('narrow', None, None, 'wide'), may hold values from -4 to 4
- block_inverses: float32 [4, 1024, 1024], P(None, 'wide'), may hold values from -1 to 2, as said below
Outputs:
- forward_solution: float32 [1, 4, 1024, 128], P(None, 'narrow', 'wide')
The draws below stay inside these ranges and needn't reach their ends.
Inputs may be any that keep to these rules, and one draw needn't show every extreme that they name: Each block of block_inverses has a diagonal between 0.4 and 1.6.
All inputs are finite; a program needn't handle non-finite values.
Results may differ from the reference program's by a relative error of at most 0.0001.
Values sent between devices are 32-bit elements; how exact they have to be, the bound alone decides.
A program may use at most 64 MiB of HBM per device.

```python
import math
import jax
import jax.numpy as jnp
from jax import lax

NB = 1024
BLK_DEV = 1
R = 128
SB = 16
NBLK = 4
FRONT = 4096
KIDS = 4
N_WIDE = 64
N_NARROW = 4


def draw_block_inverses(key, part):
    noise_key, diag_key = jax.random.split(jax.random.fold_in(key, 11))
    shape = (NBLK, NB, NB)
    noise = jax.random.truncated_normal(noise_key, -3.0, 3.0, shape, jnp.float32) * (0.5 / math.sqrt(NB))
    diag_values = jax.random.uniform(diag_key, (NBLK, NB), jnp.float32, 0.5, 1.5)
    identity = jnp.eye(NB, dtype=jnp.float32)
    return noise + identity[None, :, :] * diag_values[:, :, None]


def shard_levels(own_key, dims, pieces, smallest, largest):
    gain = 1.0
    for axis_at, parts in pieces:
        heights = jax.random.uniform(jax.random.fold_in(jax.random.fold_in(own_key, 6), axis_at), (parts,), jnp.float32, smallest / len(pieces), largest / len(pieces))
        gain = gain * jnp.repeat(jnp.exp(heights), dims[axis_at] // parts).reshape((-1,) + (1,) * (len(dims) - 1 - axis_at))
    return gain


def scatter_about(stream_key, extent, deviation, most, shards=(), kind=jnp.bfloat16):
    array = jax.random.normal(stream_key, extent, jnp.float32) * deviation
    if len(shards) > 0:
        array = shard_levels(stream_key, extent, shards, -0.22, 0.18) * array
    return jnp.clip(array, min=-most, max=most).astype(kind)


def setup_inputs(seed: int = 0) -> dict:
    key_of = jax.random.split(jax.random.key(seed), 5)
    factor_rows = scatter_about(key_of[0], (BLK_DEV, N_NARROW, NBLK, N_WIDE, SB, NB), FRONT ** -0.5, 0.09375, ((1, 4), (3, 64)), jnp.float32)
    load_vectors = scatter_about(key_of[1], (BLK_DEV, N_NARROW, NB, R), 1.0, 6.0, ((1, 4), (2, 64)), jnp.float32)
    child_updates = scatter_about(key_of[2], (KIDS, BLK_DEV, N_NARROW, NB, R), 0.5, 4.0, ((0, 4), (3, 64)), jnp.float32)
    block_inverses = draw_block_inverses(jax.random.fold_in(key_of[4], 71), 0)
    return dict(factor_rows=factor_rows, load_vectors=load_vectors, child_updates=child_updates, block_inverses=block_inverses)


def reference(factor_rows, load_vectors, child_updates, block_inverses):
    panels = factor_rows.reshape(NBLK, NBLK, NB, NB)
    kid_total = jnp.sum(child_updates, axis=0).reshape(NBLK, NB, R)
    given_part = load_vectors.reshape(NBLK, NB, R) - kid_total
    solved = []
    for block_index in range(NBLK):
        reduced = jnp.zeros((NB, R), jnp.float32)
        if block_index > 0:
            earlier = jnp.stack(solved)
            reduced = jnp.einsum("cqr,cqk->rk", panels[block_index, :block_index], earlier,
                                 precision=lax.Precision.HIGHEST)
        newest = jnp.dot(block_inverses[block_index], given_part[block_index] - reduced,
                         precision=lax.Precision.HIGHEST, preferred_element_type=jnp.float32)
        solved.append(newest)
    return jnp.stack(solved).reshape(BLK_DEV, N_NARROW, NB, R)
```

```python
import jax
import jax.numpy as jnp
from jax import lax
from jax.experimental import pallas as pl
from jax.experimental.pallas import tpu as pltpu
from jax.sharding import PartitionSpec as P

MESH = pl.DeviceIdType.MESH
F32, BF16 = jnp.float32, jnp.bfloat16


def kernel(inv_ref, fac_ref, load_ref, child_ref, out_ref,
           kid_v, load_v, stage, staged, p0_buf, p1_src, p1_buf, g_all,
           x_src, x_buf, y_src, y_buf, inv_buf, w_inv, l_buf, w_l, y_hl,
           spread, o_src, o_buf, f_buf,
           loc_sem, p0_sem, p1_sem, x_sem, y_sem, i1_sem, i2_s, i2_r, l1_s, l1_r, l2_s, l2_r,
           o_s, o_r):
    w = lax.axis_index("wide")
    n = lax.axis_index("narrow")
    c = lax.rem(w, 2)
    y = lax.rem(w // 2, 4)
    x = lax.rem(w // 8, 4)
    zh = w // 32
    z = zh * 4 + n
    yc = y * 2 + c

    def dev(zh_, x_, y_, c_, n_):
        return {"wide": ((zh_ * 4 + x_) * 4 + y_) * 2 + c_, "narrow": n_}

    def zdev(z_):
        return dev(z_ // 4, x, y, c, lax.rem(z_, 4))

    def send(src, dst, s_sem, r_sem, to):
        pltpu.make_async_remote_copy(src_ref=src, dst_ref=dst, send_sem=s_sem, recv_sem=r_sem,
                                     device_id=to, device_id_type=MESH).start()

    def settle(like, sem):
        pltpu.make_async_copy(like, like, sem).wait()

    ring = [(2, 0), (2, 1), (1, 0), (1, 1), (3, 0), (3, 1), (0, 1)]

    barrier = pltpu.get_barrier_semaphore()
    for d in (4, 3, 5, 2, 6, 1, 7):
        pl.semaphore_signal(barrier, inc=1, device_id=zdev(lax.rem(z + d, 8)), device_id_type=MESH)
    for d, e in ring:
        pl.semaphore_signal(barrier, inc=1, device_id=dev(zh, x, lax.rem(y + d, 4), lax.rem(c + e, 2), n),
                            device_id_type=MESH)
    for d, e in ring[:-1]:
        pl.semaphore_signal(barrier, inc=1, device_id=dev(zh, lax.rem(x + d, 4), y, lax.rem(c + e, 2), n),
                            device_id_type=MESH)

    kid_in = pltpu.make_async_copy(child_ref, kid_v, loc_sem.at[0])
    load_in = pltpu.make_async_copy(load_ref, load_v, loc_sem.at[1])
    kid_in.start()
    load_in.start()
    own_inv = [pltpu.make_async_copy(inv_ref.at[:, :, pl.ds(pl.multiple_of(h * 512 + x * 128, 128), 128)],
                                     inv_buf.at[:, h, zh * 4 + x], loc_sem.at[2 + h]) for h in range(2)]
    for cp in own_inv:
        cp.start()

    def own_pair(k):
        return (n * (n - 1)) // 2 + k

    def fac_slice(k, x_, c_):
        return fac_ref.at[k, :, pl.ds(pl.multiple_of(c_ * 512 + x_ * 128, 128), 128)]

    def own_fac(k):
        return pltpu.make_async_copy(fac_slice(k, x, c), l_buf.at[own_pair(k), c, zh, x], loc_sem.at[4 + k])

    for k in range(3):
        @pl.when(k < n)
        def _(k=k):
            own_fac(k).start()

    stage[...] = jnp.zeros_like(stage)
    spread[...] = jnp.zeros_like(spread)
    kid_in.wait()
    load_in.wait()

    def window(i):
        return pl.ds(pl.multiple_of(lax.rem(zh * 4 + i + yc, 8) * 16, 16), 16)

    for i in range(4):
        stage[window(i), :] = -kid_v[i]
    stage[window(n), :] = stage[window(n), :] + load_v[...]
    staged[...] = stage[...].T
    p0_buf[z] = staged[pl.ds(pl.multiple_of(z * 16, 16), 16), :]

    pl.semaphore_wait(barrier, 20)

    for d in (4, 3, 5, 2, 6, 1, 7):
        to = lax.rem(z + d, 8)
        send(staged.at[pl.ds(pl.multiple_of(to * 16, 16), 16), :], p0_buf.at[z], p0_sem.at[0], p0_sem.at[1], zdev(to))

    for part in range(2):
        for d in (2, 1, 3):
            xt = lax.rem(x + d, 4)
            for h in range(2):
                cols = pl.ds(pl.multiple_of(h * 512 + xt * 128, 128), 128)
                rows = pl.ds(0, 1) if part == 0 else pl.ds(1, 3)
                send(inv_ref.at[rows, :, cols], inv_buf.at[rows, h, zh * 4 + x], i1_sem.at[0, part], i1_sem.at[1, part],
                     dev(zh, xt, y, c, n))
    for k in range(3):
        @pl.when(k < n)
        def _(k=k):
            for d, e in ring:
                xt, ct = lax.rem(x + d, 4), lax.rem(c + e, 2)
                send(fac_slice(k, xt, ct), l_buf.at[own_pair(k), c, zh, x], l1_s.at[k], l1_r.at[k], dev(zh, xt, y, ct, n))

    def forward_inverse(i):
        mine = inv_buf.at[i, :, pl.ds(pl.multiple_of(zh * 4, 4), 4)]
        for side in range(2):
            @pl.when(n == 3 * side)
            def _():
                for m in range(2):
                    send(mine, mine, i2_s, i2_r.at[i], dev(1 - zh, x, y, c, 2 - 2 * side + m))

    for cp in own_inv:
        cp.wait()
    settle(inv_buf.at[0, :, pl.ds(0, 3)], i1_sem.at[1, 0])
    forward_inverse(0)

    settle(p0_buf.at[pl.ds(0, 7)], p0_sem.at[1])
    own = p0_buf[0]
    for k in range(1, 8):
        own = own + p0_buf[k]
    p1_src[...] = own
    p1_buf[yc] = own
    for d, e in ring:
        send(p1_src, p1_buf.at[yc], p1_sem.at[0], p1_sem.at[1], dev(zh, x, lax.rem(y + d, 4), lax.rem(c + e, 2), n))

    def forward_factor(i):
        @pl.when(n == i)
        def _():
            for k in range(i):
                own_fac(k).wait()
                settle(y_buf.at[0, pl.ds(0, 7)], l1_r.at[k])
                mine = l_buf.at[i * (i - 1) // 2 + k, :, zh]
                for d in (4, 3, 5, 2, 6, 1, 7):
                    send(mine, mine, l2_s.at[k], l2_r.at[i * (i - 1) // 2 + k], zdev(lax.rem(z + d, 8)))

    forward_factor(1)
    settle(inv_buf.at[pl.ds(1, 3), :, pl.ds(0, 3)], i1_sem.at[1, 1])
    forward_inverse(1)

    def split(v):
        hi = v.astype(BF16)
        return hi, (v - hi.astype(F32)).astype(BF16)

    def prepare_inverse(i):
        settle(inv_buf.at[i, :, pl.ds(0, 4)], i2_r.at[i])
        for h in range(2):
            hi, lo = split(inv_buf[i, h].reshape(128, 128))
            w_inv[i, 0:128, h * 128:(h + 1) * 128] = hi
            w_inv[i, 128:256, h * 128:(h + 1) * 128] = lo

    def prepare_factor(i, k):
        pair = i * (i - 1) // 2 + k

        @pl.when(n == i)
        def _():
            settle(l_buf.at[pair, :, 0], l2_r.at[pair])

        @pl.when(n != i)
        def _():
            settle(l_buf.at[pair], l2_r.at[pair])
        hi, lo = split(l_buf[pair].reshape(256, 128))
        w_l[pair, :, 0:128] = hi
        w_l[pair, :, 128:256] = lo

    def fold(d):
        return (d[0:16, 0:128] + d[16:32, 128:256]) + (d[0:16, 128:256] + d[16:32, 0:128])

    def stacked(v):
        hi, lo = split(v)
        return jnp.concatenate([hi, lo], axis=0)

    def apply_inverse(i, r):
        return fold(lax.dot_general(stacked(r), w_inv[i], (((1,), (1,)), ((), ())), preferred_element_type=F32))

    def apply_factor(i, k):
        pair = i * (i - 1) // 2 + k
        return fold(jnp.dot(y_hl[k], w_l[pair], preferred_element_type=F32))

    def spread_cases(piece):
        at = pl.ds(pl.multiple_of(z * 16, 16), 16)
        spread[at, :] = piece
        return spread[...].T

    def send_x(i, partial):
        x_src[i] = partial
        x_buf[i, c * 4 + x] = partial
        for d, e in ring:
            send(x_src.at[i], x_buf.at[i, c * 4 + x], x_sem.at[0, i], x_sem.at[1, i],
                 dev(zh, lax.rem(x + d, 4), y, lax.rem(c + e, 2), n))

    def send_y(i, partial):
        y_src[i] = partial
        y_buf[i, c * 4 + y] = partial
        for d, e in ring:
            send(y_src.at[i], y_buf.at[i, c * 4 + y], y_sem.at[0, i], y_sem.at[1, i],
                 dev(zh, x, lax.rem(y + d, 4), lax.rem(c + e, 2), n))

    def halves(buf, i):
        return [(buf[i, 4 * h] + buf[i, 4 * h + 1]) + (buf[i, 4 * h + 2] + buf[i, 4 * h + 3]) for h in range(2)]

    def solved_parts(i):
        settle(x_buf.at[i, pl.ds(0, 7)], x_sem.at[1, i])
        parts = halves(x_buf, i)
        y_hl[i] = stacked(jnp.concatenate(parts, axis=1))
        return parts

    def send_out(i, parts):
        o_src[i] = spread_cases(jnp.where(c == 0, parts[0], parts[1]))
        for g in range(2):
            rows = o_src.at[i, pl.ds(pl.multiple_of((g * 4 + x) * 16, 16), 16), :]
            own_place = jnp.logical_and(n == i, zh == g)

            @pl.when(own_place)
            def _():
                o_buf[z] = o_src[i, pl.ds(pl.multiple_of((g * 4 + x) * 16, 16), 16), :]

            @pl.when(jnp.logical_not(own_place))
            def _():
                send(rows, o_buf.at[z], o_s.at[i], o_r.at[0], dev(g, x, y, c, i))

    prepare_inverse(0)
    settle(p1_buf.at[pl.ds(0, 7)], p1_sem.at[1])
    lane_window = lax.broadcasted_iota(jnp.int32, (16, 128), 1) // 16

    def gathered(i):
        for h in range(2):
            first = h * 4 + i
            v = p1_buf[0]
            for k in range(1, 8):
                v = jnp.where(lane_window == (first + k) % 8, p1_buf[k], v)
            if first:
                v = pltpu.roll(v, 128 - first * 16, 1)
            g_all[i, :, h * 128:(h + 1) * 128] = v

    gathered(0)
    send_x(0, apply_inverse(0, g_all[0]))
    forward_factor(2)
    forward_inverse(2)
    for i in range(1, 4):
        gathered(i)
    prepare_factor(1, 0)
    parts = solved_parts(0)

    for i in range(1, 4):
        ahead = None
        for k in range(i - 1):
            term = apply_factor(i, k)
            ahead = term if ahead is None else ahead + term
        last = apply_factor(i, i - 1)
        send_y(i - 1, last if ahead is None else ahead + last)
        send_out(i - 1, parts)
        prepare_inverse(i)
        if i == 1:
            forward_factor(3)
            forward_inverse(3)
        if i < 3:
            for k in range(i + 1):
                prepare_factor(i + 1, k)
        settle(y_buf.at[i - 1, pl.ds(0, 7)], y_sem.at[1, i - 1])
        sums = halves(y_buf, i - 1)
        partial = apply_inverse(i, g_all[i] - jnp.concatenate(sums, axis=1))
        if i < 3:
            send_x(i, partial)
            parts = solved_parts(i)

    o_src[3] = spread_cases(partial)
    for g in range(2):
        for d in (2, 1, 3, 0):
            xt = lax.rem(x + d, 4)
            at = pl.ds(pl.multiple_of((g * 4 + xt) * 16, 16), 16)
            if d:
                send(o_src.at[3, at, :], f_buf.at[z * 4 + x], o_s.at[3], o_r.at[1], dev(g, xt, y, c, 3))
            else:
                own_place = jnp.logical_and(n == 3, zh == g)

                @pl.when(own_place)
                def _():
                    f_buf[z * 4 + x] = o_src[3, at, :]

                @pl.when(jnp.logical_not(own_place))
                def _():
                    send(o_src.at[3, at, :], f_buf.at[z * 4 + x], o_s.at[3], o_r.at[1], dev(g, xt, y, c, 3))

    settle(p0_buf.at[pl.ds(0, 7)], p0_sem.at[0])
    settle(p1_buf.at[pl.ds(0, 7)], p1_sem.at[0])
    for i in range(3):
        settle(x_buf.at[i, pl.ds(0, 7)], x_sem.at[0, i])
        settle(y_buf.at[i, pl.ds(0, 7)], y_sem.at[0, i])
    settle(inv_buf.at[0, :, pl.ds(0, 3)], i1_sem.at[0, 0])
    settle(inv_buf.at[pl.ds(1, 3), :, pl.ds(0, 3)], i1_sem.at[0, 1])

    @pl.when(jnp.logical_or(n == 0, n == 3))
    def _():
        settle(inv_buf, i2_s)

    for k in range(3):
        @pl.when(k < n)
        def _(k=k):
            settle(y_buf.at[0, pl.ds(0, 7)], l1_s.at[k])
            settle(inv_buf.at[:, :, pl.ds(0, 7)], l2_s.at[k])

    for i in range(4):
        count = 2 if i < 3 else 8

        @pl.when(n == i)
        def _(i=i, count=count):
            settle(f_buf.at[pl.ds(0, count - 1)], o_s.at[i])

        @pl.when(n != i)
        def _(i=i, count=count):
            settle(f_buf.at[pl.ds(0, count)], o_s.at[i])

    @pl.when(n < 3)
    def _():
        settle(o_buf.at[pl.ds(0, 7)], o_r.at[0])
        total = o_buf[0]
        for k in range(1, 8):
            total = total + o_buf[k]
        out_ref[...] = total

    @pl.when(n == 3)
    def _():
        settle(f_buf.at[pl.ds(0, 31)], o_r.at[1])
        total = f_buf[0]
        for k in range(1, 32):
            total = total + f_buf[k]
        out_ref[...] = total


def body(factor_rows, load_vectors, child_updates, block_inverses):
    dma = pltpu.SemaphoreType.DMA
    out = pl.pallas_call(
        kernel,
        out_shape=jax.ShapeDtypeStruct((16, 128), F32),
        in_specs=[pl.BlockSpec(memory_space=pl.ANY)] * 4,
        out_specs=pl.BlockSpec(memory_space=pltpu.VMEM),
        scratch_shapes=[
            pltpu.VMEM((4, 16, 128), F32), pltpu.VMEM((16, 128), F32),
            pltpu.VMEM((128, 128), F32), pltpu.VMEM((128, 128), F32),
            pltpu.VMEM((8, 16, 128), F32), pltpu.VMEM((16, 128), F32), pltpu.VMEM((8, 16, 128), F32),
            pltpu.VMEM((4, 16, 256), F32),
            pltpu.VMEM((3, 16, 128), F32), pltpu.VMEM((3, 8, 16, 128), F32),
            pltpu.VMEM((3, 16, 128), F32), pltpu.VMEM((3, 8, 16, 128), F32),
            pltpu.VMEM((4, 2, 8, 16, 128), F32), pltpu.VMEM((4, 256, 256), BF16),
            pltpu.VMEM((6, 2, 2, 4, 16, 128), F32), pltpu.VMEM((6, 256, 256), BF16),
            pltpu.VMEM((3, 32, 256), BF16),
            pltpu.VMEM((128, 128), F32), pltpu.VMEM((4, 128, 128), F32),
            pltpu.VMEM((8, 16, 128), F32), pltpu.VMEM((32, 16, 128), F32),
            dma((7,)), dma((2,)), dma((2,)), dma((2, 3)), dma((2, 3)), dma((2, 2)),
            dma, dma((4,)), dma((3,)), dma((3,)), dma((3,)), dma((6,)), dma((4,)), dma((2,)),
        ],
        compiler_params=pltpu.CompilerParams(collective_id=0, has_side_effects=True, vmem_limit_bytes=24 << 20),
        name="substitution",
    )(
        block_inverses,
        factor_rows.reshape(4, 16, 1024),
        load_vectors.reshape(16, 128),
        child_updates.reshape(4, 16, 128),
    )
    return out.reshape(1, 1, 16, 128)


def solution(mesh):
    placed = (
        P(None, "narrow", None, "wide", None, None),
        P(None, "narrow", "wide", None),
        P("narrow", None, None, "wide", None),
        P(None, "wide", None),
    )
    return jax.shard_map(
        body, mesh=mesh, in_specs=placed, out_specs=P(None, "narrow", "wide", None), check_vma=False
    )
```

```python
import jax
import jax.numpy as jnp
from jax import lax
from jax.experimental import pallas as pl
from jax.experimental.pallas import tpu as pltpu
from jax.sharding import PartitionSpec as P

MESH = pl.DeviceIdType.MESH
F32, BF16 = jnp.float32, jnp.bfloat16


def kernel(inv_ref, fac_ref, load_ref, child_ref, out_ref,
           kid_v, load_v, stage, staged, p0_buf, p1_src, p1_buf, g_all,
           x_src, x_buf, y_src, y_buf, inv_buf, w_inv, l_buf, w_l, y_hl,
           spread, o_src, o_buf, f_buf,
           loc_sem, p0_sem, p1_sem, x_sem, y_sem, i1_sem, i2_s, i2_r, l1_s, l1_r, l2_s, l2_r, l3_s,
           o_s, o_r):
    w = lax.axis_index("wide")
    n = lax.axis_index("narrow")
    c = lax.rem(w, 2)
    y = lax.rem(w // 2, 4)
    x = lax.rem(w // 8, 4)
    zh = w // 32
    z = zh * 4 + n
    yc = y * 2 + c

    def dev(zh_, x_, y_, c_, n_):
        return {"wide": ((zh_ * 4 + x_) * 4 + y_) * 2 + c_, "narrow": n_}

    def zdev(z_):
        return dev(z_ // 4, x, y, c, lax.rem(z_, 4))

    def send(src, dst, s_sem, r_sem, to):
        pltpu.make_async_remote_copy(src_ref=src, dst_ref=dst, send_sem=s_sem, recv_sem=r_sem,
                                     device_id=to, device_id_type=MESH).start()

    def settle(like, sem):
        pltpu.make_async_copy(like, like, sem).wait()

    ring = [(2, 0), (2, 1), (1, 0), (1, 1), (3, 0), (3, 1), (0, 1)]

    barrier = pltpu.get_barrier_semaphore()
    for d in (4, 3, 5, 2, 6, 1, 7):
        pl.semaphore_signal(barrier, inc=1, device_id=zdev(lax.rem(z + d, 8)), device_id_type=MESH)
    for d, e in ring:
        pl.semaphore_signal(barrier, inc=1, device_id=dev(zh, x, lax.rem(y + d, 4), lax.rem(c + e, 2), n),
                            device_id_type=MESH)
    for d, e in ring[:-1]:
        pl.semaphore_signal(barrier, inc=1, device_id=dev(zh, lax.rem(x + d, 4), y, lax.rem(c + e, 2), n),
                            device_id_type=MESH)

    kid_in = pltpu.make_async_copy(child_ref, kid_v, loc_sem.at[0])
    load_in = pltpu.make_async_copy(load_ref, load_v, loc_sem.at[1])
    kid_in.start()
    load_in.start()
    own_inv = [pltpu.make_async_copy(inv_ref.at[:, :, pl.ds(pl.multiple_of(h * 512 + x * 128, 128), 128)],
                                     inv_buf.at[:, h, zh * 4 + x], loc_sem.at[2 + h]) for h in range(2)]
    for cp in own_inv:
        cp.start()

    def own_pair(k):
        return (n * (n - 1)) // 2 + k

    def fac_slice(k, x_, c_):
        return fac_ref.at[k, :, pl.ds(pl.multiple_of(c_ * 512 + x_ * 128, 128), 128)]

    def own_fac(k):
        return pltpu.make_async_copy(fac_slice(k, x, c), l_buf.at[own_pair(k), c, zh, x], loc_sem.at[4 + k])

    for k in range(3):
        @pl.when(k < n)
        def _(k=k):
            own_fac(k).start()

    stage[...] = jnp.zeros_like(stage)
    spread[...] = jnp.zeros_like(spread)
    kid_in.wait()
    load_in.wait()

    def window(i):
        return pl.ds(pl.multiple_of(lax.rem(zh * 4 + i + yc, 8) * 16, 16), 16)

    for i in range(4):
        stage[window(i), :] = -kid_v[i]
    stage[window(n), :] = stage[window(n), :] + load_v[...]
    staged[...] = stage[...].T
    p0_buf[z] = staged[pl.ds(pl.multiple_of(z * 16, 16), 16), :]

    pl.semaphore_wait(barrier, 20)

    for d in (4, 3, 5, 2, 6, 1, 7):
        to = lax.rem(z + d, 8)
        send(staged.at[pl.ds(pl.multiple_of(to * 16, 16), 16), :], p0_buf.at[z], p0_sem.at[0], p0_sem.at[1], zdev(to))

    def start_weights():
        for part in range(2):
            for d in (2, 1, 3):
                xt = lax.rem(x + d, 4)
                for h in range(2):
                    cols = pl.ds(pl.multiple_of(h * 512 + xt * 128, 128), 128)
                    rows = pl.ds(0, 1) if part == 0 else pl.ds(1, 3)
                    send(inv_ref.at[rows, :, cols], inv_buf.at[rows, h, zh * 4 + x], i1_sem.at[0, part], i1_sem.at[1, part],
                         dev(zh, xt, y, c, n))
        for k in range(3):
            @pl.when(k < n)
            def _(k=k):
                for d, e in ring:
                    xt, ct = lax.rem(x + d, 4), lax.rem(c + e, 2)
                    send(fac_slice(k, xt, ct), l_buf.at[own_pair(k), c, zh, x], l1_s.at[k], l1_r.at[k], dev(zh, xt, y, ct, n))

    start_weights()

    def arrived_inverse(part):
        settle(inv_buf.at[pl.ds(part, 1 + 2 * part), :, pl.ds(0, 3)], i1_sem.at[1, part])

    def forward_inverse(i, both):
        mine = inv_buf.at[i, :, pl.ds(pl.multiple_of(zh * 4, 4), 4)]
        for side in range(2):
            @pl.when(n == 3 * side)
            def _(side=side):
                send(mine, mine, i2_s, i2_r.at[i], dev(1 - zh, x, y, c, 3 - 3 * side))
                if both:
                    send(mine, mine, i2_s, i2_r.at[i], dev(1 - zh, x, y, c, 2 - side))

    def relay_inverse(i):
        other = inv_buf.at[i, :, pl.ds(pl.multiple_of(4 - zh * 4, 4), 4)]

        @pl.when(jnp.logical_or(n == 0, n == 3))
        def _():
            settle(inv_buf.at[i, :, pl.ds(0, 4)], i2_r.at[i])
        for side in range(2):
            @pl.when(n == 3 * side)
            def _(side=side):
                send(other, other, i2_s, i2_r.at[i], dev(zh, x, y, c, 1 + side))

    for cp in own_inv:
        cp.wait()
    arrived_inverse(0)
    forward_inverse(0, True)

    settle(p0_buf.at[pl.ds(0, 7)], p0_sem.at[1])
    own = p0_buf[0]
    for k in range(1, 8):
        own = own + p0_buf[k]
    p1_src[...] = own
    p1_buf[yc] = own
    for d, e in ring:
        send(p1_src, p1_buf.at[yc], p1_sem.at[0], p1_sem.at[1], dev(zh, x, lax.rem(y + d, 4), lax.rem(c + e, 2), n))

    def forward_factor(i):
        @pl.when(n == i)
        def _():
            for k in range(i):
                own_fac(k).wait()
                settle(y_buf.at[0, pl.ds(0, 7)], l1_r.at[k])
                mine = l_buf.at[i * (i - 1) // 2 + k, :, zh]
                for d in (2, 6, 1, 7):
                    send(mine, mine, l2_s.at[k], l2_r.at[i * (i - 1) // 2 + k], zdev(lax.rem(z + d, 8)))

    def relay_factor(i):
        @pl.when(n == (i + 2) % 4)
        def _():
            for k in range(i):
                pair = i * (i - 1) // 2 + k
                settle(l_buf.at[pair], l2_r.at[pair])
                for d in (1, 7):
                    origin = lax.rem(z + (6 if d == 1 else 2), 8) // 4
                    held = l_buf.at[pair, :, origin]
                    send(held, held, l3_s.at[k], l2_r.at[pair], zdev(lax.rem(z + d, 8)))

                    @pl.when(c == d // 7)
                    def _(d=d, held=held):
                        send(held, held, l3_s.at[k], l2_r.at[pair], zdev(lax.rem(z + (2 if d == 1 else 6), 8)))

    forward_factor(1)
    forward_factor(2)
    arrived_inverse(1)
    forward_inverse(1, False)

    def split(v):
        hi = v.astype(BF16)
        return hi, (v - hi.astype(F32)).astype(BF16)

    def prepare_inverse(i):
        if i == 0:
            settle(inv_buf.at[i, :, pl.ds(0, 4)], i2_r.at[i])
        else:
            @pl.when(jnp.logical_and(n != 0, n != 3))
            def _():
                settle(inv_buf.at[i, :, pl.ds(0, 4)], i2_r.at[i])
        for h in range(2):
            hi, lo = split(inv_buf[i, h].reshape(128, 128))
            w_inv[i, 0:128, h * 128:(h + 1) * 128] = hi
            w_inv[i, 128:256, h * 128:(h + 1) * 128] = lo

    def prepare_factor(i, k):
        pair = i * (i - 1) // 2 + k

        @pl.when(n == i)
        def _():
            settle(l_buf.at[pair, :, 0], l2_r.at[pair])

        @pl.when(jnp.logical_and(n != i, n != (i + 2) % 4))
        def _():
            settle(l_buf.at[pair], l2_r.at[pair])
        hi, lo = split(l_buf[pair].reshape(256, 128))
        w_l[pair, :, 0:128] = hi
        w_l[pair, :, 128:256] = lo

    def fold(d):
        return (d[0:16, 0:128] + d[16:32, 128:256]) + (d[0:16, 128:256] + d[16:32, 0:128])

    def stacked(v):
        hi, lo = split(v)
        return jnp.concatenate([hi, lo], axis=0)

    def apply_inverse(i, r):
        return fold(lax.dot_general(stacked(r), w_inv[i], (((1,), (1,)), ((), ())), preferred_element_type=F32))

    def apply_factor(i, k):
        pair = i * (i - 1) // 2 + k
        return fold(jnp.dot(y_hl[k], w_l[pair], preferred_element_type=F32))

    def spread_cases(piece):
        at = pl.ds(pl.multiple_of(z * 16, 16), 16)
        spread[at, :] = piece
        return spread[...].T

    def send_x(i, partial):
        x_src[i] = partial
        x_buf[i, c * 4 + x] = partial
        for d, e in ring:
            send(x_src.at[i], x_buf.at[i, c * 4 + x], x_sem.at[0, i], x_sem.at[1, i],
                 dev(zh, lax.rem(x + d, 4), y, lax.rem(c + e, 2), n))

    def send_y(i, partial):
        y_src[i] = partial
        y_buf[i, c * 4 + y] = partial
        for d, e in ring:
            send(y_src.at[i], y_buf.at[i, c * 4 + y], y_sem.at[0, i], y_sem.at[1, i],
                 dev(zh, x, lax.rem(y + d, 4), lax.rem(c + e, 2), n))

    def halves(buf, i):
        return [(buf[i, 4 * h] + buf[i, 4 * h + 1]) + (buf[i, 4 * h + 2] + buf[i, 4 * h + 3]) for h in range(2)]

    def solved_parts(i):
        settle(x_buf.at[i, pl.ds(0, 7)], x_sem.at[1, i])
        parts = halves(x_buf, i)
        y_hl[i] = stacked(jnp.concatenate(parts, axis=1))
        return parts

    def send_out(i, parts):
        o_src[i] = spread_cases(jnp.where(c == 0, parts[0], parts[1]))
        for g in range(2):
            rows = o_src.at[i, pl.ds(pl.multiple_of((g * 4 + x) * 16, 16), 16), :]
            own_place = jnp.logical_and(n == i, zh == g)

            @pl.when(own_place)
            def _():
                o_buf[z] = o_src[i, pl.ds(pl.multiple_of((g * 4 + x) * 16, 16), 16), :]

            @pl.when(jnp.logical_not(own_place))
            def _():
                send(rows, o_buf.at[z], o_s.at[i], o_r.at[0], dev(g, x, y, c, i))

    prepare_inverse(0)
    settle(p1_buf.at[pl.ds(0, 7)], p1_sem.at[1])
    lane_window = lax.broadcasted_iota(jnp.int32, (16, 128), 1) // 16

    def gathered(i):
        for h in range(2):
            first = h * 4 + i
            v = p1_buf[0]
            for k in range(1, 8):
                v = jnp.where(lane_window == (first + k) % 8, p1_buf[k], v)
            if first:
                v = pltpu.roll(v, 128 - first * 16, 1)
            g_all[i, :, h * 128:(h + 1) * 128] = v

    gathered(0)
    send_x(0, apply_inverse(0, g_all[0]))
    relay_factor(1)
    forward_factor(3)
    relay_inverse(1)
    for i in range(1, 4):
        gathered(i)
    prepare_factor(1, 0)
    parts = solved_parts(0)

    for i in range(1, 4):
        ahead = None
        for k in range(i - 1):
            term = apply_factor(i, k)
            ahead = term if ahead is None else ahead + term
        last = apply_factor(i, i - 1)
        send_y(i - 1, last if ahead is None else ahead + last)
        send_out(i - 1, parts)
        if i == 1:
            relay_factor(2)
        if i < 3:
            forward_inverse(i + 1, False)
        prepare_inverse(i)
        settle(y_buf.at[i - 1, pl.ds(0, 7)], y_sem.at[1, i - 1])
        sums = halves(y_buf, i - 1)
        partial = apply_inverse(i, g_all[i] - jnp.concatenate(sums, axis=1))
        if i < 3:
            send_x(i, partial)
            relay_inverse(i + 1)
            if i == 1:
                relay_factor(3)
            for k in range(i + 1):
                prepare_factor(i + 1, k)
            parts = solved_parts(i)

    o_src[3] = spread_cases(partial)
    for g in range(2):
        for d in (2, 1, 3, 0):
            xt = lax.rem(x + d, 4)
            at = pl.ds(pl.multiple_of((g * 4 + xt) * 16, 16), 16)
            if d:
                send(o_src.at[3, at, :], f_buf.at[z * 4 + x], o_s.at[3], o_r.at[1], dev(g, xt, y, c, 3))
            else:
                own_place = jnp.logical_and(n == 3, zh == g)

                @pl.when(own_place)
                def _():
                    f_buf[z * 4 + x] = o_src[3, at, :]

                @pl.when(jnp.logical_not(own_place))
                def _():
                    send(o_src.at[3, at, :], f_buf.at[z * 4 + x], o_s.at[3], o_r.at[1], dev(g, xt, y, c, 3))

    def drain_weights():
        settle(inv_buf.at[0, :, pl.ds(0, 3)], i1_sem.at[0, 0])
        settle(inv_buf.at[pl.ds(1, 3), :, pl.ds(0, 3)], i1_sem.at[0, 1])

        @pl.when(jnp.logical_or(n == 0, n == 3))
        def _():
            settle(inv_buf, i2_s)

        for k in range(3):
            @pl.when(k < n)
            def _(k=k):
                settle(y_buf.at[0, pl.ds(0, 7)], l1_s.at[k])
                settle(l_buf.at[pl.ds(0, 2)], l2_s.at[k])

            @pl.when(k < lax.rem(n + 2, 4))
            def _(k=k):
                settle(inv_buf.at[:, :, pl.ds(0, 3)], l3_s.at[k])

    drain_weights()
    settle(p0_buf.at[pl.ds(0, 7)], p0_sem.at[0])
    settle(p1_buf.at[pl.ds(0, 7)], p1_sem.at[0])
    for i in range(3):
        settle(x_buf.at[i, pl.ds(0, 7)], x_sem.at[0, i])
        settle(y_buf.at[i, pl.ds(0, 7)], y_sem.at[0, i])

    for i in range(4):
        count = 2 if i < 3 else 8

        @pl.when(n == i)
        def _(i=i, count=count):
            settle(f_buf.at[pl.ds(0, count - 1)], o_s.at[i])

        @pl.when(n != i)
        def _(i=i, count=count):
            settle(f_buf.at[pl.ds(0, count)], o_s.at[i])

    @pl.when(n < 3)
    def _():
        settle(o_buf.at[pl.ds(0, 7)], o_r.at[0])
        total = o_buf[0]
        for k in range(1, 8):
            total = total + o_buf[k]
        out_ref[...] = total

    @pl.when(n == 3)
    def _():
        settle(f_buf.at[pl.ds(0, 31)], o_r.at[1])
        total = f_buf[0]
        for k in range(1, 32):
            total = total + f_buf[k]
        out_ref[...] = total


def body(factor_rows, load_vectors, child_updates, block_inverses):
    dma = pltpu.SemaphoreType.DMA
    out = pl.pallas_call(
        kernel,
        out_shape=jax.ShapeDtypeStruct((16, 128), F32),
        in_specs=[pl.BlockSpec(memory_space=pltpu.HBM)] * 4,
        out_specs=pl.BlockSpec(memory_space=pltpu.VMEM),
        scratch_shapes=[
            pltpu.VMEM((4, 16, 128), F32), pltpu.VMEM((16, 128), F32),
            pltpu.VMEM((128, 128), F32), pltpu.VMEM((128, 128), F32),
            pltpu.VMEM((8, 16, 128), F32), pltpu.VMEM((16, 128), F32), pltpu.VMEM((8, 16, 128), F32),
            pltpu.VMEM((4, 16, 256), F32),
            pltpu.VMEM((3, 16, 128), F32), pltpu.VMEM((3, 8, 16, 128), F32),
            pltpu.VMEM((3, 16, 128), F32), pltpu.VMEM((3, 8, 16, 128), F32),
            pltpu.VMEM((4, 2, 8, 16, 128), F32), pltpu.VMEM((4, 256, 256), BF16),
            pltpu.VMEM((6, 2, 2, 4, 16, 128), F32), pltpu.VMEM((6, 256, 256), BF16),
            pltpu.VMEM((3, 32, 256), BF16),
            pltpu.VMEM((128, 128), F32), pltpu.VMEM((4, 128, 128), F32),
            pltpu.VMEM((8, 16, 128), F32), pltpu.VMEM((32, 16, 128), F32),
            dma((7,)), dma((2,)), dma((2,)), dma((2, 3)), dma((2, 3)), dma((2, 2)),
            dma, dma((4,)), dma((3,)), dma((3,)), dma((3,)), dma((6,)), dma((3,)), dma((4,)), dma((2,)),
        ],
        compiler_params=pltpu.CompilerParams(collective_id=0, has_side_effects=True, vmem_limit_bytes=60 << 20),
        name="substitution",
    )(
        block_inverses,
        factor_rows.reshape(4, 16, 1024),
        load_vectors.reshape(16, 128),
        child_updates.reshape(4, 16, 128),
    )
    return out.reshape(1, 1, 16, 128)


def solution(mesh):
    placed = (
        P(None, "narrow", None, "wide", None, None),
        P(None, "narrow", "wide", None),
        P("narrow", None, None, "wide", None),
        P(None, "wide", None),
    )
    return jax.shard_map(
        body, mesh=mesh, in_specs=placed, out_specs=P(None, "narrow", "wide", None), check_vma=False
    )
```

```python
import jax
import jax.numpy as jnp
from jax import lax
from jax.experimental import pallas as pl
from jax.experimental.pallas import tpu as pltpu
from jax.sharding import PartitionSpec as P

MESH = pl.DeviceIdType.MESH
F32, BF16 = jnp.float32, jnp.bfloat16

PLAN = {
    "gather": [("f", 1), ("f", 2), ("s", 1), ("d", 1, False)],
    "gather end": [],
    "x0": [("f", 3)],
    "x0 end": [("a", 1), ("j", 1)],
    "y0": [("r", 2), ("i", 2, False)],
    "y0 end": [],
    "x1": [],
    "x1 end": [("j", 2), ("m",), ("r", 3)],
    "y1": [("i", 3, False)],
    "y1 end": [],
    "x2": [],
    "x2 end": [("j", 3)],
    "y2": [],
    "y2 end": [],
}


def kernel(inv_ref, fac_ref, load_ref, child_ref, out_ref,
           kid_v, load_v, stage, staged, p0_buf, p1_src, p1_buf, g_all,
           x_src, x_buf, y_src, y_buf, inv_buf, w_inv, l_buf, w_l, y_hl,
           spread, o_src, o_buf, f_buf, f_src, away_src, away_buf, back_src, back_buf,
           loc_sem, p0_sem, p1_sem, x_sem, y_sem, i1_sem, i2_s, i2_r, l1_s, l1_r, l2_s, l2_r, l3_s, away_sem, back_sem,
           o_s, o_r):
    w = lax.axis_index("wide")
    n = lax.axis_index("narrow")
    c = lax.rem(w, 2)
    y = lax.rem(w // 2, 4)
    x = lax.rem(w // 8, 4)
    zh = w // 32
    z = zh * 4 + n
    yc = y * 2 + c

    def dev(zh_, x_, y_, c_, n_):
        return {"wide": ((zh_ * 4 + x_) * 4 + y_) * 2 + c_, "narrow": n_}

    def zdev(z_):
        return dev(z_ // 4, x, y, c, lax.rem(z_, 4))

    def send(src, dst, s_sem, r_sem, to):
        pltpu.make_async_remote_copy(src_ref=src, dst_ref=dst, send_sem=s_sem, recv_sem=r_sem,
                                     device_id=to, device_id_type=MESH).start()

    def settle(like, sem):
        pltpu.make_async_copy(like, like, sem).wait()

    ring = [(2, 0), (2, 1), (1, 0), (1, 1), (3, 0), (3, 1), (0, 1)]

    barrier = pltpu.get_barrier_semaphore()
    for d in (4, 3, 5, 2, 6, 1, 7):
        pl.semaphore_signal(barrier, inc=1, device_id=zdev(lax.rem(z + d, 8)), device_id_type=MESH)
    for d, e in ring:
        pl.semaphore_signal(barrier, inc=1, device_id=dev(zh, x, lax.rem(y + d, 4), lax.rem(c + e, 2), n),
                            device_id_type=MESH)
    for d, e in ring[:-1]:
        pl.semaphore_signal(barrier, inc=1, device_id=dev(zh, lax.rem(x + d, 4), y, lax.rem(c + e, 2), n),
                            device_id_type=MESH)

    near = jnp.where(n < 2, 3, 0)
    for d in (2, 1, 3):
        pl.semaphore_signal(barrier, inc=1, device_id=dev(1 - zh, lax.rem(x + d, 4), y, c, near), device_id_type=MESH)
    at_end = jnp.logical_or(n == 0, n == 3)

    kid_in = pltpu.make_async_copy(child_ref, kid_v, loc_sem.at[0])
    load_in = pltpu.make_async_copy(load_ref, load_v, loc_sem.at[1])
    kid_in.start()
    load_in.start()
    own_inv = [pltpu.make_async_copy(inv_ref.at[:, :, pl.ds(pl.multiple_of(h * 512 + x * 128, 128), 128)],
                                     inv_buf.at[:, h, zh * 4 + x], loc_sem.at[2 + h]) for h in range(2)]
    for cp in own_inv:
        cp.start()

    def own_pair(k):
        return (n * (n - 1)) // 2 + k

    def fac_slice(k, x_, c_):
        return fac_ref.at[k, :, pl.ds(pl.multiple_of(c_ * 512 + x_ * 128, 128), 128)]

    def own_fac(k):
        return pltpu.make_async_copy(fac_slice(k, x, c), l_buf.at[own_pair(k), c, zh, x], loc_sem.at[4 + k])

    for k in range(3):
        @pl.when(k < n)
        def _(k=k):
            own_fac(k).start()

    stage[...] = jnp.zeros_like(stage)
    spread[...] = jnp.zeros_like(spread)
    kid_in.wait()
    load_in.wait()

    def window(i):
        return pl.ds(pl.multiple_of(lax.rem(zh * 4 + i + yc, 8) * 16, 16), 16)

    for i in range(4):
        stage[window(i), :] = -kid_v[i]
    stage[window(n), :] = stage[window(n), :] + load_v[...]
    staged[...] = stage[...].T
    p0_buf[z] = staged[pl.ds(pl.multiple_of(z * 16, 16), 16), :]

    @pl.when(at_end)
    def _():
        pl.semaphore_wait(barrier, 26)

    @pl.when(jnp.logical_not(at_end))
    def _():
        pl.semaphore_wait(barrier, 20)

    for d in (4, 3, 5, 2, 6, 1, 7):
        to = lax.rem(z + d, 8)
        send(staged.at[pl.ds(pl.multiple_of(to * 16, 16), 16), :], p0_buf.at[z], p0_sem.at[0], p0_sem.at[1], zdev(to))

    def start_inverse(part):
        for d in (2, 1, 3):
            xt = lax.rem(x + d, 4)
            for h in range(2):
                cols = pl.ds(pl.multiple_of(h * 512 + xt * 128, 128), 128)
                rows = pl.ds(0, 1) if part == 0 else pl.ds(1, 3)
                send(inv_ref.at[rows, :, cols], inv_buf.at[rows, h, zh * 4 + x], i1_sem.at[0, part], i1_sem.at[1, part],
                     dev(zh, xt, y, c, n))

    def start_factor():
        for k in range(3):
            @pl.when(k < n)
            def _(k=k):
                for d, e in ring:
                    xt, ct = lax.rem(x + d, 4), lax.rem(c + e, 2)
                    send(fac_slice(k, xt, ct), l_buf.at[own_pair(k), c, zh, x], l1_s.at[k], l1_r.at[k],
                         dev(zh, xt, y, ct, n))

    def direct_inverse(i, both):
        for side in range(2):
            @pl.when(n == 3 * side)
            def _(side=side):
                for d in (2, 1, 3, 0):
                    xt = lax.rem(x + d, 4)
                    for h in range(2):
                        cols = pl.ds(pl.multiple_of(h * 512 + xt * 128, 128), 128)
                        for lane in ((3 - 3 * side, 2 - side) if both else (3 - 3 * side,)):
                            send(inv_ref.at[i, :, cols], inv_buf.at[i, h, zh * 4 + x], i2_s, i2_r.at[i],
                                 dev(1 - zh, xt, y, c, lane))

    direct_inverse(0, True)
    start_inverse(0)
    start_factor()

    def arrived_inverse(part):
        settle(inv_buf.at[pl.ds(part, 1 + 2 * part), :, pl.ds(0, 3)], i1_sem.at[1, part])

    def forward_inverse(i, both):
        mine = inv_buf.at[i, :, pl.ds(pl.multiple_of(zh * 4, 4), 4)]
        for side in range(2):
            @pl.when(n == 3 * side)
            def _(side=side):
                send(mine, mine, i2_s, i2_r.at[i], dev(1 - zh, x, y, c, 3 - 3 * side))
                if both:
                    send(mine, mine, i2_s, i2_r.at[i], dev(1 - zh, x, y, c, 2 - side))

    def relay_inverse(i):
        other = inv_buf.at[i, :, pl.ds(pl.multiple_of(4 - zh * 4, 4), 4)]

        @pl.when(jnp.logical_or(n == 0, n == 3))
        def _():
            settle(inv_buf.at[i, :, pl.ds(0, 4)], i2_r.at[i])
        for side in range(2):
            @pl.when(n == 3 * side)
            def _(side=side):
                send(other, other, i2_s, i2_r.at[i], dev(zh, x, y, c, 1 + side))

    for cp in own_inv:
        cp.wait()
    arrived_inverse(0)

    settle(p0_buf.at[pl.ds(0, 7)], p0_sem.at[1])
    own = p0_buf[0]
    for k in range(1, 8):
        own = own + p0_buf[k]
    p1_src[...] = own
    p1_buf[yc] = own
    for d, e in ring:
        send(p1_src, p1_buf.at[yc], p1_sem.at[0], p1_sem.at[1], dev(zh, x, lax.rem(y + d, 4), lax.rem(c + e, 2), n))

    def forward_factor(i):
        @pl.when(n == i)
        def _():
            own = range(1, 3) if i == 3 else range(i)
            for k in own:
                own_fac(k).wait()
                settle(y_buf.at[0, pl.ds(0, 7)], l1_r.at[k])
            for ds in (((4, 3, 5, 2, 6, 1, 7),) if i == 1 else ((2, 6), (1, 7))):
                for k in own:
                    pair = i * (i - 1) // 2 + k
                    mine = l_buf.at[pair, :, zh]
                    for d in ds:
                        send(mine, mine, l2_s.at[k], l2_r.at[pair], zdev(lax.rem(z + d, 8)))

    def relay_factor(i):
        @pl.when(n == (i + 2) % 4)
        def _():
            own = range(1, 3) if i == 3 else range(i)
            for k in own:
                pair = i * (i - 1) // 2 + k
                settle(l_buf.at[pair], l2_r.at[pair])
            for far in range(2):
                for k in own:
                    pair = i * (i - 1) // 2 + k
                    for side in range(2):
                        held = l_buf.at[pair, :, lax.rem(z + (2 if side else 6), 8) // 4]
                        hops = 1 + far

                        @pl.when(c == side if far else c < 2)
                        def _(held=held, hops=hops, side=side, k=k, pair=pair):
                            send(held, held, l3_s.at[k], l2_r.at[pair], zdev(lax.rem(z + (8 - hops if side else hops), 8)))

    def send_first(parts):
        for g in range(2):
            piece = jnp.concatenate([p[:, g * 64:(g + 1) * 64] for p in parts], axis=1)
            away_src[g] = piece
            here = jnp.logical_and(n == 3, zh == g)

            @pl.when(here)
            def _(piece=piece):
                away_buf[z] = piece

            @pl.when(jnp.logical_not(here))
            def _(g=g):
                send(away_src.at[g], away_buf.at[z], away_sem.at[0], away_sem.at[1], dev(g, x, y, c, 3))

    def multiply_first():
        @pl.when(n == 3)
        def _():
            own_fac(0).wait()
            settle(y_buf.at[0, pl.ds(0, 7)], l1_r.at[0])
            settle(away_buf.at[pl.ds(0, 7)], away_sem.at[1])
            hi, lo = split(away_buf[...].reshape(128, 128))
            w_hi, w_lo = split(l_buf[3, :, zh].reshape(128, 128))
            d = jnp.dot(jnp.concatenate([hi, lo], axis=0), jnp.concatenate([w_hi, w_lo], axis=1), preferred_element_type=F32)
            back_src[...] = (d[0:128, 0:128] + d[128:256, 128:256]) + (d[0:128, 128:256] + d[128:256, 0:128])
            back_buf[zh] = back_src[pl.ds(pl.multiple_of(z * 16, 16), 16), :]
            for m in (4, 3, 5, 2, 6, 1, 7):
                to = lax.rem(z + m, 8)
                send(back_src.at[pl.ds(pl.multiple_of(to * 16, 16), 16), :], back_buf.at[zh], back_sem.at[0], back_sem.at[1],
                     zdev(to))

    def returned():
        @pl.when(n == 3)
        def _():
            settle(back_buf.at[0], back_sem.at[1])

        @pl.when(n != 3)
        def _():
            settle(back_buf, back_sem.at[1])
        return back_buf[0] + back_buf[1]

    def pass_on(point):
        for what, *args in PLAN[point]:
            {"f": forward_factor, "r": relay_factor, "m": multiply_first, "i": forward_inverse, "j": relay_inverse,
             "a": arrived_inverse, "s": start_inverse, "d": direct_inverse}[what](*args)

    pass_on("gather")

    def split(v):
        hi = v.astype(BF16)
        return hi, (v - hi.astype(F32)).astype(BF16)

    def prepare_inverse(i):
        if i == 0:
            settle(inv_buf.at[i, :, pl.ds(0, 4)], i2_r.at[i])
        else:
            @pl.when(jnp.logical_and(n != 0, n != 3))
            def _():
                settle(inv_buf.at[i, :, pl.ds(0, 4)], i2_r.at[i])
        for h in range(2):
            hi, lo = split(inv_buf[i, h].reshape(128, 128))
            w_inv[i, 0:128, h * 128:(h + 1) * 128] = hi
            w_inv[i, 128:256, h * 128:(h + 1) * 128] = lo

    def prepare_factor(i, k):
        pair = i * (i - 1) // 2 + k

        passes_on = -1 if i == 1 else (i + 2) % 4

        @pl.when(n == i)
        def _():
            settle(l_buf.at[pair, :, 0], l2_r.at[pair])

        @pl.when(jnp.logical_and(n != i, n != passes_on))
        def _():
            settle(l_buf.at[pair], l2_r.at[pair])
        hi, lo = split(l_buf[pair].reshape(256, 128))
        w_l[pair, :, 0:128] = hi
        w_l[pair, :, 128:256] = lo

    def fold(d):
        return (d[0:16, 0:128] + d[16:32, 128:256]) + (d[0:16, 128:256] + d[16:32, 0:128])

    def stacked(v):
        hi, lo = split(v)
        return jnp.concatenate([hi, lo], axis=0)

    def apply_inverse(i, r):
        return fold(lax.dot_general(stacked(r), w_inv[i], (((1,), (1,)), ((), ())), preferred_element_type=F32))

    def apply_factor(i, k):
        pair = i * (i - 1) // 2 + k
        return fold(jnp.dot(y_hl[k], w_l[pair], preferred_element_type=F32))

    def spread_cases(piece):
        at = pl.ds(pl.multiple_of(z * 16, 16), 16)
        spread[at, :] = piece
        return spread[...].T

    def send_x(i, partial):
        x_src[i] = partial
        x_buf[i, c * 4 + x] = partial
        for d, e in ring:
            send(x_src.at[i], x_buf.at[i, c * 4 + x], x_sem.at[0, i], x_sem.at[1, i],
                 dev(zh, lax.rem(x + d, 4), y, lax.rem(c + e, 2), n))

    def send_y(i, partial):
        y_src[i] = partial
        y_buf[i, c * 4 + y] = partial
        for d, e in ring:
            send(y_src.at[i], y_buf.at[i, c * 4 + y], y_sem.at[0, i], y_sem.at[1, i],
                 dev(zh, x, lax.rem(y + d, 4), lax.rem(c + e, 2), n))

    def halves(buf, i):
        return [(buf[i, 4 * h] + buf[i, 4 * h + 1]) + (buf[i, 4 * h + 2] + buf[i, 4 * h + 3]) for h in range(2)]

    def solved_parts(i):
        settle(x_buf.at[i, pl.ds(0, 7)], x_sem.at[1, i])
        parts = halves(x_buf, i)
        y_hl[i] = stacked(jnp.concatenate(parts, axis=1))
        return parts

    def send_out(i, parts):
        o_src[i] = spread_cases(jnp.where(c == 0, parts[0], parts[1]))
        for g in range(2):
            rows = o_src.at[i, pl.ds(pl.multiple_of((g * 4 + x) * 16, 16), 16), :]
            own_place = jnp.logical_and(n == i, zh == g)

            @pl.when(own_place)
            def _():
                o_buf[z] = o_src[i, pl.ds(pl.multiple_of((g * 4 + x) * 16, 16), 16), :]

            @pl.when(jnp.logical_not(own_place))
            def _():
                send(rows, o_buf.at[z], o_s.at[i], o_r.at[0], dev(g, x, y, c, i))

    prepare_inverse(0)
    pass_on("gather end")
    settle(p1_buf.at[pl.ds(0, 7)], p1_sem.at[1])
    lane_window = lax.broadcasted_iota(jnp.int32, (16, 128), 1) // 16

    def gathered(i):
        for h in range(2):
            first = h * 4 + i
            v = p1_buf[0]
            for k in range(1, 8):
                v = jnp.where(lane_window == (first + k) % 8, p1_buf[k], v)
            if first:
                v = pltpu.roll(v, 128 - first * 16, 1)
            g_all[i, :, h * 128:(h + 1) * 128] = v

    gathered(0)
    send_x(0, apply_inverse(0, g_all[0]))
    pass_on("x0")
    for i in range(1, 4):
        gathered(i)
    pass_on("x0 end")
    prepare_factor(1, 0)
    parts = solved_parts(0)

    for i in range(1, 4):
        ahead = returned() if i == 3 else None
        for k in range(1 if i == 3 else 0, i - 1):
            term = apply_factor(i, k)
            ahead = term if ahead is None else ahead + term
        last = apply_factor(i, i - 1)
        send_y(i - 1, last if ahead is None else ahead + last)
        send_out(i - 1, parts)
        if i == 1:
            send_first(parts)
        pass_on(f"y{i - 1}")
        pass_on(f"y{i - 1} end")
        prepare_inverse(i)
        settle(y_buf.at[i - 1, pl.ds(0, 7)], y_sem.at[1, i - 1])
        sums = halves(y_buf, i - 1)
        partial = apply_inverse(i, g_all[i] - jnp.concatenate(sums, axis=1))
        if i < 3:
            send_x(i, partial)
            pass_on(f"x{i}")
            pass_on(f"x{i} end")
            for k in range(1 if i == 2 else 0, i + 1):
                prepare_factor(i + 1, k)
            parts = solved_parts(i)

    low = lax.rem(lax.broadcasted_iota(jnp.int32, (16, 128), 1) // 8, 2) == 0
    spread[pl.ds(pl.multiple_of(z * 16, 16), 16), :] = jnp.where(low, partial, 0.0)
    spread[pl.ds(pl.multiple_of((1 - zh) * 64 + n * 16, 16), 16), :] = jnp.where(low, 0.0, partial)
    wide_rows = spread[...].T.reshape(8, 2, 8, 128)
    f_src[...] = (wide_rows[:, 0] + wide_rows[:, 1]).reshape(64, 128)
    for g in range(2):
        for d in (2, 1, 3, 0):
            xt = lax.rem(x + d, 4)
            at = pl.ds(pl.multiple_of((g * 4 + xt) * 8, 8), 8)
            if d:
                send(f_src.at[at, :], f_buf.at[z * 4 + x], o_s.at[3], o_r.at[1], dev(g, xt, y, c, 3))
            else:
                own_place = jnp.logical_and(n == 3, zh == g)

                @pl.when(own_place)
                def _():
                    f_buf[z * 4 + x] = f_src[at, :]

                @pl.when(jnp.logical_not(own_place))
                def _():
                    send(f_src.at[at, :], f_buf.at[z * 4 + x], o_s.at[3], o_r.at[1], dev(g, xt, y, c, 3))

    def drain_weights():
        settle(inv_buf.at[0, :, pl.ds(0, 3)], i1_sem.at[0, 0])
        settle(inv_buf.at[pl.ds(1, 3), :, pl.ds(0, 3)], i1_sem.at[0, 1])

        @pl.when(jnp.logical_or(n == 0, n == 3))
        def _():
            settle(inv_buf, i2_s)

        for k in range(3):
            @pl.when(k < n)
            def _(k=k):
                settle(y_buf.at[0, pl.ds(0, 7)], l1_s.at[k])

        @pl.when(n == 1)
        def _():
            settle(inv_buf.at[:, :, pl.ds(0, 7)], l2_s.at[0])

        for i in range(2, 4):
            own = range(1, 3) if i == 3 else range(i)

            @pl.when(n == i)
            def _(own=own):
                for k in own:
                    settle(l_buf.at[pl.ds(0, 2)], l2_s.at[k])

            @pl.when(n == (i + 2) % 4)
            def _(own=own):
                for k in own:
                    settle(inv_buf.at[:, :, pl.ds(0, 3)], l3_s.at[k])

        @pl.when(n == 3)
        def _():
            settle(away_src.at[0], away_sem.at[0])
            settle(away_buf.at[pl.ds(0, 7)], back_sem.at[0])

        @pl.when(n != 3)
        def _():
            settle(away_src, away_sem.at[0])

    drain_weights()
    settle(p0_buf.at[pl.ds(0, 7)], p0_sem.at[0])
    settle(p1_buf.at[pl.ds(0, 7)], p1_sem.at[0])
    for i in range(3):
        settle(x_buf.at[i, pl.ds(0, 7)], x_sem.at[0, i])
        settle(y_buf.at[i, pl.ds(0, 7)], y_sem.at[0, i])

    for i in range(4):
        count = 2 if i < 3 else 8
        sized = o_buf if i < 3 else f_buf

        @pl.when(n == i)
        def _(i=i, count=count, sized=sized):
            settle(sized.at[pl.ds(0, count - 1)], o_s.at[i])

        @pl.when(n != i)
        def _(i=i, count=count, sized=sized):
            settle(sized.at[pl.ds(0, count)], o_s.at[i])

    @pl.when(n < 3)
    def _():
        settle(o_buf.at[pl.ds(0, 7)], o_r.at[0])
        total = o_buf[0]
        for k in range(1, 8):
            total = total + o_buf[k]
        out_ref[...] = total

    @pl.when(n == 3)
    def _():
        settle(f_buf.at[pl.ds(0, 31)], o_r.at[1])
        groups = []
        for first in (0, 16):
            total = f_buf[first]
            for k in range(1, 16):
                total = total + f_buf[first + k]
            groups.append(total)
        left = lax.broadcasted_iota(jnp.int32, (8, 128), 1) < 64
        out_ref[0:8, :] = jnp.where(left, groups[0], groups[1])
        out_ref[8:16, :] = pltpu.roll(jnp.where(left, groups[1], groups[0]), 64, 1)


def body(factor_rows, load_vectors, child_updates, block_inverses):
    dma = pltpu.SemaphoreType.DMA
    out = pl.pallas_call(
        kernel,
        out_shape=jax.ShapeDtypeStruct((16, 128), F32),
        in_specs=[pl.BlockSpec(memory_space=pltpu.HBM)] * 4,
        out_specs=pl.BlockSpec(memory_space=pltpu.VMEM),
        scratch_shapes=[
            pltpu.VMEM((4, 16, 128), F32), pltpu.VMEM((16, 128), F32),
            pltpu.VMEM((128, 128), F32), pltpu.VMEM((128, 128), F32),
            pltpu.VMEM((8, 16, 128), F32), pltpu.VMEM((16, 128), F32), pltpu.VMEM((8, 16, 128), F32),
            pltpu.VMEM((4, 16, 256), F32),
            pltpu.VMEM((3, 16, 128), F32), pltpu.VMEM((3, 8, 16, 128), F32),
            pltpu.VMEM((3, 16, 128), F32), pltpu.VMEM((3, 8, 16, 128), F32),
            pltpu.VMEM((4, 2, 8, 16, 128), F32), pltpu.VMEM((4, 256, 256), BF16),
            pltpu.VMEM((6, 2, 2, 4, 16, 128), F32), pltpu.VMEM((6, 256, 256), BF16),
            pltpu.VMEM((3, 32, 256), BF16),
            pltpu.VMEM((128, 128), F32), pltpu.VMEM((3, 128, 128), F32),
            pltpu.VMEM((8, 16, 128), F32), pltpu.VMEM((32, 8, 128), F32), pltpu.VMEM((64, 128), F32),
            pltpu.VMEM((2, 16, 128), F32), pltpu.VMEM((8, 16, 128), F32),
            pltpu.VMEM((128, 128), F32), pltpu.VMEM((2, 16, 128), F32),
            dma((7,)), dma((2,)), dma((2,)), dma((2, 3)), dma((2, 3)), dma((2, 2)),
            dma, dma((4,)), dma((3,)), dma((3,)), dma((3,)), dma((6,)), dma((3,)), dma((2,)), dma((2,)), dma((4,)), dma((2,)),
        ],
        compiler_params=pltpu.CompilerParams(collective_id=0, has_side_effects=True, vmem_limit_bytes=60 << 20),
        name="substitution",
    )(
        block_inverses,
        factor_rows.reshape(4, 16, 1024),
        load_vectors.reshape(16, 128),
        child_updates.reshape(4, 16, 128),
    )
    return out.reshape(1, 1, 16, 128)


def solution(mesh):
    placed = (
        P(None, "narrow", None, "wide", None, None),
        P(None, "narrow", "wide", None),
        P("narrow", None, None, "wide", None),
        P(None, "wide", None),
    )
    return jax.shard_map(
        body, mesh=mesh, in_specs=placed, out_specs=P(None, "narrow", "wide", None), check_vma=False
    )
```

```python
import jax
import jax.numpy as jnp
from jax import lax
from jax.experimental import pallas as pl
from jax.experimental.pallas import tpu as pltpu
from jax.sharding import PartitionSpec as P

MESH = pl.DeviceIdType.MESH
F32, BF16 = jnp.float32, jnp.bfloat16

PLAN = {
    "gather": [("f", 1), ("f", 2), ("s", 1), ("d", 1, False)],
    "gather end": [],
    "x0": [],
    "x0 end": [("a", 1), ("j", 1), ("f", 3)],
    "y0": [("r", 2), ("i", 2, False)],
    "y0 end": [],
    "x1": [],
    "x1 end": [("j", 2)],
    "y1": [("m",), ("r", 3), ("i", 3, False)],
    "y1 end": [],
    "x2": [],
    "x2 end": [("j", 3)],
    "y2": [],
    "y2 end": [],
}
WHOLE = (0,)


def kernel(inv_ref, fac_ref, load_ref, child_ref, out_ref,
           kid_v, load_v, stage, staged, p0_buf, p1_src, p1_buf, g_all,
           x_src, x_buf, y_src, y_buf, inv_buf, w_inv, l_buf, w_l, y_hl,
           spread, o_src, o_buf, f_buf, f_src, away_src, away_buf, back_src, back_buf,
           loc_sem, p0_sem, p1_sem, x_sem, y_sem, i1_sem, i2_s, i2_r, l1_s, l1_r, l2_s, l2_r, l3_s, away_sem, back_sem,
           o_s, o_r):
    w = lax.axis_index("wide")
    n = lax.axis_index("narrow")
    c = lax.rem(w, 2)
    y = lax.rem(w // 2, 4)
    x = lax.rem(w // 8, 4)
    zh = w // 32
    z = zh * 4 + n
    yc = y * 2 + c

    def dev(zh_, x_, y_, c_, n_):
        return {"wide": ((zh_ * 4 + x_) * 4 + y_) * 2 + c_, "narrow": n_}

    def zdev(z_):
        return dev(z_ // 4, x, y, c, lax.rem(z_, 4))

    def send(src, dst, s_sem, r_sem, to):
        pltpu.make_async_remote_copy(src_ref=src, dst_ref=dst, send_sem=s_sem, recv_sem=r_sem,
                                     device_id=to, device_id_type=MESH).start()

    def settle(like, sem):
        pltpu.make_async_copy(like, like, sem).wait()

    ring = [(2, 0), (2, 1), (1, 0), (1, 1), (3, 0), (3, 1), (0, 1)]

    barrier = pltpu.get_barrier_semaphore()
    for d in (4, 3, 5, 2, 6, 1, 7):
        pl.semaphore_signal(barrier, inc=1, device_id=zdev(lax.rem(z + d, 8)), device_id_type=MESH)
    for d, e in ring:
        pl.semaphore_signal(barrier, inc=1, device_id=dev(zh, x, lax.rem(y + d, 4), lax.rem(c + e, 2), n),
                            device_id_type=MESH)
    for d, e in ring[:-1]:
        pl.semaphore_signal(barrier, inc=1, device_id=dev(zh, lax.rem(x + d, 4), y, lax.rem(c + e, 2), n),
                            device_id_type=MESH)

    near = jnp.where(n < 2, 3, 0)
    for d in (2, 1, 3):
        pl.semaphore_signal(barrier, inc=1, device_id=dev(1 - zh, lax.rem(x + d, 4), y, c, near), device_id_type=MESH)
    at_end = jnp.logical_or(n == 0, n == 3)

    kid_in = pltpu.make_async_copy(child_ref, kid_v, loc_sem.at[0])
    load_in = pltpu.make_async_copy(load_ref, load_v, loc_sem.at[1])
    kid_in.start()
    load_in.start()
    own_inv = [pltpu.make_async_copy(inv_ref.at[:, :, pl.ds(pl.multiple_of(h * 512 + x * 128, 128), 128)],
                                     inv_buf.at[:, h, zh * 4 + x], loc_sem.at[2 + h]) for h in range(2)]
    for cp in own_inv:
        cp.start()

    def own_pair(k):
        return (n * (n - 1)) // 2 + k

    def fac_slice(k, x_, c_):
        return fac_ref.at[k, :, pl.ds(pl.multiple_of(c_ * 512 + x_ * 128, 128), 128)]

    def own_fac(k):
        return pltpu.make_async_copy(fac_slice(k, x, c), l_buf.at[own_pair(k), c, zh, x], loc_sem.at[4 + k])

    for k in range(3):
        @pl.when(k < n)
        def _(k=k):
            own_fac(k).start()

    stage[...] = jnp.zeros_like(stage)
    spread[...] = jnp.zeros_like(spread)
    kid_in.wait()
    load_in.wait()

    def window(i):
        return pl.ds(pl.multiple_of(lax.rem(zh * 4 + i + yc, 8) * 16, 16), 16)

    for i in range(4):
        stage[window(i), :] = -kid_v[i]
    stage[window(n), :] = stage[window(n), :] + load_v[...]
    staged[...] = stage[...].T
    p0_buf[z] = staged[pl.ds(pl.multiple_of(z * 16, 16), 16), :]

    @pl.when(at_end)
    def _():
        pl.semaphore_wait(barrier, 26)

    @pl.when(jnp.logical_not(at_end))
    def _():
        pl.semaphore_wait(barrier, 20)

    for d in (4, 3, 5, 2, 6, 1, 7):
        to = lax.rem(z + d, 8)
        send(staged.at[pl.ds(pl.multiple_of(to * 16, 16), 16), :], p0_buf.at[z], p0_sem.at[0], p0_sem.at[1], zdev(to))

    def start_inverse(part):
        for d in (2, 1, 3):
            xt = lax.rem(x + d, 4)
            for h in range(2):
                cols = pl.ds(pl.multiple_of(h * 512 + xt * 128, 128), 128)
                rows = pl.ds(0, 1) if part == 0 else pl.ds(1, 3)
                send(inv_ref.at[rows, :, cols], inv_buf.at[rows, h, zh * 4 + x], i1_sem.at[0, part], i1_sem.at[1, part],
                     dev(zh, xt, y, c, n))

    def start_factor():
        for k in range(3):
            @pl.when(k < n)
            def _(k=k):
                for d, e in ring:
                    xt, ct = lax.rem(x + d, 4), lax.rem(c + e, 2)
                    send(fac_slice(k, xt, ct), l_buf.at[own_pair(k), c, zh, x], l1_s.at[k], l1_r.at[k],
                         dev(zh, xt, y, ct, n))

    def direct_inverse(i, both):
        for side in range(2):
            @pl.when(n == 3 * side)
            def _(side=side):
                for d in (2, 1, 3, 0):
                    xt = lax.rem(x + d, 4)
                    for h in range(2):
                        cols = pl.ds(pl.multiple_of(h * 512 + xt * 128, 128), 128)
                        for lane in ((3 - 3 * side, 2 - side) if both else (3 - 3 * side,)):
                            send(inv_ref.at[i, :, cols], inv_buf.at[i, h, zh * 4 + x], i2_s, i2_r.at[i],
                                 dev(1 - zh, xt, y, c, lane))

    direct_inverse(0, True)
    start_inverse(0)
    start_factor()

    def arrived_inverse(part):
        settle(inv_buf.at[pl.ds(part, 1 + 2 * part), :, pl.ds(0, 3)], i1_sem.at[1, part])

    def forward_inverse(i, both):
        mine = inv_buf.at[i, :, pl.ds(pl.multiple_of(zh * 4, 4), 4)]
        for side in range(2):
            @pl.when(n == 3 * side)
            def _(side=side):
                send(mine, mine, i2_s, i2_r.at[i], dev(1 - zh, x, y, c, 3 - 3 * side))
                if both:
                    send(mine, mine, i2_s, i2_r.at[i], dev(1 - zh, x, y, c, 2 - side))

    def relay_inverse(i):
        other = inv_buf.at[i, :, pl.ds(pl.multiple_of(4 - zh * 4, 4), 4)]

        @pl.when(jnp.logical_or(n == 0, n == 3))
        def _():
            settle(inv_buf.at[i, :, pl.ds(0, 4)], i2_r.at[i])
        for side in range(2):
            @pl.when(n == 3 * side)
            def _(side=side):
                send(other, other, i2_s, i2_r.at[i], dev(zh, x, y, c, 1 + side))

    for cp in own_inv:
        cp.wait()
    arrived_inverse(0)

    settle(p0_buf.at[pl.ds(0, 7)], p0_sem.at[1])
    own = p0_buf[0]
    for k in range(1, 8):
        own = own + p0_buf[k]
    p1_src[...] = own
    p1_buf[yc] = own
    for d, e in ring:
        send(p1_src, p1_buf.at[yc], p1_sem.at[0], p1_sem.at[1], dev(zh, x, lax.rem(y + d, 4), lax.rem(c + e, 2), n))

    def forward_factor(i):
        @pl.when(n == i)
        def _():
            own = range(1, 3) if i == 3 else range(i)
            for k in own:
                own_fac(k).wait()
                settle(y_buf.at[0, pl.ds(0, 7)], l1_r.at[k])
            for ds in (((4, 3, 5, 2, 6, 1, 7),) if i == 1 else ((2, 6), (1, 7))):
                for k in own:
                    pair = i * (i - 1) // 2 + k
                    mine = l_buf.at[pair, :, zh]
                    for d in ds:
                        send(mine, mine, l2_s.at[k], l2_r.at[pair], zdev(lax.rem(z + d, 8)))

    def relay_factor(i):
        @pl.when(n == (i + 2) % 4)
        def _():
            own = range(1, 3) if i == 3 else range(i)
            for k in own:
                pair = i * (i - 1) // 2 + k
                settle(l_buf.at[pair], l2_r.at[pair])
            for far in range(2):
                for k in own:
                    pair = i * (i - 1) // 2 + k
                    for side in range(2):
                        held = l_buf.at[pair, :, lax.rem(z + (2 if side else 6), 8) // 4]
                        hops = 1 + far

                        @pl.when(c == side if far else c < 2)
                        def _(held=held, hops=hops, side=side, k=k, pair=pair):
                            send(held, held, l3_s.at[k], l2_r.at[pair], zdev(lax.rem(z + (8 - hops if side else hops), 8)))

    def send_first(parts):
        for g in range(2):
            piece = jnp.concatenate([p[:, g * 64:(g + 1) * 64] for p in parts], axis=1)
            away_src[g] = piece
            here = jnp.logical_and(n == 3, zh == g)

            @pl.when(here)
            def _(piece=piece):
                away_buf[z] = piece

            @pl.when(jnp.logical_not(here))
            def _(g=g):
                send(away_src.at[g], away_buf.at[z], away_sem.at[0], away_sem.at[1], dev(g, x, y, c, 3))

    def multiply_first():
        @pl.when(n == 3)
        def _():
            own_fac(0).wait()
            settle(y_buf.at[0, pl.ds(0, 7)], l1_r.at[0])
            settle(away_buf.at[pl.ds(0, 7)], away_sem.at[1])
            hi, lo = split(away_buf[...].reshape(128, 128))
            w_hi, w_lo = split(l_buf[3, :, zh].reshape(128, 128))
            d = jnp.dot(jnp.concatenate([hi, lo], axis=0), jnp.concatenate([w_hi, w_lo], axis=1), preferred_element_type=F32)
            back_src[...] = (d[0:128, 0:128] + d[128:256, 128:256]) + (d[0:128, 128:256] + d[128:256, 0:128])
            back_buf[zh] = back_src[pl.ds(pl.multiple_of(z * 16, 16), 16), :]
            for m in (4, 3, 5, 2, 6, 1, 7):
                to = lax.rem(z + m, 8)
                send(back_src.at[pl.ds(pl.multiple_of(to * 16, 16), 16), :], back_buf.at[zh], back_sem.at[0], back_sem.at[1],
                     zdev(to))

    def returned():
        @pl.when(n == 3)
        def _():
            settle(back_buf.at[0], back_sem.at[1])

        @pl.when(n != 3)
        def _():
            settle(back_buf, back_sem.at[1])
        return back_buf[0] + back_buf[1]

    def pass_on(point):
        for what, *args in PLAN[point]:
            {"f": forward_factor, "r": relay_factor, "m": multiply_first, "i": forward_inverse, "j": relay_inverse,
             "a": arrived_inverse, "s": start_inverse, "d": direct_inverse}[what](*args)

    pass_on("gather")

    def split(v):
        hi = v.astype(BF16)
        return hi, (v - hi.astype(F32)).astype(BF16)

    def prepare_inverse(i):
        if i in WHOLE:
            settle(inv_buf.at[i, :, pl.ds(0, 4)], i2_r.at[i])
        else:
            @pl.when(jnp.logical_and(n != 0, n != 3))
            def _():
                settle(inv_buf.at[i, :, pl.ds(0, 4)], i2_r.at[i])
        for h in range(2):
            hi, lo = split(inv_buf[i, h].reshape(128, 128))
            w_inv[i, 0:128, h * 128:(h + 1) * 128] = hi
            w_inv[i, 128:256, h * 128:(h + 1) * 128] = lo

    def prepare_factor(i, k):
        pair = i * (i - 1) // 2 + k

        passes_on = -1 if i == 1 else (i + 2) % 4

        @pl.when(n == i)
        def _():
            settle(l_buf.at[pair, :, 0], l2_r.at[pair])

        @pl.when(jnp.logical_and(n != i, n != passes_on))
        def _():
            settle(l_buf.at[pair], l2_r.at[pair])
        hi, lo = split(l_buf[pair].reshape(256, 128))
        w_l[pair, :, 0:128] = hi
        w_l[pair, :, 128:256] = lo

    def fold(d):
        return (d[0:16, 0:128] + d[16:32, 128:256]) + (d[0:16, 128:256] + d[16:32, 0:128])

    def stacked(v):
        hi, lo = split(v)
        return jnp.concatenate([hi, lo], axis=0)

    def apply_inverse(i, r):
        return fold(lax.dot_general(stacked(r), w_inv[i], (((1,), (1,)), ((), ())), preferred_element_type=F32))

    def apply_factor(i, k):
        pair = i * (i - 1) // 2 + k
        return fold(jnp.dot(y_hl[k], w_l[pair], preferred_element_type=F32))

    def spread_cases(piece):
        at = pl.ds(pl.multiple_of(z * 16, 16), 16)
        spread[at, :] = piece
        return spread[...].T

    def send_x(i, partial):
        x_src[i] = partial
        x_buf[i, c * 4 + x] = partial
        for d, e in ring:
            send(x_src.at[i], x_buf.at[i, c * 4 + x], x_sem.at[0, i], x_sem.at[1, i],
                 dev(zh, lax.rem(x + d, 4), y, lax.rem(c + e, 2), n))

    def send_y(i, partial):
        y_src[i] = partial
        y_buf[i, c * 4 + y] = partial
        for d, e in ring:
            send(y_src.at[i], y_buf.at[i, c * 4 + y], y_sem.at[0, i], y_sem.at[1, i],
                 dev(zh, x, lax.rem(y + d, 4), lax.rem(c + e, 2), n))

    def halves(buf, i):
        return [(buf[i, 4 * h] + buf[i, 4 * h + 1]) + (buf[i, 4 * h + 2] + buf[i, 4 * h + 3]) for h in range(2)]

    def solved_parts(i):
        settle(x_buf.at[i, pl.ds(0, 7)], x_sem.at[1, i])
        parts = halves(x_buf, i)
        y_hl[i] = stacked(jnp.concatenate(parts, axis=1))
        return parts

    def send_out(i, parts):
        o_src[i] = spread_cases(jnp.where(c == 0, parts[0], parts[1]))
        for g in range(2):
            rows = o_src.at[i, pl.ds(pl.multiple_of((g * 4 + x) * 16, 16), 16), :]
            own_place = jnp.logical_and(n == i, zh == g)

            @pl.when(own_place)
            def _():
                o_buf[z] = o_src[i, pl.ds(pl.multiple_of((g * 4 + x) * 16, 16), 16), :]

            @pl.when(jnp.logical_not(own_place))
            def _():
                send(rows, o_buf.at[z], o_s.at[i], o_r.at[0], dev(g, x, y, c, i))

    prepare_inverse(0)
    pass_on("gather end")
    settle(p1_buf.at[pl.ds(0, 7)], p1_sem.at[1])
    lane_window = lax.broadcasted_iota(jnp.int32, (16, 128), 1) // 16

    def gathered(i):
        for h in range(2):
            first = h * 4 + i
            v = p1_buf[0]
            for k in range(1, 8):
                v = jnp.where(lane_window == (first + k) % 8, p1_buf[k], v)
            if first:
                v = pltpu.roll(v, 128 - first * 16, 1)
            g_all[i, :, h * 128:(h + 1) * 128] = v

    gathered(0)
    send_x(0, apply_inverse(0, g_all[0]))
    pass_on("x0")
    for i in range(1, 4):
        gathered(i)
    pass_on("x0 end")
    prepare_factor(1, 0)
    parts = solved_parts(0)

    for i in range(1, 4):
        ahead = returned() if i == 3 else None
        for k in range(1 if i == 3 else 0, i - 1):
            term = apply_factor(i, k)
            ahead = term if ahead is None else ahead + term
        last = apply_factor(i, i - 1)
        send_y(i - 1, last if ahead is None else ahead + last)
        if i == 1:
            send_first(parts)
        send_out(i - 1, parts)
        pass_on(f"y{i - 1}")
        pass_on(f"y{i - 1} end")
        prepare_inverse(i)
        settle(y_buf.at[i - 1, pl.ds(0, 7)], y_sem.at[1, i - 1])
        sums = halves(y_buf, i - 1)
        partial = apply_inverse(i, g_all[i] - jnp.concatenate(sums, axis=1))
        if i < 3:
            send_x(i, partial)
            pass_on(f"x{i}")
            pass_on(f"x{i} end")
            for k in range(1 if i == 2 else 0, i + 1):
                prepare_factor(i + 1, k)
            parts = solved_parts(i)

    low = lax.rem(lax.broadcasted_iota(jnp.int32, (16, 128), 1) // 8, 2) == 0
    spread[pl.ds(pl.multiple_of(z * 16, 16), 16), :] = jnp.where(low, partial, 0.0)
    spread[pl.ds(pl.multiple_of((1 - zh) * 64 + n * 16, 16), 16), :] = jnp.where(low, 0.0, partial)
    wide_rows = spread[...].T.reshape(8, 2, 8, 128)
    f_src[...] = (wide_rows[:, 0] + wide_rows[:, 1]).reshape(64, 128)
    for g in range(2):
        for d in (2, 1, 3, 0):
            xt = lax.rem(x + d, 4)
            at = pl.ds(pl.multiple_of((g * 4 + xt) * 8, 8), 8)
            if d:
                send(f_src.at[at, :], f_buf.at[z * 4 + x], o_s.at[3], o_r.at[1], dev(g, xt, y, c, 3))
            else:
                own_place = jnp.logical_and(n == 3, zh == g)

                @pl.when(own_place)
                def _():
                    f_buf[z * 4 + x] = f_src[at, :]

                @pl.when(jnp.logical_not(own_place))
                def _():
                    send(f_src.at[at, :], f_buf.at[z * 4 + x], o_s.at[3], o_r.at[1], dev(g, xt, y, c, 3))

    def drain_weights():
        settle(inv_buf.at[0, :, pl.ds(0, 3)], i1_sem.at[0, 0])
        settle(inv_buf.at[pl.ds(1, 3), :, pl.ds(0, 3)], i1_sem.at[0, 1])

        @pl.when(jnp.logical_or(n == 0, n == 3))
        def _():
            settle(inv_buf, i2_s)

        for k in range(3):
            @pl.when(k < n)
            def _(k=k):
                settle(y_buf.at[0, pl.ds(0, 7)], l1_s.at[k])

        @pl.when(n == 1)
        def _():
            settle(inv_buf.at[:, :, pl.ds(0, 7)], l2_s.at[0])

        for i in range(2, 4):
            own = range(1, 3) if i == 3 else range(i)

            @pl.when(n == i)
            def _(own=own):
                for k in own:
                    settle(l_buf.at[pl.ds(0, 2)], l2_s.at[k])

            @pl.when(n == (i + 2) % 4)
            def _(own=own):
                for k in own:
                    settle(inv_buf.at[:, :, pl.ds(0, 3)], l3_s.at[k])

        @pl.when(n == 3)
        def _():
            settle(away_src.at[0], away_sem.at[0])
            settle(away_buf.at[pl.ds(0, 7)], back_sem.at[0])

        @pl.when(n != 3)
        def _():
            settle(away_src, away_sem.at[0])

    drain_weights()
    settle(p0_buf.at[pl.ds(0, 7)], p0_sem.at[0])
    settle(p1_buf.at[pl.ds(0, 7)], p1_sem.at[0])
    for i in range(3):
        settle(x_buf.at[i, pl.ds(0, 7)], x_sem.at[0, i])
        settle(y_buf.at[i, pl.ds(0, 7)], y_sem.at[0, i])

    for i in range(4):
        count = 2 if i < 3 else 8
        sized = o_buf if i < 3 else f_buf

        @pl.when(n == i)
        def _(i=i, count=count, sized=sized):
            settle(sized.at[pl.ds(0, count - 1)], o_s.at[i])

        @pl.when(n != i)
        def _(i=i, count=count, sized=sized):
            settle(sized.at[pl.ds(0, count)], o_s.at[i])

    @pl.when(n < 3)
    def _():
        settle(o_buf.at[pl.ds(0, 7)], o_r.at[0])
        total = o_buf[0]
        for k in range(1, 8):
            total = total + o_buf[k]
        out_ref[...] = total

    @pl.when(n == 3)
    def _():
        settle(f_buf.at[pl.ds(0, 31)], o_r.at[1])
        groups = []
        for first in (0, 16):
            total = f_buf[first]
            for k in range(1, 16):
                total = total + f_buf[first + k]
            groups.append(total)
        left = lax.broadcasted_iota(jnp.int32, (8, 128), 1) < 64
        out_ref[0:8, :] = jnp.where(left, groups[0], groups[1])
        out_ref[8:16, :] = pltpu.roll(jnp.where(left, groups[1], groups[0]), 64, 1)


def body(factor_rows, load_vectors, child_updates, block_inverses):
    dma = pltpu.SemaphoreType.DMA
    out = pl.pallas_call(
        kernel,
        out_shape=jax.ShapeDtypeStruct((16, 128), F32),
        in_specs=[pl.BlockSpec(memory_space=pltpu.HBM)] * 4,
        out_specs=pl.BlockSpec(memory_space=pltpu.VMEM),
        scratch_shapes=[
            pltpu.VMEM((4, 16, 128), F32), pltpu.VMEM((16, 128), F32),
            pltpu.VMEM((128, 128), F32), pltpu.VMEM((128, 128), F32),
            pltpu.VMEM((8, 16, 128), F32), pltpu.VMEM((16, 128), F32), pltpu.VMEM((8, 16, 128), F32),
            pltpu.VMEM((4, 16, 256), F32),
            pltpu.VMEM((3, 16, 128), F32), pltpu.VMEM((3, 8, 16, 128), F32),
            pltpu.VMEM((3, 16, 128), F32), pltpu.VMEM((3, 8, 16, 128), F32),
            pltpu.VMEM((4, 2, 8, 16, 128), F32), pltpu.VMEM((4, 256, 256), BF16),
            pltpu.VMEM((6, 2, 2, 4, 16, 128), F32), pltpu.VMEM((6, 256, 256), BF16),
            pltpu.VMEM((3, 32, 256), BF16),
            pltpu.VMEM((128, 128), F32), pltpu.VMEM((3, 128, 128), F32),
            pltpu.VMEM((8, 16, 128), F32), pltpu.VMEM((32, 8, 128), F32), pltpu.VMEM((64, 128), F32),
            pltpu.VMEM((2, 16, 128), F32), pltpu.VMEM((8, 16, 128), F32),
            pltpu.VMEM((128, 128), F32), pltpu.VMEM((2, 16, 128), F32),
            dma((7,)), dma((2,)), dma((2,)), dma((2, 3)), dma((2, 3)), dma((2, 2)),
            dma, dma((4,)), dma((3,)), dma((3,)), dma((3,)), dma((6,)), dma((3,)), dma((2,)), dma((2,)), dma((4,)), dma((2,)),
        ],
        compiler_params=pltpu.CompilerParams(collective_id=0, has_side_effects=True, vmem_limit_bytes=60 << 20),
        name="substitution",
    )(
        block_inverses,
        factor_rows.reshape(4, 16, 1024),
        load_vectors.reshape(16, 128),
        child_updates.reshape(4, 16, 128),
    )
    return out.reshape(1, 1, 16, 128)


def solution(mesh):
    placed = (
        P(None, "narrow", None, "wide", None, None),
        P(None, "narrow", "wide", None),
        P("narrow", None, None, "wide", None),
        P(None, "wide", None),
    )
    return jax.shard_map(
        body, mesh=mesh, in_specs=placed, out_specs=P(None, "narrow", "wide", None), check_vma=False
    )
```

```python
import jax
import jax.numpy as jnp
from jax import lax
from jax.experimental import pallas as pl
from jax.experimental.pallas import tpu as pltpu
from jax.sharding import PartitionSpec as P

MESH = pl.DeviceIdType.MESH
F32, BF16 = jnp.float32, jnp.bfloat16

PLAN = {
    "gather": [("f", 1), ("f", 2), ("s", 1), ("d", 1, False)],
    "gather end": [],
    "x0": [],
    "x0 end": [("a", 1), ("j", 1), ("f", 3)],
    "y0": [("r", 2), ("i", 2, False)],
    "y0 end": [],
    "x1": [],
    "x1 end": [("j", 2)],
    "y1": [("m",), ("r", 3), ("i", 3, False)],
    "y1 end": [],
    "x2": [],
    "x2 end": [("j", 3)],
    "y2": [],
    "y2 end": [],
}
WHOLE = (0,)


def kernel(inv_ref, fac_ref, load_ref, child_ref, out_ref,
           kid_v, load_v, stage, staged, p0_buf, p1_src, p1_buf, g_all,
           x_src, x_buf, y_src, y_buf, inv_buf, w_inv, l_buf, w_l, y_hl,
           spread, o_src, o_buf, f_buf, f_src, away_src, away_buf, back_src, back_buf,
           loc_sem, p0_sem, p1_sem, x_sem, y_sem, i1_sem, i2_s, i2_r, l1_s, l1_r, l2_s, l2_r, l3_s, away_sem, back_sem,
           o_s, o_r):
    w = lax.axis_index("wide")
    n = lax.axis_index("narrow")
    c = lax.rem(w, 2)
    y = lax.rem(w // 2, 4)
    x = lax.rem(w // 8, 4)
    zh = w // 32
    z = zh * 4 + n
    yc = y * 2 + c

    def dev(zh_, x_, y_, c_, n_):
        return {"wide": ((zh_ * 4 + x_) * 4 + y_) * 2 + c_, "narrow": n_}

    def zdev(z_):
        return dev(z_ // 4, x, y, c, lax.rem(z_, 4))

    def send(src, dst, s_sem, r_sem, to):
        pltpu.make_async_remote_copy(src_ref=src, dst_ref=dst, send_sem=s_sem, recv_sem=r_sem,
                                     device_id=to, device_id_type=MESH).start()

    def settle(like, sem):
        pltpu.make_async_copy(like, like, sem).wait()

    ring = [(2, 0), (2, 1), (1, 0), (1, 1), (3, 0), (3, 1), (0, 1)]

    barrier = pltpu.get_barrier_semaphore()
    for d in (4, 3, 5, 2, 6, 1, 7):
        pl.semaphore_signal(barrier, inc=1, device_id=zdev(lax.rem(z + d, 8)), device_id_type=MESH)
    for d, e in ring:
        pl.semaphore_signal(barrier, inc=1, device_id=dev(zh, x, lax.rem(y + d, 4), lax.rem(c + e, 2), n),
                            device_id_type=MESH)
    for d, e in ring[:-1]:
        pl.semaphore_signal(barrier, inc=1, device_id=dev(zh, lax.rem(x + d, 4), y, lax.rem(c + e, 2), n),
                            device_id_type=MESH)

    near = jnp.where(n < 2, 3, 0)
    for d in (2, 1, 3):
        pl.semaphore_signal(barrier, inc=1, device_id=dev(1 - zh, lax.rem(x + d, 4), y, c, near), device_id_type=MESH)
    at_end = jnp.logical_or(n == 0, n == 3)

    kid_in = pltpu.make_async_copy(child_ref, kid_v, loc_sem.at[0])
    load_in = pltpu.make_async_copy(load_ref, load_v, loc_sem.at[1])
    kid_in.start()
    load_in.start()
    own_inv = [pltpu.make_async_copy(inv_ref.at[:, :, pl.ds(pl.multiple_of(h * 512 + x * 128, 128), 128)],
                                     inv_buf.at[:, h, zh * 4 + x], loc_sem.at[2 + h]) for h in range(2)]
    for cp in own_inv:
        cp.start()

    def own_pair(k):
        return (n * (n - 1)) // 2 + k

    def fac_slice(k, x_, c_):
        return fac_ref.at[k, :, pl.ds(pl.multiple_of(c_ * 512 + x_ * 128, 128), 128)]

    def own_fac(k):
        return pltpu.make_async_copy(fac_slice(k, x, c), l_buf.at[own_pair(k), c, zh, x], loc_sem.at[4 + k])

    for k in range(3):
        @pl.when(k < n)
        def _(k=k):
            own_fac(k).start()

    stage[...] = jnp.zeros_like(stage)
    spread[...] = jnp.zeros_like(spread)
    kid_in.wait()
    load_in.wait()

    def window(i):
        return pl.ds(pl.multiple_of(lax.rem(zh * 4 + i + yc, 8) * 16, 16), 16)

    for i in range(4):
        stage[window(i), :] = -kid_v[i]
    stage[window(n), :] = stage[window(n), :] + load_v[...]
    staged[...] = stage[...].T
    p0_buf[z] = staged[pl.ds(pl.multiple_of(z * 16, 16), 16), :]

    @pl.when(at_end)
    def _():
        pl.semaphore_wait(barrier, 26)

    @pl.when(jnp.logical_not(at_end))
    def _():
        pl.semaphore_wait(barrier, 20)

    for d in (4, 3, 5, 2, 6, 1, 7):
        to = lax.rem(z + d, 8)
        send(staged.at[pl.ds(pl.multiple_of(to * 16, 16), 16), :], p0_buf.at[z], p0_sem.at[0], p0_sem.at[1], zdev(to))

    def start_inverse(part):
        for d in (2, 1, 3):
            xt = lax.rem(x + d, 4)
            for h in range(2):
                cols = pl.ds(pl.multiple_of(h * 512 + xt * 128, 128), 128)
                rows = pl.ds(0, 1) if part == 0 else pl.ds(1, 3)
                send(inv_ref.at[rows, :, cols], inv_buf.at[rows, h, zh * 4 + x], i1_sem.at[0, part], i1_sem.at[1, part],
                     dev(zh, xt, y, c, n))

    def start_factor():
        for k in range(3):
            @pl.when(k < n)
            def _(k=k):
                for d, e in ring:
                    xt, ct = lax.rem(x + d, 4), lax.rem(c + e, 2)
                    send(fac_slice(k, xt, ct), l_buf.at[own_pair(k), c, zh, x], l1_s.at[k], l1_r.at[k],
                         dev(zh, xt, y, ct, n))

    def direct_inverse(i, both):
        for side in range(2):
            @pl.when(n == 3 * side)
            def _(side=side):
                for d in (2, 1, 3, 0):
                    xt = lax.rem(x + d, 4)
                    for h in range(2):
                        cols = pl.ds(pl.multiple_of(h * 512 + xt * 128, 128), 128)
                        for lane in ((3 - 3 * side, 2 - side) if both else (3 - 3 * side,)):
                            send(inv_ref.at[i, :, cols], inv_buf.at[i, h, zh * 4 + x], i2_s, i2_r.at[i],
                                 dev(1 - zh, xt, y, c, lane))

    direct_inverse(0, True)
    start_inverse(0)
    start_factor()

    def arrived_inverse(part):
        settle(inv_buf.at[pl.ds(part, 1 + 2 * part), :, pl.ds(0, 3)], i1_sem.at[1, part])

    def forward_inverse(i, both):
        mine = inv_buf.at[i, :, pl.ds(pl.multiple_of(zh * 4, 4), 4)]
        for side in range(2):
            @pl.when(n == 3 * side)
            def _(side=side):
                send(mine, mine, i2_s, i2_r.at[i], dev(1 - zh, x, y, c, 3 - 3 * side))
                if both:
                    send(mine, mine, i2_s, i2_r.at[i], dev(1 - zh, x, y, c, 2 - side))

    def relay_inverse(i):
        other = inv_buf.at[i, :, pl.ds(pl.multiple_of(4 - zh * 4, 4), 4)]

        @pl.when(jnp.logical_or(n == 0, n == 3))
        def _():
            settle(inv_buf.at[i, :, pl.ds(0, 4)], i2_r.at[i])
        for side in range(2):
            @pl.when(n == 3 * side)
            def _(side=side):
                send(other, other, i2_s, i2_r.at[i], dev(zh, x, y, c, 1 + side))

    for cp in own_inv:
        cp.wait()
    arrived_inverse(0)

    settle(p0_buf.at[pl.ds(0, 7)], p0_sem.at[1])
    own = p0_buf[0]
    for k in range(1, 8):
        own = own + p0_buf[k]
    p1_src[...] = own
    p1_buf[yc] = own
    for d, e in ring:
        send(p1_src, p1_buf.at[yc], p1_sem.at[0], p1_sem.at[1], dev(zh, x, lax.rem(y + d, 4), lax.rem(c + e, 2), n))

    def forward_factor(i):
        @pl.when(n == i)
        def _():
            own = range(1, 3) if i == 3 else range(i)
            for k in own:
                own_fac(k).wait()
                settle(y_buf.at[0, pl.ds(0, 7)], l1_r.at[k])
            for ds in (((4, 3, 5, 2, 6, 1, 7),) if i == 1 else ((2, 6), (1, 7))):
                for k in own:
                    pair = i * (i - 1) // 2 + k
                    mine = l_buf.at[pair, :, zh]
                    for d in ds:
                        send(mine, mine, l2_s.at[k], l2_r.at[pair], zdev(lax.rem(z + d, 8)))

    def relay_factor(i):
        @pl.when(n == (i + 2) % 4)
        def _():
            own = range(1, 3) if i == 3 else range(i)
            for k in own:
                pair = i * (i - 1) // 2 + k
                settle(l_buf.at[pair], l2_r.at[pair])
            for far in range(2):
                for k in own:
                    pair = i * (i - 1) // 2 + k
                    for side in range(2):
                        held = l_buf.at[pair, :, lax.rem(z + (2 if side else 6), 8) // 4]
                        hops = 1 + far

                        @pl.when(c == side if far else c < 2)
                        def _(held=held, hops=hops, side=side, k=k, pair=pair):
                            send(held, held, l3_s.at[k], l2_r.at[pair], zdev(lax.rem(z + (8 - hops if side else hops), 8)))

    def send_first(parts):
        for g in range(2):
            piece = jnp.concatenate([p[:, g * 64:(g + 1) * 64] for p in parts], axis=1)
            away_src[g] = piece
            here = jnp.logical_and(n == 3, zh == g)

            @pl.when(here)
            def _(piece=piece):
                away_buf[z] = piece

            @pl.when(jnp.logical_not(here))
            def _(g=g):
                send(away_src.at[g], away_buf.at[z], away_sem.at[0], away_sem.at[1], dev(g, x, y, c, 3))

    def multiply_first():
        @pl.when(n == 3)
        def _():
            own_fac(0).wait()
            settle(y_buf.at[0, pl.ds(0, 7)], l1_r.at[0])
            settle(away_buf.at[pl.ds(0, 7)], away_sem.at[1])
            hi, lo = split(away_buf[...].reshape(128, 128))
            w_hi, w_lo = split(l_buf[3, :, zh].reshape(128, 128))
            d = jnp.dot(jnp.concatenate([hi, lo], axis=0), jnp.concatenate([w_hi, w_lo], axis=1), preferred_element_type=F32)
            back_src[...] = (d[0:128, 0:128] + d[128:256, 128:256]) + (d[0:128, 128:256] + d[128:256, 0:128])
            back_buf[zh] = back_src[pl.ds(pl.multiple_of(z * 16, 16), 16), :]
            for m in (4, 3, 5, 2, 6, 1, 7):
                to = lax.rem(z + m, 8)
                send(back_src.at[pl.ds(pl.multiple_of(to * 16, 16), 16), :], back_buf.at[zh], back_sem.at[0], back_sem.at[1],
                     zdev(to))

    def returned():
        @pl.when(n == 3)
        def _():
            settle(back_buf.at[0], back_sem.at[1])

        @pl.when(n != 3)
        def _():
            settle(back_buf, back_sem.at[1])
        return back_buf[0] + back_buf[1]

    def pass_on(point):
        for what, *args in PLAN[point]:
            {"f": forward_factor, "r": relay_factor, "m": multiply_first, "i": forward_inverse, "j": relay_inverse,
             "a": arrived_inverse, "s": start_inverse, "d": direct_inverse}[what](*args)

    pass_on("gather")

    def split(v):
        hi = v.astype(BF16)
        return hi, (v - hi.astype(F32)).astype(BF16)

    def prepare_inverse(i):
        if i in WHOLE:
            settle(inv_buf.at[i, :, pl.ds(0, 4)], i2_r.at[i])
        else:
            @pl.when(jnp.logical_and(n != 0, n != 3))
            def _():
                settle(inv_buf.at[i, :, pl.ds(0, 4)], i2_r.at[i])
        for h in range(2):
            hi, lo = split(inv_buf[i, h].reshape(128, 128))
            w_inv[i, 0:128, h * 128:(h + 1) * 128] = hi
            w_inv[i, 128:256, h * 128:(h + 1) * 128] = lo

    def prepare_factor(i, k):
        pair = i * (i - 1) // 2 + k

        passes_on = -1 if i == 1 else (i + 2) % 4

        @pl.when(n == i)
        def _():
            settle(l_buf.at[pair, :, 0], l2_r.at[pair])

        @pl.when(jnp.logical_and(n != i, n != passes_on))
        def _():
            settle(l_buf.at[pair], l2_r.at[pair])
        hi, lo = split(l_buf[pair].reshape(256, 128))
        w_l[pair, :, 0:128] = hi
        w_l[pair, :, 128:256] = lo

    def fold(d):
        return (d[0:16, 0:128] + d[16:32, 128:256]) + (d[0:16, 128:256] + d[16:32, 0:128])

    def stacked(v):
        hi, lo = split(v)
        return jnp.concatenate([hi, lo], axis=0)

    def apply_inverse(i, r):
        return fold(lax.dot_general(stacked(r), w_inv[i], (((1,), (1,)), ((), ())), preferred_element_type=F32))

    def apply_factor(i, k):
        pair = i * (i - 1) // 2 + k
        return fold(jnp.dot(y_hl[k], w_l[pair], preferred_element_type=F32))

    def spread_cases(piece):
        at = pl.ds(pl.multiple_of(z * 16, 16), 16)
        spread[at, :] = piece
        return spread[...].T

    def send_x(i, partial):
        x_src[i] = partial
        x_buf[i, c * 4 + x] = partial
        for d, e in ring:
            send(x_src.at[i], x_buf.at[i, c * 4 + x], x_sem.at[0, i], x_sem.at[1, i],
                 dev(zh, lax.rem(x + d, 4), y, lax.rem(c + e, 2), n))

    def send_y(i, partial):
        y_src[i] = partial
        y_buf[i, c * 4 + y] = partial
        for d, e in ring:
            send(y_src.at[i], y_buf.at[i, c * 4 + y], y_sem.at[0, i], y_sem.at[1, i],
                 dev(zh, x, lax.rem(y + d, 4), lax.rem(c + e, 2), n))

    def halves(buf, i):
        return [(buf[i, 4 * h] + buf[i, 4 * h + 1]) + (buf[i, 4 * h + 2] + buf[i, 4 * h + 3]) for h in range(2)]

    def solved_parts(i):
        settle(x_buf.at[i, pl.ds(0, 7)], x_sem.at[1, i])
        parts = halves(x_buf, i)
        y_hl[i] = stacked(jnp.concatenate(parts, axis=1))
        return parts

    def send_out(i, parts):
        o_src[i] = spread_cases(jnp.where(c == 0, parts[0], parts[1]))
        for g in range(2):
            rows = o_src.at[i, pl.ds(pl.multiple_of((g * 4 + x) * 16, 16), 16), :]
            own_place = jnp.logical_and(n == i, zh == g)

            @pl.when(own_place)
            def _():
                o_buf[z] = o_src[i, pl.ds(pl.multiple_of((g * 4 + x) * 16, 16), 16), :]

            @pl.when(jnp.logical_not(own_place))
            def _():
                send(rows, o_buf.at[z], o_s.at[i], o_r.at[0], dev(g, x, y, c, i))

    prepare_inverse(0)
    pass_on("gather end")
    settle(p1_buf.at[pl.ds(0, 7)], p1_sem.at[1])
    lane_window = lax.broadcasted_iota(jnp.int32, (16, 128), 1) // 16

    def gathered(i):
        for h in range(2):
            first = h * 4 + i
            v = p1_buf[0]
            for k in range(1, 8):
                v = jnp.where(lane_window == (first + k) % 8, p1_buf[k], v)
            if first:
                v = pltpu.roll(v, 128 - first * 16, 1)
            g_all[i, :, h * 128:(h + 1) * 128] = v

    gathered(0)
    send_x(0, apply_inverse(0, g_all[0]))
    pass_on("x0")
    for i in range(1, 4):
        gathered(i)
    pass_on("x0 end")
    prepare_factor(1, 0)
    ahead = None
    parts = solved_parts(0)

    for i in range(1, 4):
        total = apply_factor(i, i - 1)
        if i > 1:
            total = ahead + total
        if i == 3:
            total = returned() + total
        send_y(i - 1, total)
        if i == 1:
            send_first(parts)
        send_out(i - 1, parts)
        pass_on(f"y{i - 1}")
        pass_on(f"y{i - 1} end")
        prepare_inverse(i)
        settle(y_buf.at[i - 1, pl.ds(0, 7)], y_sem.at[1, i - 1])
        sums = halves(y_buf, i - 1)
        partial = apply_inverse(i, g_all[i] - jnp.concatenate(sums, axis=1))
        if i < 3:
            send_x(i, partial)
            pass_on(f"x{i}")
            pass_on(f"x{i} end")
            for k in range(1 if i == 2 else 0, i + 1):
                prepare_factor(i + 1, k)
            ahead = apply_factor(i + 1, i - 1)
            parts = solved_parts(i)

    low = lax.rem(lax.broadcasted_iota(jnp.int32, (16, 128), 1) // 8, 2) == 0
    spread[pl.ds(pl.multiple_of(z * 16, 16), 16), :] = jnp.where(low, partial, 0.0)
    spread[pl.ds(pl.multiple_of((1 - zh) * 64 + n * 16, 16), 16), :] = jnp.where(low, 0.0, partial)
    wide_rows = spread[...].T.reshape(8, 2, 8, 128)
    f_src[...] = (wide_rows[:, 0] + wide_rows[:, 1]).reshape(64, 128)
    far = jnp.where(n < 2, zh, 1 - zh)
    for d, g in [(d, far) for d in (2, 1, 3, 0)] + [(d, 1 - far) for d in (2, 1, 3, 0)]:
        xt = lax.rem(x + d, 4)
        at = pl.ds(pl.multiple_of((g * 4 + xt) * 8, 8), 8)
        if d:
            send(f_src.at[at, :], f_buf.at[z * 4 + x], o_s.at[3], o_r.at[1], dev(g, xt, y, c, 3))
        else:
            own_place = jnp.logical_and(n == 3, zh == g)

            @pl.when(own_place)
            def _(at=at):
                f_buf[z * 4 + x] = f_src[at, :]

            @pl.when(jnp.logical_not(own_place))
            def _(at=at, xt=xt, g=g):
                send(f_src.at[at, :], f_buf.at[z * 4 + x], o_s.at[3], o_r.at[1], dev(g, xt, y, c, 3))

    def drain_weights():
        settle(inv_buf.at[0, :, pl.ds(0, 3)], i1_sem.at[0, 0])
        settle(inv_buf.at[pl.ds(1, 3), :, pl.ds(0, 3)], i1_sem.at[0, 1])

        @pl.when(jnp.logical_or(n == 0, n == 3))
        def _():
            settle(inv_buf, i2_s)

        for k in range(3):
            @pl.when(k < n)
            def _(k=k):
                settle(y_buf.at[0, pl.ds(0, 7)], l1_s.at[k])

        @pl.when(n == 1)
        def _():
            settle(inv_buf.at[:, :, pl.ds(0, 7)], l2_s.at[0])

        for i in range(2, 4):
            own = range(1, 3) if i == 3 else range(i)

            @pl.when(n == i)
            def _(own=own):
                for k in own:
                    settle(l_buf.at[pl.ds(0, 2)], l2_s.at[k])

            @pl.when(n == (i + 2) % 4)
            def _(own=own):
                for k in own:
                    settle(inv_buf.at[:, :, pl.ds(0, 3)], l3_s.at[k])

        @pl.when(n == 3)
        def _():
            settle(away_src.at[0], away_sem.at[0])
            settle(away_buf.at[pl.ds(0, 7)], back_sem.at[0])

        @pl.when(n != 3)
        def _():
            settle(away_src, away_sem.at[0])

    drain_weights()
    settle(p0_buf.at[pl.ds(0, 7)], p0_sem.at[0])
    settle(p1_buf.at[pl.ds(0, 7)], p1_sem.at[0])
    for i in range(3):
        settle(x_buf.at[i, pl.ds(0, 7)], x_sem.at[0, i])
        settle(y_buf.at[i, pl.ds(0, 7)], y_sem.at[0, i])

    for i in range(4):
        count = 2 if i < 3 else 8
        sized = o_buf if i < 3 else f_buf

        @pl.when(n == i)
        def _(i=i, count=count, sized=sized):
            settle(sized.at[pl.ds(0, count - 1)], o_s.at[i])

        @pl.when(n != i)
        def _(i=i, count=count, sized=sized):
            settle(sized.at[pl.ds(0, count)], o_s.at[i])

    @pl.when(n < 3)
    def _():
        settle(o_buf.at[pl.ds(0, 7)], o_r.at[0])
        total = o_buf[0]
        for k in range(1, 8):
            total = total + o_buf[k]
        out_ref[...] = total

    @pl.when(n == 3)
    def _():
        settle(f_buf.at[pl.ds(0, 31)], o_r.at[1])
        groups = []
        for first in (0, 16):
            total = f_buf[first]
            for k in range(1, 16):
                total = total + f_buf[first + k]
            groups.append(total)
        left = lax.broadcasted_iota(jnp.int32, (8, 128), 1) < 64
        out_ref[0:8, :] = jnp.where(left, groups[0], groups[1])
        out_ref[8:16, :] = pltpu.roll(jnp.where(left, groups[1], groups[0]), 64, 1)


def body(factor_rows, load_vectors, child_updates, block_inverses):
    dma = pltpu.SemaphoreType.DMA
    out = pl.pallas_call(
        kernel,
        out_shape=pltpu.VMEM((16, 128), F32),
        in_specs=[pl.BlockSpec(memory_space=pltpu.HBM)] * 4,
        out_specs=pl.BlockSpec(memory_space=pltpu.VMEM),
        scratch_shapes=[
            pltpu.VMEM((4, 16, 128), F32), pltpu.VMEM((16, 128), F32),
            pltpu.VMEM((128, 128), F32), pltpu.VMEM((128, 128), F32),
            pltpu.VMEM((8, 16, 128), F32), pltpu.VMEM((16, 128), F32), pltpu.VMEM((8, 16, 128), F32),
            pltpu.VMEM((4, 16, 256), F32),
            pltpu.VMEM((3, 16, 128), F32), pltpu.VMEM((3, 8, 16, 128), F32),
            pltpu.VMEM((3, 16, 128), F32), pltpu.VMEM((3, 8, 16, 128), F32),
            pltpu.VMEM((4, 2, 8, 16, 128), F32), pltpu.VMEM((4, 256, 256), BF16),
            pltpu.VMEM((6, 2, 2, 4, 16, 128), F32), pltpu.VMEM((6, 256, 256), BF16),
            pltpu.VMEM((3, 32, 256), BF16),
            pltpu.VMEM((128, 128), F32), pltpu.VMEM((3, 128, 128), F32),
            pltpu.VMEM((8, 16, 128), F32), pltpu.VMEM((32, 8, 128), F32), pltpu.VMEM((64, 128), F32),
            pltpu.VMEM((2, 16, 128), F32), pltpu.VMEM((8, 16, 128), F32),
            pltpu.VMEM((128, 128), F32), pltpu.VMEM((2, 16, 128), F32),
            dma((7,)), dma((2,)), dma((2,)), dma((2, 3)), dma((2, 3)), dma((2, 2)),
            dma, dma((4,)), dma((3,)), dma((3,)), dma((3,)), dma((6,)), dma((3,)), dma((2,)), dma((2,)), dma((4,)), dma((2,)),
        ],
        compiler_params=pltpu.CompilerParams(collective_id=0, has_side_effects=True, vmem_limit_bytes=60 << 20),
        name="substitution",
    )(
        block_inverses,
        factor_rows.reshape(4, 16, 1024),
        load_vectors.reshape(16, 128),
        child_updates.reshape(4, 16, 128),
    )
    return out.reshape(1, 1, 16, 128)


def solution(mesh):
    placed = (
        P(None, "narrow", None, "wide", None, None),
        P(None, "narrow", "wide", None),
        P("narrow", None, None, "wide", None),
        P(None, "wide", None),
    )
    return jax.shard_map(
        body, mesh=mesh, in_specs=placed, out_specs=P(None, "narrow", "wide", None), check_vma=False
    )
```

```python
import jax
import jax.numpy as jnp
from jax import lax
from jax.experimental import pallas as pl
from jax.experimental.pallas import tpu as pltpu
from jax.sharding import PartitionSpec as P

MESH = pl.DeviceIdType.MESH
F32, BF16 = jnp.float32, jnp.bfloat16

PLAN = {
    "enter": [("f", 1)],
    "gather": [("f", 2), ("s", 1), ("d", 1, False)],
    "gather end": [],
    "x0": [],
    "x0 end": [("a", 1), ("j", 1), ("f", 3), ("r", 2)],
    "y0": [("i", 2, False)],
    "y0 end": [],
    "x1": [],
    "x1 end": [("j", 2)],
    "y1": [("m",), ("r", 3), ("i", 3, False)],
    "y1 end": [],
    "x2": [],
    "x2 end": [("j", 3)],
    "y2": [],
    "y2 end": [],
}
WHOLE = (0,)


def kernel(inv_ref, fac_ref, load_ref, child_ref, out_ref,
           kid_v, load_v, stage, staged, p0_buf, p1_src, p1_buf, g_all,
           x_src, x_buf, y_src, y_buf, inv_buf, w_inv, l_buf, w_l, y_hl,
           spread, o_src, o_buf, f_buf, f_src, away_src, away_buf, back_src, back_buf,
           loc_sem, p0_sem, p1_sem, x_sem, y_sem, i1_sem, i2_s, i2_r, l1_s, l1_r, l2_s, l2_r, l3_s, away_sem, back_sem,
           o_s, o_r):
    w = lax.axis_index("wide")
    n = lax.axis_index("narrow")
    c = lax.rem(w, 2)
    y = lax.rem(w // 2, 4)
    x = lax.rem(w // 8, 4)
    zh = w // 32
    z = zh * 4 + n
    yc = y * 2 + c

    def dev(zh_, x_, y_, c_, n_):
        return {"wide": ((zh_ * 4 + x_) * 4 + y_) * 2 + c_, "narrow": n_}

    def zdev(z_):
        return dev(z_ // 4, x, y, c, lax.rem(z_, 4))

    def send(src, dst, s_sem, r_sem, to):
        pltpu.make_async_remote_copy(src_ref=src, dst_ref=dst, send_sem=s_sem, recv_sem=r_sem,
                                     device_id=to, device_id_type=MESH).start()

    def settle(like, sem):
        pltpu.make_async_copy(like, like, sem).wait()

    ring = [(2, 0), (2, 1), (1, 0), (1, 1), (3, 0), (3, 1), (0, 1)]

    barrier = pltpu.get_barrier_semaphore()
    for d in (4, 3, 5, 2, 6, 1, 7):
        pl.semaphore_signal(barrier, inc=1, device_id=zdev(lax.rem(z + d, 8)), device_id_type=MESH)
    for d, e in ring:
        pl.semaphore_signal(barrier, inc=1, device_id=dev(zh, x, lax.rem(y + d, 4), lax.rem(c + e, 2), n),
                            device_id_type=MESH)
    for d, e in ring[:-1]:
        pl.semaphore_signal(barrier, inc=1, device_id=dev(zh, lax.rem(x + d, 4), y, lax.rem(c + e, 2), n),
                            device_id_type=MESH)

    near = jnp.where(n < 2, 3, 0)
    for d in (2, 1, 3):
        pl.semaphore_signal(barrier, inc=1, device_id=dev(1 - zh, lax.rem(x + d, 4), y, c, near), device_id_type=MESH)
    at_end = jnp.logical_or(n == 0, n == 3)

    kid_in = pltpu.make_async_copy(child_ref, kid_v, loc_sem.at[0])
    load_in = pltpu.make_async_copy(load_ref, load_v, loc_sem.at[1])
    kid_in.start()
    load_in.start()
    own_inv = [pltpu.make_async_copy(inv_ref.at[:, :, pl.ds(pl.multiple_of(h * 512 + x * 128, 128), 128)],
                                     inv_buf.at[:, h, zh * 4 + x], loc_sem.at[2 + h]) for h in range(2)]
    for cp in own_inv:
        cp.start()

    def own_pair(k):
        return (n * (n - 1)) // 2 + k

    def fac_slice(k, x_, c_):
        return fac_ref.at[k, :, pl.ds(pl.multiple_of(c_ * 512 + x_ * 128, 128), 128)]

    def own_fac(k):
        return pltpu.make_async_copy(fac_slice(k, x, c), l_buf.at[own_pair(k), c, zh, x], loc_sem.at[4 + k])

    for k in range(3):
        @pl.when(k < n)
        def _(k=k):
            own_fac(k).start()

    stage[...] = jnp.zeros_like(stage)
    spread[...] = jnp.zeros_like(spread)
    kid_in.wait()
    load_in.wait()

    def window(i):
        return pl.ds(pl.multiple_of(lax.rem(zh * 4 + i + yc, 8) * 16, 16), 16)

    for i in range(4):
        stage[window(i), :] = -kid_v[i]
    stage[window(n), :] = stage[window(n), :] + load_v[...]
    staged[...] = stage[...].T
    p0_buf[z] = staged[pl.ds(pl.multiple_of(z * 16, 16), 16), :]

    @pl.when(at_end)
    def _():
        pl.semaphore_wait(barrier, 26)

    @pl.when(jnp.logical_not(at_end))
    def _():
        pl.semaphore_wait(barrier, 20)

    for d in (4, 3, 5, 2, 6, 1, 7):
        to = lax.rem(z + d, 8)
        send(staged.at[pl.ds(pl.multiple_of(to * 16, 16), 16), :], p0_buf.at[z], p0_sem.at[0], p0_sem.at[1], zdev(to))

    def start_inverse(part):
        for d in (2, 1, 3):
            xt = lax.rem(x + d, 4)
            for h in range(2):
                cols = pl.ds(pl.multiple_of(h * 512 + xt * 128, 128), 128)
                rows = pl.ds(0, 1) if part == 0 else pl.ds(1, 3)
                send(inv_ref.at[rows, :, cols], inv_buf.at[rows, h, zh * 4 + x], i1_sem.at[0, part], i1_sem.at[1, part],
                     dev(zh, xt, y, c, n))

    def start_factor():
        for k in range(3):
            @pl.when(k < n)
            def _(k=k):
                for d, e in ring:
                    xt, ct = lax.rem(x + d, 4), lax.rem(c + e, 2)
                    send(fac_slice(k, xt, ct), l_buf.at[own_pair(k), c, zh, x], l1_s.at[k], l1_r.at[k],
                         dev(zh, xt, y, ct, n))

    def direct_inverse(i, both):
        for side in range(2):
            @pl.when(n == 3 * side)
            def _(side=side):
                for d in (2, 1, 3, 0):
                    xt = lax.rem(x + d, 4)
                    for h in range(2):
                        cols = pl.ds(pl.multiple_of(h * 512 + xt * 128, 128), 128)
                        for lane in ((3 - 3 * side, 2 - side) if both else (3 - 3 * side,)):
                            send(inv_ref.at[i, :, cols], inv_buf.at[i, h, zh * 4 + x], i2_s, i2_r.at[i],
                                 dev(1 - zh, xt, y, c, lane))

    direct_inverse(0, True)
    for part in range(2):
        @pl.when(n == 1 if part == 0 else n > 1)
        def _():
            start_factor()
        if part == 0:
            start_inverse(0)

    def arrived_inverse(part):
        settle(inv_buf.at[pl.ds(part, 1 + 2 * part), :, pl.ds(0, 3)], i1_sem.at[1, part])

    def forward_inverse(i, both):
        mine = inv_buf.at[i, :, pl.ds(pl.multiple_of(zh * 4, 4), 4)]
        for side in range(2):
            @pl.when(n == 3 * side)
            def _(side=side):
                send(mine, mine, i2_s, i2_r.at[i], dev(1 - zh, x, y, c, 3 - 3 * side))
                if both:
                    send(mine, mine, i2_s, i2_r.at[i], dev(1 - zh, x, y, c, 2 - side))

    def relay_inverse(i):
        other = inv_buf.at[i, :, pl.ds(pl.multiple_of(4 - zh * 4, 4), 4)]

        @pl.when(jnp.logical_or(n == 0, n == 3))
        def _():
            settle(inv_buf.at[i, :, pl.ds(0, 4)], i2_r.at[i])
        for side in range(2):
            @pl.when(n == 3 * side)
            def _(side=side):
                send(other, other, i2_s, i2_r.at[i], dev(zh, x, y, c, 1 + side))

    for cp in own_inv:
        cp.wait()
    arrived_inverse(0)

    def forward_factor(i):
        @pl.when(n == i)
        def _():
            own = range(1, 3) if i == 3 else range(i)
            for k in own:
                own_fac(k).wait()
                settle(y_buf.at[0, pl.ds(0, 7)], l1_r.at[k])
            for ds in (((4, 3, 5, 2, 6, 1, 7),) if i == 1 else ((2, 6), (1, 7))):
                for k in own:
                    pair = i * (i - 1) // 2 + k
                    mine = l_buf.at[pair, :, zh]
                    for d in ds:
                        send(mine, mine, l2_s.at[k], l2_r.at[pair], zdev(lax.rem(z + d, 8)))

    def relay_factor(i):
        @pl.when(n == (i + 2) % 4)
        def _():
            own = range(1, 3) if i == 3 else range(i)
            for k in own:
                pair = i * (i - 1) // 2 + k
                settle(l_buf.at[pair], l2_r.at[pair])
            for far in range(2):
                for k in own:
                    pair = i * (i - 1) // 2 + k
                    for side in range(2):
                        held = l_buf.at[pair, :, lax.rem(z + (2 if side else 6), 8) // 4]
                        hops = 1 + far

                        @pl.when(c == side if far else c < 2)
                        def _(held=held, hops=hops, side=side, k=k, pair=pair):
                            send(held, held, l3_s.at[k], l2_r.at[pair], zdev(lax.rem(z + (8 - hops if side else hops), 8)))

    def send_first(parts):
        for g in range(2):
            piece = jnp.concatenate([p[:, g * 64:(g + 1) * 64] for p in parts], axis=1)
            away_src[g] = piece
            here = jnp.logical_and(n == 3, zh == g)

            @pl.when(here)
            def _(piece=piece):
                away_buf[z] = piece

            @pl.when(jnp.logical_not(here))
            def _(g=g):
                send(away_src.at[g], away_buf.at[z], away_sem.at[0], away_sem.at[1], dev(g, x, y, c, 3))

    def multiply_first():
        @pl.when(n == 3)
        def _():
            own_fac(0).wait()
            settle(y_buf.at[0, pl.ds(0, 7)], l1_r.at[0])
            settle(away_buf.at[pl.ds(0, 7)], away_sem.at[1])
            hi, lo = split(away_buf[...].reshape(128, 128))
            w_hi, w_lo = split(l_buf[3, :, zh].reshape(128, 128))
            d = jnp.dot(jnp.concatenate([hi, lo], axis=0), jnp.concatenate([w_hi, w_lo], axis=1), preferred_element_type=F32)
            back_src[...] = (d[0:128, 0:128] + d[128:256, 128:256]) + (d[0:128, 128:256] + d[128:256, 0:128])
            back_buf[zh] = back_src[pl.ds(pl.multiple_of(z * 16, 16), 16), :]
            for m in (4, 3, 5, 2, 6, 1, 7):
                to = lax.rem(z + m, 8)
                send(back_src.at[pl.ds(pl.multiple_of(to * 16, 16), 16), :], back_buf.at[zh], back_sem.at[0], back_sem.at[1],
                     zdev(to))

    def returned():
        @pl.when(n == 3)
        def _():
            settle(back_buf.at[0], back_sem.at[1])

        @pl.when(n != 3)
        def _():
            settle(back_buf, back_sem.at[1])
        return back_buf[0] + back_buf[1]

    def pass_on(point):
        for what, *args in PLAN[point]:
            {"f": forward_factor, "r": relay_factor, "m": multiply_first, "i": forward_inverse, "j": relay_inverse,
             "a": arrived_inverse, "s": start_inverse, "d": direct_inverse}[what](*args)

    pass_on("enter")

    settle(p0_buf.at[pl.ds(0, 7)], p0_sem.at[1])
    own = p0_buf[0]
    for k in range(1, 8):
        own = own + p0_buf[k]
    p1_src[...] = own
    p1_buf[yc] = own
    for d, e in ring:
        send(p1_src, p1_buf.at[yc], p1_sem.at[0], p1_sem.at[1], dev(zh, x, lax.rem(y + d, 4), lax.rem(c + e, 2), n))

    pass_on("gather")

    def split(v):
        hi = v.astype(BF16)
        return hi, (v - hi.astype(F32)).astype(BF16)

    def prepare_inverse(i):
        if i in WHOLE:
            settle(inv_buf.at[i, :, pl.ds(0, 4)], i2_r.at[i])
        else:
            @pl.when(jnp.logical_and(n != 0, n != 3))
            def _():
                settle(inv_buf.at[i, :, pl.ds(0, 4)], i2_r.at[i])
        for h in range(2):
            hi, lo = split(inv_buf[i, h].reshape(128, 128))
            w_inv[i, 0:128, h * 128:(h + 1) * 128] = hi
            w_inv[i, 128:256, h * 128:(h + 1) * 128] = lo

    def prepare_factor(i, k):
        pair = i * (i - 1) // 2 + k

        passes_on = -1 if i == 1 else (i + 2) % 4

        @pl.when(n == i)
        def _():
            settle(l_buf.at[pair, :, 0], l2_r.at[pair])

        @pl.when(jnp.logical_and(n != i, n != passes_on))
        def _():
            settle(l_buf.at[pair], l2_r.at[pair])
        hi, lo = split(l_buf[pair].reshape(256, 128))
        w_l[pair, :, 0:128] = hi
        w_l[pair, :, 128:256] = lo

    def fold(d):
        return (d[0:16, 0:128] + d[16:32, 128:256]) + (d[0:16, 128:256] + d[16:32, 0:128])

    def stacked(v):
        hi, lo = split(v)
        return jnp.concatenate([hi, lo], axis=0)

    def apply_inverse(i, r):
        return fold(lax.dot_general(stacked(r), w_inv[i], (((1,), (1,)), ((), ())), preferred_element_type=F32))

    def apply_factor(i, k):
        pair = i * (i - 1) // 2 + k
        return fold(jnp.dot(y_hl[k], w_l[pair], preferred_element_type=F32))

    def spread_cases(piece):
        at = pl.ds(pl.multiple_of(z * 16, 16), 16)
        spread[at, :] = piece
        return spread[...].T

    def send_x(i, partial):
        x_src[i] = partial
        x_buf[i, c * 4 + x] = partial
        for d, e in ring:
            send(x_src.at[i], x_buf.at[i, c * 4 + x], x_sem.at[0, i], x_sem.at[1, i],
                 dev(zh, lax.rem(x + d, 4), y, lax.rem(c + e, 2), n))

    def send_y(i, partial):
        y_src[i] = partial
        y_buf[i, c * 4 + y] = partial
        for d, e in ring:
            send(y_src.at[i], y_buf.at[i, c * 4 + y], y_sem.at[0, i], y_sem.at[1, i],
                 dev(zh, x, lax.rem(y + d, 4), lax.rem(c + e, 2), n))

    def halves(buf, i):
        return [(buf[i, 4 * h] + buf[i, 4 * h + 1]) + (buf[i, 4 * h + 2] + buf[i, 4 * h + 3]) for h in range(2)]

    def solved_parts(i):
        settle(x_buf.at[i, pl.ds(0, 7)], x_sem.at[1, i])
        parts = halves(x_buf, i)
        y_hl[i] = stacked(jnp.concatenate(parts, axis=1))
        return parts

    def send_out(i, parts):
        o_src[i] = spread_cases(jnp.where(c == 0, parts[0], parts[1]))
        for g in range(2):
            rows = o_src.at[i, pl.ds(pl.multiple_of((g * 4 + x) * 16, 16), 16), :]
            own_place = jnp.logical_and(n == i, zh == g)

            @pl.when(own_place)
            def _():
                o_buf[z] = o_src[i, pl.ds(pl.multiple_of((g * 4 + x) * 16, 16), 16), :]

            @pl.when(jnp.logical_not(own_place))
            def _():
                send(rows, o_buf.at[z], o_s.at[i], o_r.at[0], dev(g, x, y, c, i))

    prepare_inverse(0)
    pass_on("gather end")
    settle(p1_buf.at[pl.ds(0, 7)], p1_sem.at[1])
    lane_window = lax.broadcasted_iota(jnp.int32, (16, 128), 1) // 16

    def gathered(i):
        for h in range(2):
            first = h * 4 + i
            v = p1_buf[0]
            for k in range(1, 8):
                v = jnp.where(lane_window == (first + k) % 8, p1_buf[k], v)
            if first:
                v = pltpu.roll(v, 128 - first * 16, 1)
            g_all[i, :, h * 128:(h + 1) * 128] = v

    gathered(0)
    send_x(0, apply_inverse(0, g_all[0]))
    pass_on("x0")
    for i in range(1, 4):
        gathered(i)
    pass_on("x0 end")
    prepare_factor(1, 0)
    ahead = None
    parts = solved_parts(0)

    for i in range(1, 4):
        total = apply_factor(i, i - 1)
        if i > 1:
            total = ahead + total
        if i == 3:
            total = returned() + total
        send_y(i - 1, total)
        if i == 1:
            send_first(parts)
        send_out(i - 1, parts)
        pass_on(f"y{i - 1}")
        pass_on(f"y{i - 1} end")
        prepare_inverse(i)
        settle(y_buf.at[i - 1, pl.ds(0, 7)], y_sem.at[1, i - 1])
        sums = halves(y_buf, i - 1)
        partial = apply_inverse(i, g_all[i] - jnp.concatenate(sums, axis=1))
        if i < 3:
            send_x(i, partial)
            pass_on(f"x{i}")
            pass_on(f"x{i} end")
            for k in range(1 if i == 2 else 0, i + 1):
                prepare_factor(i + 1, k)
            ahead = apply_factor(i + 1, i - 1)
            parts = solved_parts(i)

    low = lax.rem(lax.broadcasted_iota(jnp.int32, (16, 128), 1) // 8, 2) == 0
    spread[pl.ds(pl.multiple_of(z * 16, 16), 16), :] = jnp.where(low, partial, 0.0)
    spread[pl.ds(pl.multiple_of((1 - zh) * 64 + n * 16, 16), 16), :] = jnp.where(low, 0.0, partial)
    wide_rows = spread[...].T.reshape(8, 2, 8, 128)
    f_src[...] = (wide_rows[:, 0] + wide_rows[:, 1]).reshape(64, 128)
    far = jnp.where(n < 2, zh, 1 - zh)
    for d, g in [(d, far) for d in (2, 1, 3, 0)] + [(d, 1 - far) for d in (2, 1, 3, 0)]:
        xt = lax.rem(x + d, 4)
        at = pl.ds(pl.multiple_of((g * 4 + xt) * 8, 8), 8)
        if d:
            send(f_src.at[at, :], f_buf.at[z * 4 + x], o_s.at[3], o_r.at[1], dev(g, xt, y, c, 3))
        else:
            own_place = jnp.logical_and(n == 3, zh == g)

            @pl.when(own_place)
            def _(at=at):
                f_buf[z * 4 + x] = f_src[at, :]

            @pl.when(jnp.logical_not(own_place))
            def _(at=at, xt=xt, g=g):
                send(f_src.at[at, :], f_buf.at[z * 4 + x], o_s.at[3], o_r.at[1], dev(g, xt, y, c, 3))

    def drain_weights():
        settle(inv_buf.at[0, :, pl.ds(0, 3)], i1_sem.at[0, 0])
        settle(inv_buf.at[pl.ds(1, 3), :, pl.ds(0, 3)], i1_sem.at[0, 1])

        @pl.when(jnp.logical_or(n == 0, n == 3))
        def _():
            settle(inv_buf, i2_s)

        for k in range(3):
            @pl.when(k < n)
            def _(k=k):
                settle(y_buf.at[0, pl.ds(0, 7)], l1_s.at[k])

        @pl.when(n == 1)
        def _():
            settle(inv_buf.at[:, :, pl.ds(0, 7)], l2_s.at[0])

        for i in range(2, 4):
            own = range(1, 3) if i == 3 else range(i)

            @pl.when(n == i)
            def _(own=own):
                for k in own:
                    settle(l_buf.at[pl.ds(0, 2)], l2_s.at[k])

            @pl.when(n == (i + 2) % 4)
            def _(own=own):
                for k in own:
                    settle(inv_buf.at[:, :, pl.ds(0, 3)], l3_s.at[k])

        @pl.when(n == 3)
        def _():
            settle(away_src.at[0], away_sem.at[0])
            settle(away_buf.at[pl.ds(0, 7)], back_sem.at[0])

        @pl.when(n != 3)
        def _():
            settle(away_src, away_sem.at[0])

    drain_weights()
    settle(p0_buf.at[pl.ds(0, 7)], p0_sem.at[0])
    settle(p1_buf.at[pl.ds(0, 7)], p1_sem.at[0])
    for i in range(3):
        settle(x_buf.at[i, pl.ds(0, 7)], x_sem.at[0, i])
        settle(y_buf.at[i, pl.ds(0, 7)], y_sem.at[0, i])

    for i in range(4):
        count = 2 if i < 3 else 8
        sized = o_buf if i < 3 else f_buf

        @pl.when(n == i)
        def _(i=i, count=count, sized=sized):
            settle(sized.at[pl.ds(0, count - 1)], o_s.at[i])

        @pl.when(n != i)
        def _(i=i, count=count, sized=sized):
            settle(sized.at[pl.ds(0, count)], o_s.at[i])

    @pl.when(n < 3)
    def _():
        settle(o_buf.at[pl.ds(0, 7)], o_r.at[0])
        total = o_buf[0]
        for k in range(1, 8):
            total = total + o_buf[k]
        out_ref[...] = total

    @pl.when(n == 3)
    def _():
        settle(f_buf.at[pl.ds(0, 31)], o_r.at[1])
        groups = []
        for first in (0, 16):
            total = f_buf[first]
            for k in range(1, 16):
                total = total + f_buf[first + k]
            groups.append(total)
        left = lax.broadcasted_iota(jnp.int32, (8, 128), 1) < 64
        out_ref[0:8, :] = jnp.where(left, groups[0], groups[1])
        out_ref[8:16, :] = pltpu.roll(jnp.where(left, groups[1], groups[0]), 64, 1)


def body(factor_rows, load_vectors, child_updates, block_inverses):
    dma = pltpu.SemaphoreType.DMA
    out = pl.pallas_call(
        kernel,
        out_shape=pltpu.VMEM((16, 128), F32),
        in_specs=[pl.BlockSpec(memory_space=pltpu.HBM)] * 4,
        out_specs=pl.BlockSpec(memory_space=pltpu.VMEM),
        scratch_shapes=[
            pltpu.VMEM((4, 16, 128), F32), pltpu.VMEM((16, 128), F32),
            pltpu.VMEM((128, 128), F32), pltpu.VMEM((128, 128), F32),
            pltpu.VMEM((8, 16, 128), F32), pltpu.VMEM((16, 128), F32), pltpu.VMEM((8, 16, 128), F32),
            pltpu.VMEM((4, 16, 256), F32),
            pltpu.VMEM((3, 16, 128), F32), pltpu.VMEM((3, 8, 16, 128), F32),
            pltpu.VMEM((3, 16, 128), F32), pltpu.VMEM((3, 8, 16, 128), F32),
            pltpu.VMEM((4, 2, 8, 16, 128), F32), pltpu.VMEM((4, 256, 256), BF16),
            pltpu.VMEM((6, 2, 2, 4, 16, 128), F32), pltpu.VMEM((6, 256, 256), BF16),
            pltpu.VMEM((3, 32, 256), BF16),
            pltpu.VMEM((128, 128), F32), pltpu.VMEM((3, 128, 128), F32),
            pltpu.VMEM((8, 16, 128), F32), pltpu.VMEM((32, 8, 128), F32), pltpu.VMEM((64, 128), F32),
            pltpu.VMEM((2, 16, 128), F32), pltpu.VMEM((8, 16, 128), F32),
            pltpu.VMEM((128, 128), F32), pltpu.VMEM((2, 16, 128), F32),
            dma((7,)), dma((2,)), dma((2,)), dma((2, 3)), dma((2, 3)), dma((2, 2)),
            dma, dma((4,)), dma((3,)), dma((3,)), dma((3,)), dma((6,)), dma((3,)), dma((2,)), dma((2,)), dma((4,)), dma((2,)),
        ],
        compiler_params=pltpu.CompilerParams(collective_id=0, has_side_effects=True, vmem_limit_bytes=60 << 20),
        name="substitution",
    )(
        block_inverses,
        factor_rows.reshape(4, 16, 1024),
        load_vectors.reshape(16, 128),
        child_updates.reshape(4, 16, 128),
    )
    return out.reshape(1, 1, 16, 128)


def solution(mesh):
    placed = (
        P(None, "narrow", None, "wide", None, None),
        P(None, "narrow", "wide", None),
        P("narrow", None, None, "wide", None),
        P(None, "wide", None),
    )
    return jax.shard_map(
        body, mesh=mesh, in_specs=placed, out_specs=P(None, "narrow", "wide", None), check_vma=False
    )
```

```python
import jax
import jax.numpy as jnp
from jax import lax
from jax.experimental import pallas as pl
from jax.experimental.pallas import tpu as pltpu
from jax.sharding import PartitionSpec as P

MESH = pl.DeviceIdType.MESH
F32, BF16 = jnp.float32, jnp.bfloat16

PLAN = {
    "enter": [("f", 1)],
    "gather": [("f", 2), ("s", 1), ("d", 1, True)],
    "gather end": [],
    "x0": [],
    "x0 end": [("a", 1), ("f", 3), ("r", 2)],
    "y0": [("i", 2, False)],
    "y0 end": [],
    "x1": [],
    "x1 end": [("j", 2)],
    "y1": [("m",), ("r", 3), ("i", 3, False)],
    "y1 end": [],
    "x2": [],
    "x2 end": [("j", 3)],
    "y2": [],
    "y2 end": [],
}
WHOLE = (0, 1)


def kernel(inv_ref, fac_ref, load_ref, child_ref, out_ref,
           kid_v, load_v, stage, staged, p0_buf, p1_src, p1_buf, g_all,
           x_src, x_buf, y_src, y_buf, inv_buf, w_inv, l_buf, w_l, y_hl,
           spread, o_src, o_buf, f_buf, f_src, away_src, away_buf, back_src, back_buf,
           loc_sem, p0_sem, p1_sem, x_sem, y_sem, i1_sem, i2_s, i2_r, l1_s, l1_r, l2_s, l2_r, l3_s, away_sem, back_sem,
           o_s, o_r):
    w = lax.axis_index("wide")
    n = lax.axis_index("narrow")
    c = lax.rem(w, 2)
    y = lax.rem(w // 2, 4)
    x = lax.rem(w // 8, 4)
    zh = w // 32
    z = zh * 4 + n
    yc = y * 2 + c

    def dev(zh_, x_, y_, c_, n_):
        return {"wide": ((zh_ * 4 + x_) * 4 + y_) * 2 + c_, "narrow": n_}

    def zdev(z_):
        return dev(z_ // 4, x, y, c, lax.rem(z_, 4))

    def send(src, dst, s_sem, r_sem, to):
        pltpu.make_async_remote_copy(src_ref=src, dst_ref=dst, send_sem=s_sem, recv_sem=r_sem,
                                     device_id=to, device_id_type=MESH).start()

    def settle(like, sem):
        pltpu.make_async_copy(like, like, sem).wait()

    ring = [(2, 0), (2, 1), (1, 0), (1, 1), (3, 0), (3, 1), (0, 1)]

    barrier = pltpu.get_barrier_semaphore()
    for d in (4, 3, 5, 2, 6, 1, 7):
        pl.semaphore_signal(barrier, inc=1, device_id=zdev(lax.rem(z + d, 8)), device_id_type=MESH)
    for d, e in ring:
        pl.semaphore_signal(barrier, inc=1, device_id=dev(zh, x, lax.rem(y + d, 4), lax.rem(c + e, 2), n),
                            device_id_type=MESH)
    for d, e in ring[:-1]:
        pl.semaphore_signal(barrier, inc=1, device_id=dev(zh, lax.rem(x + d, 4), y, lax.rem(c + e, 2), n),
                            device_id_type=MESH)

    near = jnp.where(n < 2, 3, 0)
    for d in (2, 1, 3):
        pl.semaphore_signal(barrier, inc=1, device_id=dev(1 - zh, lax.rem(x + d, 4), y, c, near), device_id_type=MESH)
    at_end = jnp.logical_or(n == 0, n == 3)

    kid_in = pltpu.make_async_copy(child_ref, kid_v, loc_sem.at[0])
    load_in = pltpu.make_async_copy(load_ref, load_v, loc_sem.at[1])
    kid_in.start()
    load_in.start()
    own_inv = [pltpu.make_async_copy(inv_ref.at[:, :, pl.ds(pl.multiple_of(h * 512 + x * 128, 128), 128)],
                                     inv_buf.at[:, h, zh * 4 + x], loc_sem.at[2 + h]) for h in range(2)]
    for cp in own_inv:
        cp.start()

    def own_pair(k):
        return (n * (n - 1)) // 2 + k

    def fac_slice(k, x_, c_):
        return fac_ref.at[k, :, pl.ds(pl.multiple_of(c_ * 512 + x_ * 128, 128), 128)]

    def own_fac(k):
        return pltpu.make_async_copy(fac_slice(k, x, c), l_buf.at[own_pair(k), c, zh, x], loc_sem.at[4 + k])

    for k in range(3):
        @pl.when(k < n)
        def _(k=k):
            own_fac(k).start()

    stage[...] = jnp.zeros_like(stage)
    spread[...] = jnp.zeros_like(spread)
    kid_in.wait()
    load_in.wait()

    def window(i):
        return pl.ds(pl.multiple_of(lax.rem(zh * 4 + i + yc, 8) * 16, 16), 16)

    for i in range(4):
        stage[window(i), :] = -kid_v[i]
    stage[window(n), :] = stage[window(n), :] + load_v[...]
    staged[...] = stage[...].T
    p0_buf[z] = staged[pl.ds(pl.multiple_of(z * 16, 16), 16), :]

    @pl.when(at_end)
    def _():
        pl.semaphore_wait(barrier, 26)

    @pl.when(jnp.logical_not(at_end))
    def _():
        pl.semaphore_wait(barrier, 20)

    for d in (4, 3, 5, 2, 6, 1, 7):
        to = lax.rem(z + d, 8)
        send(staged.at[pl.ds(pl.multiple_of(to * 16, 16), 16), :], p0_buf.at[z], p0_sem.at[0], p0_sem.at[1], zdev(to))

    def start_inverse(part):
        for d in (2, 1, 3):
            xt = lax.rem(x + d, 4)
            for h in range(2):
                cols = pl.ds(pl.multiple_of(h * 512 + xt * 128, 128), 128)
                rows = pl.ds(0, 1) if part == 0 else pl.ds(1, 3)
                send(inv_ref.at[rows, :, cols], inv_buf.at[rows, h, zh * 4 + x], i1_sem.at[0, part], i1_sem.at[1, part],
                     dev(zh, xt, y, c, n))

    def start_factor():
        for k in range(3):
            @pl.when(k < n)
            def _(k=k):
                for d, e in ring:
                    xt, ct = lax.rem(x + d, 4), lax.rem(c + e, 2)
                    send(fac_slice(k, xt, ct), l_buf.at[own_pair(k), c, zh, x], l1_s.at[k], l1_r.at[k],
                         dev(zh, xt, y, ct, n))

    def direct_inverse(i, both):
        for side in range(2):
            @pl.when(n == 3 * side)
            def _(side=side):
                for d in (2, 1, 3, 0):
                    xt = lax.rem(x + d, 4)
                    for h in range(2):
                        cols = pl.ds(pl.multiple_of(h * 512 + xt * 128, 128), 128)
                        for lane in ((3 - 3 * side, 2 - side) if both else (3 - 3 * side,)):
                            send(inv_ref.at[i, :, cols], inv_buf.at[i, h, zh * 4 + x], i2_s, i2_r.at[i],
                                 dev(1 - zh, xt, y, c, lane))

    direct_inverse(0, True)
    for part in range(2):
        @pl.when(n == 1 if part == 0 else n > 1)
        def _():
            start_factor()
        if part == 0:
            start_inverse(0)

    def arrived_inverse(part):
        settle(inv_buf.at[pl.ds(part, 1 + 2 * part), :, pl.ds(0, 3)], i1_sem.at[1, part])

    def forward_inverse(i, both):
        mine = inv_buf.at[i, :, pl.ds(pl.multiple_of(zh * 4, 4), 4)]
        for side in range(2):
            @pl.when(n == 3 * side)
            def _(side=side):
                send(mine, mine, i2_s, i2_r.at[i], dev(1 - zh, x, y, c, 3 - 3 * side))
                if both:
                    send(mine, mine, i2_s, i2_r.at[i], dev(1 - zh, x, y, c, 2 - side))

    def relay_inverse(i):
        other = inv_buf.at[i, :, pl.ds(pl.multiple_of(4 - zh * 4, 4), 4)]

        @pl.when(jnp.logical_or(n == 0, n == 3))
        def _():
            settle(inv_buf.at[i, :, pl.ds(0, 4)], i2_r.at[i])
        for side in range(2):
            @pl.when(n == 3 * side)
            def _(side=side):
                send(other, other, i2_s, i2_r.at[i], dev(zh, x, y, c, 1 + side))

    for cp in own_inv:
        cp.wait()
    arrived_inverse(0)

    def forward_factor(i):
        @pl.when(n == i)
        def _():
            own = range(1, 3) if i == 3 else range(i)
            for k in own:
                own_fac(k).wait()
                settle(y_buf.at[0, pl.ds(0, 7)], l1_r.at[k])
            for ds in (((4, 3, 5, 2, 6, 1, 7),) if i == 1 else ((2, 6), (1, 7))):
                for k in own:
                    pair = i * (i - 1) // 2 + k
                    mine = l_buf.at[pair, :, zh]
                    for d in ds:
                        send(mine, mine, l2_s.at[k], l2_r.at[pair], zdev(lax.rem(z + d, 8)))

    def relay_factor(i):
        @pl.when(n == (i + 2) % 4)
        def _():
            own = range(1, 3) if i == 3 else range(i)
            for k in own:
                pair = i * (i - 1) // 2 + k
                settle(l_buf.at[pair], l2_r.at[pair])
            for far in range(2):
                for k in own:
                    pair = i * (i - 1) // 2 + k
                    for side in range(2):
                        held = l_buf.at[pair, :, lax.rem(z + (2 if side else 6), 8) // 4]
                        hops = 1 + far

                        @pl.when(c == side if far else c < 2)
                        def _(held=held, hops=hops, side=side, k=k, pair=pair):
                            send(held, held, l3_s.at[k], l2_r.at[pair], zdev(lax.rem(z + (8 - hops if side else hops), 8)))

    def send_first(parts):
        for g in range(2):
            piece = jnp.concatenate([p[:, g * 64:(g + 1) * 64] for p in parts], axis=1)
            away_src[g] = piece
            here = jnp.logical_and(n == 3, zh == g)

            @pl.when(here)
            def _(piece=piece):
                away_buf[z] = piece

            @pl.when(jnp.logical_not(here))
            def _(g=g):
                send(away_src.at[g], away_buf.at[z], away_sem.at[0], away_sem.at[1], dev(g, x, y, c, 3))

    def multiply_first():
        @pl.when(n == 3)
        def _():
            own_fac(0).wait()
            settle(y_buf.at[0, pl.ds(0, 7)], l1_r.at[0])
            settle(away_buf.at[pl.ds(0, 7)], away_sem.at[1])
            hi, lo = split(away_buf[...].reshape(128, 128))
            w_hi, w_lo = split(l_buf[3, :, zh].reshape(128, 128))
            d = jnp.dot(jnp.concatenate([hi, lo], axis=0), jnp.concatenate([w_hi, w_lo], axis=1), preferred_element_type=F32)
            back_src[...] = (d[0:128, 0:128] + d[128:256, 128:256]) + (d[0:128, 128:256] + d[128:256, 0:128])
            back_buf[zh] = back_src[pl.ds(pl.multiple_of(z * 16, 16), 16), :]
            for m in (4, 3, 5, 2, 6, 1, 7):
                to = lax.rem(z + m, 8)
                send(back_src.at[pl.ds(pl.multiple_of(to * 16, 16), 16), :], back_buf.at[zh], back_sem.at[0], back_sem.at[1],
                     zdev(to))

    def returned():
        @pl.when(n == 3)
        def _():
            settle(back_buf.at[0], back_sem.at[1])

        @pl.when(n != 3)
        def _():
            settle(back_buf, back_sem.at[1])
        return back_buf[0] + back_buf[1]

    def pass_on(point):
        for what, *args in PLAN[point]:
            {"f": forward_factor, "r": relay_factor, "m": multiply_first, "i": forward_inverse, "j": relay_inverse,
             "a": arrived_inverse, "s": start_inverse, "d": direct_inverse}[what](*args)

    pass_on("enter")

    settle(p0_buf.at[pl.ds(0, 7)], p0_sem.at[1])
    own = p0_buf[0]
    for k in range(1, 8):
        own = own + p0_buf[k]
    p1_src[...] = own
    p1_buf[yc] = own
    for d, e in ring:
        send(p1_src, p1_buf.at[yc], p1_sem.at[0], p1_sem.at[1], dev(zh, x, lax.rem(y + d, 4), lax.rem(c + e, 2), n))

    pass_on("gather")

    def split(v):
        hi = v.astype(BF16)
        return hi, (v - hi.astype(F32)).astype(BF16)

    def prepare_inverse(i):
        if i in WHOLE:
            settle(inv_buf.at[i, :, pl.ds(0, 4)], i2_r.at[i])
        else:
            @pl.when(jnp.logical_and(n != 0, n != 3))
            def _():
                settle(inv_buf.at[i, :, pl.ds(0, 4)], i2_r.at[i])
        for h in range(2):
            hi, lo = split(inv_buf[i, h].reshape(128, 128))
            w_inv[i, 0:128, h * 128:(h + 1) * 128] = hi
            w_inv[i, 128:256, h * 128:(h + 1) * 128] = lo

    def prepare_factor(i, k):
        pair = i * (i - 1) // 2 + k

        passes_on = -1 if i == 1 else (i + 2) % 4

        @pl.when(n == i)
        def _():
            settle(l_buf.at[pair, :, 0], l2_r.at[pair])

        @pl.when(jnp.logical_and(n != i, n != passes_on))
        def _():
            settle(l_buf.at[pair], l2_r.at[pair])
        hi, lo = split(l_buf[pair].reshape(256, 128))
        w_l[pair, :, 0:128] = hi
        w_l[pair, :, 128:256] = lo

    def fold(d):
        return (d[0:16, 0:128] + d[16:32, 128:256]) + (d[0:16, 128:256] + d[16:32, 0:128])

    def stacked(v):
        hi, lo = split(v)
        return jnp.concatenate([hi, lo], axis=0)

    def apply_inverse(i, r):
        return fold(lax.dot_general(stacked(r), w_inv[i], (((1,), (1,)), ((), ())), preferred_element_type=F32))

    def apply_factor(i, k):
        pair = i * (i - 1) // 2 + k
        return fold(jnp.dot(y_hl[k], w_l[pair], preferred_element_type=F32))

    def spread_cases(piece):
        at = pl.ds(pl.multiple_of(z * 16, 16), 16)
        spread[at, :] = piece
        return spread[...].T

    def send_x(i, partial):
        x_src[i] = partial
        x_buf[i, c * 4 + x] = partial
        for d, e in ring:
            send(x_src.at[i], x_buf.at[i, c * 4 + x], x_sem.at[0, i], x_sem.at[1, i],
                 dev(zh, lax.rem(x + d, 4), y, lax.rem(c + e, 2), n))

    def send_y(i, partial):
        y_src[i] = partial
        y_buf[i, c * 4 + y] = partial
        for d, e in ring:
            send(y_src.at[i], y_buf.at[i, c * 4 + y], y_sem.at[0, i], y_sem.at[1, i],
                 dev(zh, x, lax.rem(y + d, 4), lax.rem(c + e, 2), n))

    def halves(buf, i):
        return [(buf[i, 4 * h] + buf[i, 4 * h + 1]) + (buf[i, 4 * h + 2] + buf[i, 4 * h + 3]) for h in range(2)]

    def solved_parts(i):
        settle(x_buf.at[i, pl.ds(0, 7)], x_sem.at[1, i])
        parts = halves(x_buf, i)
        y_hl[i] = stacked(jnp.concatenate(parts, axis=1))
        return parts

    def send_out(i, parts):
        o_src[i] = spread_cases(jnp.where(c == 0, parts[0], parts[1]))
        for g in range(2):
            rows = o_src.at[i, pl.ds(pl.multiple_of((g * 4 + x) * 16, 16), 16), :]
            own_place = jnp.logical_and(n == i, zh == g)

            @pl.when(own_place)
            def _():
                o_buf[z] = o_src[i, pl.ds(pl.multiple_of((g * 4 + x) * 16, 16), 16), :]

            @pl.when(jnp.logical_not(own_place))
            def _():
                send(rows, o_buf.at[z], o_s.at[i], o_r.at[0], dev(g, x, y, c, i))

    prepare_inverse(0)
    pass_on("gather end")
    settle(p1_buf.at[pl.ds(0, 7)], p1_sem.at[1])
    lane_window = lax.broadcasted_iota(jnp.int32, (16, 128), 1) // 16

    def gathered(i):
        for h in range(2):
            first = h * 4 + i
            v = p1_buf[0]
            for k in range(1, 8):
                v = jnp.where(lane_window == (first + k) % 8, p1_buf[k], v)
            if first:
                v = pltpu.roll(v, 128 - first * 16, 1)
            g_all[i, :, h * 128:(h + 1) * 128] = v

    gathered(0)
    send_x(0, apply_inverse(0, g_all[0]))
    pass_on("x0")
    for i in range(1, 4):
        gathered(i)
    pass_on("x0 end")
    prepare_factor(1, 0)
    ahead = None
    parts = solved_parts(0)

    for i in range(1, 4):
        total = apply_factor(i, i - 1)
        if i > 1:
            total = ahead + total
        if i == 3:
            total = returned() + total
        send_y(i - 1, total)
        if i == 1:
            send_first(parts)
        send_out(i - 1, parts)
        pass_on(f"y{i - 1}")
        pass_on(f"y{i - 1} end")
        prepare_inverse(i)
        settle(y_buf.at[i - 1, pl.ds(0, 7)], y_sem.at[1, i - 1])
        sums = halves(y_buf, i - 1)
        partial = apply_inverse(i, g_all[i] - jnp.concatenate(sums, axis=1))
        if i < 3:
            send_x(i, partial)
            pass_on(f"x{i}")
            pass_on(f"x{i} end")
            for k in range(1 if i == 2 else 0, i + 1):
                prepare_factor(i + 1, k)
            ahead = apply_factor(i + 1, i - 1)
            parts = solved_parts(i)

    low = lax.rem(lax.broadcasted_iota(jnp.int32, (16, 128), 1) // 8, 2) == 0
    spread[pl.ds(pl.multiple_of(z * 16, 16), 16), :] = jnp.where(low, partial, 0.0)
    spread[pl.ds(pl.multiple_of((1 - zh) * 64 + n * 16, 16), 16), :] = jnp.where(low, 0.0, partial)
    wide_rows = spread[...].T.reshape(8, 2, 8, 128)
    f_src[...] = (wide_rows[:, 0] + wide_rows[:, 1]).reshape(64, 128)
    far = jnp.where(n < 2, zh, 1 - zh)
    for d, g in [(d, far) for d in (2, 1, 3, 0)] + [(d, 1 - far) for d in (2, 1, 3, 0)]:
        xt = lax.rem(x + d, 4)
        at = pl.ds(pl.multiple_of((g * 4 + xt) * 8, 8), 8)
        if d:
            send(f_src.at[at, :], f_buf.at[z * 4 + x], o_s.at[3], o_r.at[1], dev(g, xt, y, c, 3))
        else:
            own_place = jnp.logical_and(n == 3, zh == g)

            @pl.when(own_place)
            def _(at=at):
                f_buf[z * 4 + x] = f_src[at, :]

            @pl.when(jnp.logical_not(own_place))
            def _(at=at, xt=xt, g=g):
                send(f_src.at[at, :], f_buf.at[z * 4 + x], o_s.at[3], o_r.at[1], dev(g, xt, y, c, 3))

    def drain_weights():
        settle(inv_buf.at[0, :, pl.ds(0, 3)], i1_sem.at[0, 0])
        settle(inv_buf.at[pl.ds(1, 3), :, pl.ds(0, 3)], i1_sem.at[0, 1])

        @pl.when(jnp.logical_or(n == 0, n == 3))
        def _():
            settle(inv_buf, i2_s)

        for k in range(3):
            @pl.when(k < n)
            def _(k=k):
                settle(y_buf.at[0, pl.ds(0, 7)], l1_s.at[k])

        @pl.when(n == 1)
        def _():
            settle(inv_buf.at[:, :, pl.ds(0, 7)], l2_s.at[0])

        for i in range(2, 4):
            own = range(1, 3) if i == 3 else range(i)

            @pl.when(n == i)
            def _(own=own):
                for k in own:
                    settle(l_buf.at[pl.ds(0, 2)], l2_s.at[k])

            @pl.when(n == (i + 2) % 4)
            def _(own=own):
                for k in own:
                    settle(inv_buf.at[:, :, pl.ds(0, 3)], l3_s.at[k])

        @pl.when(n == 3)
        def _():
            settle(away_src.at[0], away_sem.at[0])
            settle(away_buf.at[pl.ds(0, 7)], back_sem.at[0])

        @pl.when(n != 3)
        def _():
            settle(away_src, away_sem.at[0])

    drain_weights()
    settle(p0_buf.at[pl.ds(0, 7)], p0_sem.at[0])
    settle(p1_buf.at[pl.ds(0, 7)], p1_sem.at[0])
    for i in range(3):
        settle(x_buf.at[i, pl.ds(0, 7)], x_sem.at[0, i])
        settle(y_buf.at[i, pl.ds(0, 7)], y_sem.at[0, i])

    for i in range(4):
        count = 2 if i < 3 else 8
        sized = o_buf if i < 3 else f_buf

        @pl.when(n == i)
        def _(i=i, count=count, sized=sized):
            settle(sized.at[pl.ds(0, count - 1)], o_s.at[i])

        @pl.when(n != i)
        def _(i=i, count=count, sized=sized):
            settle(sized.at[pl.ds(0, count)], o_s.at[i])

    @pl.when(n < 3)
    def _():
        settle(o_buf.at[pl.ds(0, 7)], o_r.at[0])
        total = o_buf[0]
        for k in range(1, 8):
            total = total + o_buf[k]
        out_ref[...] = total

    @pl.when(n == 3)
    def _():
        settle(f_buf.at[pl.ds(0, 31)], o_r.at[1])
        groups = []
        for first in (0, 16):
            total = f_buf[first]
            for k in range(1, 16):
                total = total + f_buf[first + k]
            groups.append(total)
        left = lax.broadcasted_iota(jnp.int32, (8, 128), 1) < 64
        out_ref[0:8, :] = jnp.where(left, groups[0], groups[1])
        out_ref[8:16, :] = pltpu.roll(jnp.where(left, groups[1], groups[0]), 64, 1)


def body(factor_rows, load_vectors, child_updates, block_inverses):
    dma = pltpu.SemaphoreType.DMA
    out = pl.pallas_call(
        kernel,
        out_shape=pltpu.VMEM((16, 128), F32),
        in_specs=[pl.BlockSpec(memory_space=pltpu.HBM)] * 4,
        out_specs=pl.BlockSpec(memory_space=pltpu.VMEM),
        scratch_shapes=[
            pltpu.VMEM((4, 16, 128), F32), pltpu.VMEM((16, 128), F32),
            pltpu.VMEM((128, 128), F32), pltpu.VMEM((128, 128), F32),
            pltpu.VMEM((8, 16, 128), F32), pltpu.VMEM((16, 128), F32), pltpu.VMEM((8, 16, 128), F32),
            pltpu.VMEM((4, 16, 256), F32),
            pltpu.VMEM((3, 16, 128), F32), pltpu.VMEM((3, 8, 16, 128), F32),
            pltpu.VMEM((3, 16, 128), F32), pltpu.VMEM((3, 8, 16, 128), F32),
            pltpu.VMEM((4, 2, 8, 16, 128), F32), pltpu.VMEM((4, 256, 256), BF16),
            pltpu.VMEM((6, 2, 2, 4, 16, 128), F32), pltpu.VMEM((6, 256, 256), BF16),
            pltpu.VMEM((3, 32, 256), BF16),
            pltpu.VMEM((128, 128), F32), pltpu.VMEM((3, 128, 128), F32),
            pltpu.VMEM((8, 16, 128), F32), pltpu.VMEM((32, 8, 128), F32), pltpu.VMEM((64, 128), F32),
            pltpu.VMEM((2, 16, 128), F32), pltpu.VMEM((8, 16, 128), F32),
            pltpu.VMEM((128, 128), F32), pltpu.VMEM((2, 16, 128), F32),
            dma((7,)), dma((2,)), dma((2,)), dma((2, 3)), dma((2, 3)), dma((2, 2)),
            dma, dma((4,)), dma((3,)), dma((3,)), dma((3,)), dma((6,)), dma((3,)), dma((2,)), dma((2,)), dma((4,)), dma((2,)),
        ],
        compiler_params=pltpu.CompilerParams(collective_id=0, has_side_effects=True, vmem_limit_bytes=60 << 20),
        name="substitution",
    )(
        block_inverses,
        factor_rows.reshape(4, 16, 1024),
        load_vectors.reshape(16, 128),
        child_updates.reshape(4, 16, 128),
    )
    return out.reshape(1, 1, 16, 128)


def solution(mesh):
    placed = (
        P(None, "narrow", None, "wide", None, None),
        P(None, "narrow", "wide", None),
        P("narrow", None, None, "wide", None),
        P(None, "wide", None),
    )
    return jax.shard_map(
        body, mesh=mesh, in_specs=placed, out_specs=P(None, "narrow", "wide", None), check_vma=False
    )
```

```python
import jax
import jax.numpy as jnp
from jax import lax
from jax.experimental import pallas as pl
from jax.experimental.pallas import tpu as pltpu
from jax.sharding import PartitionSpec as P

MESH = pl.DeviceIdType.MESH
F32, BF16 = jnp.float32, jnp.bfloat16

PLAN = {
    "enter": [("f", 1)],
    "gather": [("f", 2), ("s", 1), ("d", 1, True)],
    "gather end": [],
    "x0": [],
    "x0 end": [("a", 1), ("f", 3), ("r", 2)],
    "y0": [("i", 2, False)],
    "y0 end": [],
    "x1": [],
    "x1 end": [("j", 2)],
    "y1": [("m",), ("r", 3), ("i", 3, True)],
    "y1 end": [],
    "x2": [],
    "x2 end": [],
    "y2": [],
    "y2 end": [],
}
WHOLE = (0, 1, 3)


def kernel(inv_ref, fac_ref, load_ref, child_ref, out_ref,
           kid_v, load_v, stage, staged, p0_buf, p1_src, p1_buf, g_all,
           x_src, x_buf, y_src, y_buf, inv_buf, w_inv, l_buf, w_l, y_hl,
           spread, o_src, o_buf, f_buf, f_src, away_src, away_buf, back_src, back_buf,
           loc_sem, p0_sem, p1_sem, x_sem, y_sem, i1_sem, i2_s, i2_r, l1_s, l1_r, l2_s, l2_r, l3_s, away_sem, back_sem,
           o_s, o_r):
    w = lax.axis_index("wide")
    n = lax.axis_index("narrow")
    c = lax.rem(w, 2)
    y = lax.rem(w // 2, 4)
    x = lax.rem(w // 8, 4)
    zh = w // 32
    z = zh * 4 + n
    yc = y * 2 + c

    def dev(zh_, x_, y_, c_, n_):
        return {"wide": ((zh_ * 4 + x_) * 4 + y_) * 2 + c_, "narrow": n_}

    def zdev(z_):
        return dev(z_ // 4, x, y, c, lax.rem(z_, 4))

    def send(src, dst, s_sem, r_sem, to):
        pltpu.make_async_remote_copy(src_ref=src, dst_ref=dst, send_sem=s_sem, recv_sem=r_sem,
                                     device_id=to, device_id_type=MESH).start()

    def settle(like, sem):
        pltpu.make_async_copy(like, like, sem).wait()

    ring = [(2, 0), (2, 1), (1, 0), (1, 1), (3, 0), (3, 1), (0, 1)]

    barrier = pltpu.get_barrier_semaphore()
    for d in (4, 3, 5, 2, 6, 1, 7):
        pl.semaphore_signal(barrier, inc=1, device_id=zdev(lax.rem(z + d, 8)), device_id_type=MESH)
    for d, e in ring:
        pl.semaphore_signal(barrier, inc=1, device_id=dev(zh, x, lax.rem(y + d, 4), lax.rem(c + e, 2), n),
                            device_id_type=MESH)
    for d, e in ring[:-1]:
        pl.semaphore_signal(barrier, inc=1, device_id=dev(zh, lax.rem(x + d, 4), y, lax.rem(c + e, 2), n),
                            device_id_type=MESH)

    near = jnp.where(n < 2, 3, 0)
    for d in (2, 1, 3):
        pl.semaphore_signal(barrier, inc=1, device_id=dev(1 - zh, lax.rem(x + d, 4), y, c, near), device_id_type=MESH)
    at_end = jnp.logical_or(n == 0, n == 3)

    kid_in = pltpu.make_async_copy(child_ref, kid_v, loc_sem.at[0])
    load_in = pltpu.make_async_copy(load_ref, load_v, loc_sem.at[1])
    kid_in.start()
    load_in.start()
    own_inv = [pltpu.make_async_copy(inv_ref.at[:, :, pl.ds(pl.multiple_of(h * 512 + x * 128, 128), 128)],
                                     inv_buf.at[:, h, zh * 4 + x], loc_sem.at[2 + h]) for h in range(2)]
    for cp in own_inv:
        cp.start()

    def own_pair(k):
        return (n * (n - 1)) // 2 + k

    def fac_slice(k, x_, c_):
        return fac_ref.at[k, :, pl.ds(pl.multiple_of(c_ * 512 + x_ * 128, 128), 128)]

    def own_fac(k):
        return pltpu.make_async_copy(fac_slice(k, x, c), l_buf.at[own_pair(k), c, zh, x], loc_sem.at[4 + k])

    for k in range(3):
        @pl.when(k < n)
        def _(k=k):
            own_fac(k).start()

    stage[...] = jnp.zeros_like(stage)
    spread[...] = jnp.zeros_like(spread)
    kid_in.wait()
    load_in.wait()

    def window(i):
        return pl.ds(pl.multiple_of(lax.rem(zh * 4 + i + yc, 8) * 16, 16), 16)

    for i in range(4):
        stage[window(i), :] = -kid_v[i]
    stage[window(n), :] = stage[window(n), :] + load_v[...]
    staged[...] = stage[...].T
    p0_buf[z] = staged[pl.ds(pl.multiple_of(z * 16, 16), 16), :]

    @pl.when(at_end)
    def _():
        pl.semaphore_wait(barrier, 26)

    @pl.when(jnp.logical_not(at_end))
    def _():
        pl.semaphore_wait(barrier, 20)

    for d in (4, 3, 5, 2, 6, 1, 7):
        to = lax.rem(z + d, 8)
        send(staged.at[pl.ds(pl.multiple_of(to * 16, 16), 16), :], p0_buf.at[z], p0_sem.at[0], p0_sem.at[1], zdev(to))

    def start_inverse(part):
        for d in (2, 1, 3):
            xt = lax.rem(x + d, 4)
            for h in range(2):
                cols = pl.ds(pl.multiple_of(h * 512 + xt * 128, 128), 128)
                rows = pl.ds(0, 1) if part == 0 else pl.ds(1, 3)
                send(inv_ref.at[rows, :, cols], inv_buf.at[rows, h, zh * 4 + x], i1_sem.at[0, part], i1_sem.at[1, part],
                     dev(zh, xt, y, c, n))

    def start_factor():
        for k in range(3):
            @pl.when(k < n)
            def _(k=k):
                for d, e in ring:
                    xt, ct = lax.rem(x + d, 4), lax.rem(c + e, 2)
                    send(fac_slice(k, xt, ct), l_buf.at[own_pair(k), c, zh, x], l1_s.at[k], l1_r.at[k],
                         dev(zh, xt, y, ct, n))

    def direct_inverse(i, both):
        for side in range(2):
            @pl.when(n == 3 * side)
            def _(side=side):
                for d in (2, 1, 3, 0):
                    xt = lax.rem(x + d, 4)
                    for h in range(2):
                        cols = pl.ds(pl.multiple_of(h * 512 + xt * 128, 128), 128)
                        for lane in ((3 - 3 * side, 2 - side) if both else (3 - 3 * side,)):
                            send(inv_ref.at[i, :, cols], inv_buf.at[i, h, zh * 4 + x], i2_s, i2_r.at[i],
                                 dev(1 - zh, xt, y, c, lane))

    direct_inverse(0, True)
    for part in range(2):
        @pl.when(n == 1 if part == 0 else n > 1)
        def _():
            start_factor()
        if part == 0:
            start_inverse(0)

    def arrived_inverse(part):
        settle(inv_buf.at[pl.ds(part, 1 + 2 * part), :, pl.ds(0, 3)], i1_sem.at[1, part])

    def forward_inverse(i, both):
        mine = inv_buf.at[i, :, pl.ds(pl.multiple_of(zh * 4, 4), 4)]
        for side in range(2):
            @pl.when(n == 3 * side)
            def _(side=side):
                send(mine, mine, i2_s, i2_r.at[i], dev(1 - zh, x, y, c, 3 - 3 * side))
                if both:
                    send(mine, mine, i2_s, i2_r.at[i], dev(1 - zh, x, y, c, 2 - side))

    def relay_inverse(i):
        other = inv_buf.at[i, :, pl.ds(pl.multiple_of(4 - zh * 4, 4), 4)]

        @pl.when(jnp.logical_or(n == 0, n == 3))
        def _():
            settle(inv_buf.at[i, :, pl.ds(0, 4)], i2_r.at[i])
        for side in range(2):
            @pl.when(n == 3 * side)
            def _(side=side):
                send(other, other, i2_s, i2_r.at[i], dev(zh, x, y, c, 1 + side))

    for cp in own_inv:
        cp.wait()
    arrived_inverse(0)

    def forward_factor(i):
        @pl.when(n == i)
        def _():
            own = range(1, 3) if i == 3 else range(i)
            for k in own:
                own_fac(k).wait()
                settle(y_buf.at[0, pl.ds(0, 7)], l1_r.at[k])
            for ds in (((4, 3, 5, 2, 6, 1, 7),) if i == 1 else ((2, 6), (1, 7))):
                for k in own:
                    pair = i * (i - 1) // 2 + k
                    mine = l_buf.at[pair, :, zh]
                    for d in ds:
                        send(mine, mine, l2_s.at[k], l2_r.at[pair], zdev(lax.rem(z + d, 8)))

    def relay_factor(i):
        @pl.when(n == (i + 2) % 4)
        def _():
            own = range(1, 3) if i == 3 else range(i)
            for k in own:
                pair = i * (i - 1) // 2 + k
                settle(l_buf.at[pair], l2_r.at[pair])
            for far in range(2):
                for k in own:
                    pair = i * (i - 1) // 2 + k
                    for side in range(2):
                        held = l_buf.at[pair, :, lax.rem(z + (2 if side else 6), 8) // 4]
                        hops = 1 + far

                        @pl.when(c == side if far else c < 2)
                        def _(held=held, hops=hops, side=side, k=k, pair=pair):
                            send(held, held, l3_s.at[k], l2_r.at[pair], zdev(lax.rem(z + (8 - hops if side else hops), 8)))

    def send_first(parts):
        for g in range(2):
            piece = jnp.concatenate([p[:, g * 64:(g + 1) * 64] for p in parts], axis=1)
            away_src[g] = piece
            here = jnp.logical_and(n == 3, zh == g)

            @pl.when(here)
            def _(piece=piece):
                away_buf[z] = piece

            @pl.when(jnp.logical_not(here))
            def _(g=g):
                send(away_src.at[g], away_buf.at[z], away_sem.at[0], away_sem.at[1], dev(g, x, y, c, 3))

    def multiply_first():
        @pl.when(n == 3)
        def _():
            own_fac(0).wait()
            settle(y_buf.at[0, pl.ds(0, 7)], l1_r.at[0])
            settle(away_buf.at[pl.ds(0, 7)], away_sem.at[1])
            hi, lo = split(away_buf[...].reshape(128, 128))
            w_hi, w_lo = split(l_buf[3, :, zh].reshape(128, 128))
            d = jnp.dot(jnp.concatenate([hi, lo], axis=0), jnp.concatenate([w_hi, w_lo], axis=1), preferred_element_type=F32)
            back_src[...] = (d[0:128, 0:128] + d[128:256, 128:256]) + (d[0:128, 128:256] + d[128:256, 0:128])
            back_buf[zh] = back_src[pl.ds(pl.multiple_of(z * 16, 16), 16), :]
            for m in (4, 3, 5, 2, 6, 1, 7):
                to = lax.rem(z + m, 8)
                send(back_src.at[pl.ds(pl.multiple_of(to * 16, 16), 16), :], back_buf.at[zh], back_sem.at[0], back_sem.at[1],
                     zdev(to))

    def returned():
        @pl.when(n == 3)
        def _():
            settle(back_buf.at[0], back_sem.at[1])

        @pl.when(n != 3)
        def _():
            settle(back_buf, back_sem.at[1])
        return back_buf[0] + back_buf[1]

    def pass_on(point):
        for what, *args in PLAN[point]:
            {"f": forward_factor, "r": relay_factor, "m": multiply_first, "i": forward_inverse, "j": relay_inverse,
             "a": arrived_inverse, "s": start_inverse, "d": direct_inverse}[what](*args)

    pass_on("enter")

    settle(p0_buf.at[pl.ds(0, 7)], p0_sem.at[1])
    own = p0_buf[0]
    for k in range(1, 8):
        own = own + p0_buf[k]
    p1_src[...] = own
    p1_buf[yc] = own
    for d, e in ring:
        send(p1_src, p1_buf.at[yc], p1_sem.at[0], p1_sem.at[1], dev(zh, x, lax.rem(y + d, 4), lax.rem(c + e, 2), n))

    pass_on("gather")

    def split(v):
        hi = v.astype(BF16)
        return hi, (v - hi.astype(F32)).astype(BF16)

    def prepare_inverse(i):
        if i in WHOLE:
            settle(inv_buf.at[i, :, pl.ds(0, 4)], i2_r.at[i])
        else:
            @pl.when(jnp.logical_and(n != 0, n != 3))
            def _():
                settle(inv_buf.at[i, :, pl.ds(0, 4)], i2_r.at[i])
        for h in range(2):
            hi, lo = split(inv_buf[i, h].reshape(128, 128))
            w_inv[i, 0:128, h * 128:(h + 1) * 128] = hi
            w_inv[i, 128:256, h * 128:(h + 1) * 128] = lo

    def prepare_factor(i, k):
        pair = i * (i - 1) // 2 + k

        passes_on = -1 if i == 1 else (i + 2) % 4

        @pl.when(n == i)
        def _():
            settle(l_buf.at[pair, :, 0], l2_r.at[pair])

        @pl.when(jnp.logical_and(n != i, n != passes_on))
        def _():
            settle(l_buf.at[pair], l2_r.at[pair])
        hi, lo = split(l_buf[pair].reshape(256, 128))
        w_l[pair, :, 0:128] = hi
        w_l[pair, :, 128:256] = lo

    def fold(d):
        return (d[0:16, 0:128] + d[16:32, 128:256]) + (d[0:16, 128:256] + d[16:32, 0:128])

    def stacked(v):
        hi, lo = split(v)
        return jnp.concatenate([hi, lo], axis=0)

    def apply_inverse(i, r):
        return fold(lax.dot_general(stacked(r), w_inv[i], (((1,), (1,)), ((), ())), preferred_element_type=F32))

    def apply_factor(i, k):
        pair = i * (i - 1) // 2 + k
        return fold(jnp.dot(y_hl[k], w_l[pair], preferred_element_type=F32))

    def spread_cases(piece):
        at = pl.ds(pl.multiple_of(z * 16, 16), 16)
        spread[at, :] = piece
        return spread[...].T

    def send_x(i, partial):
        x_src[i] = partial
        x_buf[i, c * 4 + x] = partial
        for d, e in ring:
            send(x_src.at[i], x_buf.at[i, c * 4 + x], x_sem.at[0, i], x_sem.at[1, i],
                 dev(zh, lax.rem(x + d, 4), y, lax.rem(c + e, 2), n))

    def send_y(i, partial):
        y_src[i] = partial
        y_buf[i, c * 4 + y] = partial
        for d, e in ring:
            send(y_src.at[i], y_buf.at[i, c * 4 + y], y_sem.at[0, i], y_sem.at[1, i],
                 dev(zh, x, lax.rem(y + d, 4), lax.rem(c + e, 2), n))

    def halves(buf, i):
        return [(buf[i, 4 * h] + buf[i, 4 * h + 1]) + (buf[i, 4 * h + 2] + buf[i, 4 * h + 3]) for h in range(2)]

    def solved_parts(i):
        settle(x_buf.at[i, pl.ds(0, 7)], x_sem.at[1, i])
        parts = halves(x_buf, i)
        y_hl[i] = stacked(jnp.concatenate(parts, axis=1))
        return parts

    def send_out(i, parts):
        o_src[i] = spread_cases(jnp.where(c == 0, parts[0], parts[1]))
        for g in range(2):
            rows = o_src.at[i, pl.ds(pl.multiple_of((g * 4 + x) * 16, 16), 16), :]
            own_place = jnp.logical_and(n == i, zh == g)

            @pl.when(own_place)
            def _():
                o_buf[z] = o_src[i, pl.ds(pl.multiple_of((g * 4 + x) * 16, 16), 16), :]

            @pl.when(jnp.logical_not(own_place))
            def _():
                send(rows, o_buf.at[z], o_s.at[i], o_r.at[0], dev(g, x, y, c, i))

    prepare_inverse(0)
    pass_on("gather end")
    settle(p1_buf.at[pl.ds(0, 7)], p1_sem.at[1])
    lane_window = lax.broadcasted_iota(jnp.int32, (16, 128), 1) // 16

    def gathered(i):
        for h in range(2):
            first = h * 4 + i
            v = p1_buf[0]
            for k in range(1, 8):
                v = jnp.where(lane_window == (first + k) % 8, p1_buf[k], v)
            if first:
                v = pltpu.roll(v, 128 - first * 16, 1)
            g_all[i, :, h * 128:(h + 1) * 128] = v

    gathered(0)
    send_x(0, apply_inverse(0, g_all[0]))
    pass_on("x0")
    for i in range(1, 4):
        gathered(i)
    pass_on("x0 end")
    prepare_factor(1, 0)
    ahead = None
    parts = solved_parts(0)

    for i in range(1, 4):
        total = apply_factor(i, i - 1)
        if i > 1:
            total = ahead + total
        if i == 3:
            total = returned() + total
        send_y(i - 1, total)
        if i == 1:
            send_first(parts)
        send_out(i - 1, parts)
        pass_on(f"y{i - 1}")
        pass_on(f"y{i - 1} end")
        prepare_inverse(i)
        settle(y_buf.at[i - 1, pl.ds(0, 7)], y_sem.at[1, i - 1])
        sums = halves(y_buf, i - 1)
        partial = apply_inverse(i, g_all[i] - jnp.concatenate(sums, axis=1))
        if i < 3:
            send_x(i, partial)
            pass_on(f"x{i}")
            pass_on(f"x{i} end")
            for k in range(1 if i == 2 else 0, i + 1):
                prepare_factor(i + 1, k)
            ahead = apply_factor(i + 1, i - 1)
            parts = solved_parts(i)

    low = lax.rem(lax.broadcasted_iota(jnp.int32, (16, 128), 1) // 8, 2) == 0
    spread[pl.ds(pl.multiple_of(z * 16, 16), 16), :] = jnp.where(low, partial, 0.0)
    spread[pl.ds(pl.multiple_of((1 - zh) * 64 + n * 16, 16), 16), :] = jnp.where(low, 0.0, partial)
    wide_rows = spread[...].T.reshape(8, 2, 8, 128)
    f_src[...] = (wide_rows[:, 0] + wide_rows[:, 1]).reshape(64, 128)
    far = jnp.where(n < 2, zh, 1 - zh)
    for d, g in [(d, far) for d in (2, 1, 3, 0)] + [(d, 1 - far) for d in (2, 1, 3, 0)]:
        xt = lax.rem(x + d, 4)
        at = pl.ds(pl.multiple_of((g * 4 + xt) * 8, 8), 8)
        if d:
            send(f_src.at[at, :], f_buf.at[z * 4 + x], o_s.at[3], o_r.at[1], dev(g, xt, y, c, 3))
        else:
            own_place = jnp.logical_and(n == 3, zh == g)

            @pl.when(own_place)
            def _(at=at):
                f_buf[z * 4 + x] = f_src[at, :]

            @pl.when(jnp.logical_not(own_place))
            def _(at=at, xt=xt, g=g):
                send(f_src.at[at, :], f_buf.at[z * 4 + x], o_s.at[3], o_r.at[1], dev(g, xt, y, c, 3))

    def drain_weights():
        settle(inv_buf.at[0, :, pl.ds(0, 3)], i1_sem.at[0, 0])
        settle(inv_buf.at[pl.ds(1, 3), :, pl.ds(0, 3)], i1_sem.at[0, 1])

        @pl.when(jnp.logical_or(n == 0, n == 3))
        def _():
            settle(inv_buf, i2_s)

        for k in range(3):
            @pl.when(k < n)
            def _(k=k):
                settle(y_buf.at[0, pl.ds(0, 7)], l1_s.at[k])

        @pl.when(n == 1)
        def _():
            settle(inv_buf.at[:, :, pl.ds(0, 7)], l2_s.at[0])

        for i in range(2, 4):
            own = range(1, 3) if i == 3 else range(i)

            @pl.when(n == i)
            def _(own=own):
                for k in own:
                    settle(l_buf.at[pl.ds(0, 2)], l2_s.at[k])

            @pl.when(n == (i + 2) % 4)
            def _(own=own):
                for k in own:
                    settle(inv_buf.at[:, :, pl.ds(0, 3)], l3_s.at[k])

        @pl.when(n == 3)
        def _():
            settle(away_src.at[0], away_sem.at[0])
            settle(away_buf.at[pl.ds(0, 7)], back_sem.at[0])

        @pl.when(n != 3)
        def _():
            settle(away_src, away_sem.at[0])

    drain_weights()
    settle(p0_buf.at[pl.ds(0, 7)], p0_sem.at[0])
    settle(p1_buf.at[pl.ds(0, 7)], p1_sem.at[0])
    for i in range(3):
        settle(x_buf.at[i, pl.ds(0, 7)], x_sem.at[0, i])
        settle(y_buf.at[i, pl.ds(0, 7)], y_sem.at[0, i])

    for i in range(4):
        count = 2 if i < 3 else 8
        sized = o_buf if i < 3 else f_buf

        @pl.when(n == i)
        def _(i=i, count=count, sized=sized):
            settle(sized.at[pl.ds(0, count - 1)], o_s.at[i])

        @pl.when(n != i)
        def _(i=i, count=count, sized=sized):
            settle(sized.at[pl.ds(0, count)], o_s.at[i])

    @pl.when(n < 3)
    def _():
        settle(o_buf.at[pl.ds(0, 7)], o_r.at[0])
        total = o_buf[0]
        for k in range(1, 8):
            total = total + o_buf[k]
        out_ref[...] = total

    @pl.when(n == 3)
    def _():
        settle(f_buf.at[pl.ds(0, 31)], o_r.at[1])
        groups = []
        for first in (0, 16):
            total = f_buf[first]
            for k in range(1, 16):
                total = total + f_buf[first + k]
            groups.append(total)
        left = lax.broadcasted_iota(jnp.int32, (8, 128), 1) < 64
        out_ref[0:8, :] = jnp.where(left, groups[0], groups[1])
        out_ref[8:16, :] = pltpu.roll(jnp.where(left, groups[1], groups[0]), 64, 1)


def body(factor_rows, load_vectors, child_updates, block_inverses):
    dma = pltpu.SemaphoreType.DMA
    out = pl.pallas_call(
        kernel,
        out_shape=pltpu.VMEM((16, 128), F32),
        in_specs=[pl.BlockSpec(memory_space=pltpu.HBM)] * 4,
        out_specs=pl.BlockSpec(memory_space=pltpu.VMEM),
        scratch_shapes=[
            pltpu.VMEM((4, 16, 128), F32), pltpu.VMEM((16, 128), F32),
            pltpu.VMEM((128, 128), F32), pltpu.VMEM((128, 128), F32),
            pltpu.VMEM((8, 16, 128), F32), pltpu.VMEM((16, 128), F32), pltpu.VMEM((8, 16, 128), F32),
            pltpu.VMEM((4, 16, 256), F32),
            pltpu.VMEM((3, 16, 128), F32), pltpu.VMEM((3, 8, 16, 128), F32),
            pltpu.VMEM((3, 16, 128), F32), pltpu.VMEM((3, 8, 16, 128), F32),
            pltpu.VMEM((4, 2, 8, 16, 128), F32), pltpu.VMEM((4, 256, 256), BF16),
            pltpu.VMEM((6, 2, 2, 4, 16, 128), F32), pltpu.VMEM((6, 256, 256), BF16),
            pltpu.VMEM((3, 32, 256), BF16),
            pltpu.VMEM((128, 128), F32), pltpu.VMEM((3, 128, 128), F32),
            pltpu.VMEM((8, 16, 128), F32), pltpu.VMEM((32, 8, 128), F32), pltpu.VMEM((64, 128), F32),
            pltpu.VMEM((2, 16, 128), F32), pltpu.VMEM((8, 16, 128), F32),
            pltpu.VMEM((128, 128), F32), pltpu.VMEM((2, 16, 128), F32),
            dma((7,)), dma((2,)), dma((2,)), dma((2, 3)), dma((2, 3)), dma((2, 2)),
            dma, dma((4,)), dma((3,)), dma((3,)), dma((3,)), dma((6,)), dma((3,)), dma((2,)), dma((2,)), dma((4,)), dma((2,)),
        ],
        compiler_params=pltpu.CompilerParams(collective_id=0, has_side_effects=True, vmem_limit_bytes=60 << 20),
        name="substitution",
    )(
        block_inverses,
        factor_rows.reshape(4, 16, 1024),
        load_vectors.reshape(16, 128),
        child_updates.reshape(4, 16, 128),
    )
    return out.reshape(1, 1, 16, 128)


def solution(mesh):
    placed = (
        P(None, "narrow", None, "wide", None, None),
        P(None, "narrow", "wide", None),
        P("narrow", None, None, "wide", None),
        P(None, "wide", None),
    )
    return jax.shard_map(
        body, mesh=mesh, in_specs=placed, out_specs=P(None, "narrow", "wide", None), check_vma=False
    )
```

```python
import jax
import jax.numpy as jnp
from jax import lax
from jax.experimental import pallas as pl
from jax.experimental.pallas import tpu as pltpu
from jax.sharding import PartitionSpec as P

MESH = pl.DeviceIdType.MESH
F32, BF16 = jnp.float32, jnp.bfloat16

PLAN = {
    "enter": [("f", 1)],
    "gather": [("f", 2), ("s", 1), ("d", 1, True)],
    "gather end": [],
    "x0": [],
    "x0 end": [("a", 1), ("f", 3), ("r", 2)],
    "y0": [("i", 2, False)],
    "y0 end": [],
    "x1": [],
    "x1 end": [("j", 2)],
    "y1": [("m",), ("r", 3), ("i", 3, False)],
    "y1 end": [],
    "x2": [],
    "x2 end": [("j", 3)],
    "y2": [],
    "y2 end": [],
}
WHOLE = (0, 1)


def kernel(inv_ref, fac_ref, load_ref, child_ref, out_ref,
           kid_v, load_v, stage, staged, p0_buf, p1_src, p1_buf, g_all,
           x_src, x_buf, y_src, y_buf, inv_buf, w_inv, l_buf, w_l, y_hl,
           spread, o_src, o_buf, f_buf, f_src, away_src, away_buf, back_src, back_buf,
           loc_sem, p0_sem, p1_sem, x_sem, y_sem, i1_sem, i2_s, i2_r, l1_s, l1_r, l2_s, l2_r, l3_s, away_sem, back_sem,
           o_s, o_r):
    w = lax.axis_index("wide")
    n = lax.axis_index("narrow")
    c = lax.rem(w, 2)
    y = lax.rem(w // 2, 4)
    x = lax.rem(w // 8, 4)
    zh = w // 32
    z = zh * 4 + n
    yc = y * 2 + c

    def dev(zh_, x_, y_, c_, n_):
        return {"wide": ((zh_ * 4 + x_) * 4 + y_) * 2 + c_, "narrow": n_}

    def zdev(z_):
        return dev(z_ // 4, x, y, c, lax.rem(z_, 4))

    def send(src, dst, s_sem, r_sem, to):
        pltpu.make_async_remote_copy(src_ref=src, dst_ref=dst, send_sem=s_sem, recv_sem=r_sem,
                                     device_id=to, device_id_type=MESH).start()

    def settle(like, sem):
        pltpu.make_async_copy(like, like, sem).wait()

    ring = [(2, 0), (2, 1), (1, 0), (1, 1), (3, 0), (3, 1), (0, 1)]

    barrier = pltpu.get_barrier_semaphore()
    near = jnp.where(n < 2, 3, 0)

    def greet(to):
        pl.semaphore_signal(barrier, inc=1, device_id=to, device_id_type=MESH)

    greet(zdev(lax.rem(z + 4, 8)))
    greet(dev(1 - zh, lax.rem(x + 2, 4), y, c, near))
    for d in (3, 5):
        greet(zdev(lax.rem(z + d, 8)))
    for d in (1, 3):
        greet(dev(1 - zh, lax.rem(x + d, 4), y, c, near))
    for d in (2, 6):
        greet(zdev(lax.rem(z + d, 8)))
    for d, e in ring:
        greet(dev(zh, x, lax.rem(y + d, 4), lax.rem(c + e, 2), n))
    for d, e in ring[:-1]:
        greet(dev(zh, lax.rem(x + d, 4), y, lax.rem(c + e, 2), n))
    for d in (1, 7):
        greet(zdev(lax.rem(z + d, 8)))
    at_end = jnp.logical_or(n == 0, n == 3)

    kid_in = pltpu.make_async_copy(child_ref, kid_v, loc_sem.at[0])
    load_in = pltpu.make_async_copy(load_ref, load_v, loc_sem.at[1])
    kid_in.start()
    load_in.start()
    own_inv = [pltpu.make_async_copy(inv_ref.at[:, :, pl.ds(pl.multiple_of(h * 512 + x * 128, 128), 128)],
                                     inv_buf.at[:, h, zh * 4 + x], loc_sem.at[2 + h]) for h in range(2)]
    for cp in own_inv:
        cp.start()

    def own_pair(k):
        return (n * (n - 1)) // 2 + k

    def fac_slice(k, x_, c_):
        return fac_ref.at[k, :, pl.ds(pl.multiple_of(c_ * 512 + x_ * 128, 128), 128)]

    def own_fac(k):
        return pltpu.make_async_copy(fac_slice(k, x, c), l_buf.at[own_pair(k), c, zh, x], loc_sem.at[4 + k])

    for k in range(3):
        @pl.when(k < n)
        def _(k=k):
            own_fac(k).start()

    stage[...] = jnp.zeros_like(stage)
    spread[...] = jnp.zeros_like(spread)
    kid_in.wait()
    load_in.wait()

    def window(i):
        return pl.ds(pl.multiple_of(lax.rem(zh * 4 + i + yc, 8) * 16, 16), 16)

    for i in range(4):
        stage[window(i), :] = -kid_v[i]
    stage[window(n), :] = stage[window(n), :] + load_v[...]
    staged[...] = stage[...].T
    p0_buf[z] = staged[pl.ds(pl.multiple_of(z * 16, 16), 16), :]

    @pl.when(at_end)
    def _():
        pl.semaphore_wait(barrier, 26)

    @pl.when(jnp.logical_not(at_end))
    def _():
        pl.semaphore_wait(barrier, 20)

    for d in (4, 3, 5, 2, 6, 1, 7):
        to = lax.rem(z + d, 8)
        send(staged.at[pl.ds(pl.multiple_of(to * 16, 16), 16), :], p0_buf.at[z], p0_sem.at[0], p0_sem.at[1], zdev(to))

    def start_inverse(part):
        for d in (2, 1, 3):
            xt = lax.rem(x + d, 4)
            for h in range(2):
                cols = pl.ds(pl.multiple_of(h * 512 + xt * 128, 128), 128)
                rows = pl.ds(0, 1) if part == 0 else pl.ds(1, 3)
                send(inv_ref.at[rows, :, cols], inv_buf.at[rows, h, zh * 4 + x], i1_sem.at[0, part], i1_sem.at[1, part],
                     dev(zh, xt, y, c, n))

    def start_factor():
        for k in range(3):
            @pl.when(k < n)
            def _(k=k):
                for d, e in ring:
                    xt, ct = lax.rem(x + d, 4), lax.rem(c + e, 2)
                    send(fac_slice(k, xt, ct), l_buf.at[own_pair(k), c, zh, x], l1_s.at[k], l1_r.at[k],
                         dev(zh, xt, y, ct, n))

    def direct_inverse(i, both):
        for side in range(2):
            @pl.when(n == 3 * side)
            def _(side=side):
                for d in (2, 1, 3, 0):
                    xt = lax.rem(x + d, 4)
                    for h in range(2):
                        cols = pl.ds(pl.multiple_of(h * 512 + xt * 128, 128), 128)
                        for lane in ((3 - 3 * side, 2 - side) if both else (3 - 3 * side,)):
                            send(inv_ref.at[i, :, cols], inv_buf.at[i, h, zh * 4 + x], i2_s, i2_r.at[i],
                                 dev(1 - zh, xt, y, c, lane))

    direct_inverse(0, True)
    for part in range(2):
        @pl.when(n == 1 if part == 0 else n > 1)
        def _():
            start_factor()
        if part == 0:
            start_inverse(0)

    def arrived_inverse(part):
        settle(inv_buf.at[pl.ds(part, 1 + 2 * part), :, pl.ds(0, 3)], i1_sem.at[1, part])

    def forward_inverse(i, both):
        mine = inv_buf.at[i, :, pl.ds(pl.multiple_of(zh * 4, 4), 4)]
        for side in range(2):
            @pl.when(n == 3 * side)
            def _(side=side):
                send(mine, mine, i2_s, i2_r.at[i], dev(1 - zh, x, y, c, 3 - 3 * side))
                if both:
                    send(mine, mine, i2_s, i2_r.at[i], dev(1 - zh, x, y, c, 2 - side))

    def relay_inverse(i):
        other = inv_buf.at[i, :, pl.ds(pl.multiple_of(4 - zh * 4, 4), 4)]

        @pl.when(jnp.logical_or(n == 0, n == 3))
        def _():
            settle(inv_buf.at[i, :, pl.ds(0, 4)], i2_r.at[i])
        for side in range(2):
            @pl.when(n == 3 * side)
            def _(side=side):
                send(other, other, i2_s, i2_r.at[i], dev(zh, x, y, c, 1 + side))

    for cp in own_inv:
        cp.wait()
    arrived_inverse(0)

    def forward_factor(i):
        @pl.when(n == i)
        def _():
            own = range(1, 3) if i == 3 else range(i)
            for k in own:
                own_fac(k).wait()
                settle(y_buf.at[0, pl.ds(0, 7)], l1_r.at[k])
            for ds in (((4, 3, 5, 2, 6, 1, 7),) if i == 1 else ((2, 6), (1, 7))):
                for k in own:
                    pair = i * (i - 1) // 2 + k
                    mine = l_buf.at[pair, :, zh]
                    for d in ds:
                        send(mine, mine, l2_s.at[k], l2_r.at[pair], zdev(lax.rem(z + d, 8)))

    def relay_factor(i):
        @pl.when(n == (i + 2) % 4)
        def _():
            own = range(1, 3) if i == 3 else range(i)
            for k in own:
                pair = i * (i - 1) // 2 + k
                settle(l_buf.at[pair], l2_r.at[pair])
            for far in range(2):
                for k in own:
                    pair = i * (i - 1) // 2 + k
                    for side in range(2):
                        held = l_buf.at[pair, :, lax.rem(z + (2 if side else 6), 8) // 4]
                        hops = 1 + far

                        @pl.when(c == side if far else c < 2)
                        def _(held=held, hops=hops, side=side, k=k, pair=pair):
                            send(held, held, l3_s.at[k], l2_r.at[pair], zdev(lax.rem(z + (8 - hops if side else hops), 8)))

    def send_first(parts):
        for g in range(2):
            piece = jnp.concatenate([p[:, g * 64:(g + 1) * 64] for p in parts], axis=1)
            away_src[g] = piece
            here = jnp.logical_and(n == 3, zh == g)

            @pl.when(here)
            def _(piece=piece):
                away_buf[z] = piece

            @pl.when(jnp.logical_not(here))
            def _(g=g):
                send(away_src.at[g], away_buf.at[z], away_sem.at[0], away_sem.at[1], dev(g, x, y, c, 3))

    def multiply_first():
        @pl.when(n == 3)
        def _():
            own_fac(0).wait()
            settle(y_buf.at[0, pl.ds(0, 7)], l1_r.at[0])
            settle(away_buf.at[pl.ds(0, 7)], away_sem.at[1])
            hi, lo = split(away_buf[...].reshape(128, 128))
            w_hi, w_lo = split(l_buf[3, :, zh].reshape(128, 128))
            d = jnp.dot(jnp.concatenate([hi, lo], axis=0), jnp.concatenate([w_hi, w_lo], axis=1), preferred_element_type=F32)
            back_src[...] = (d[0:128, 0:128] + d[128:256, 128:256]) + (d[0:128, 128:256] + d[128:256, 0:128])
            back_buf[zh] = back_src[pl.ds(pl.multiple_of(z * 16, 16), 16), :]
            for m in (4, 3, 5, 2, 6, 1, 7):
                to = lax.rem(z + m, 8)
                send(back_src.at[pl.ds(pl.multiple_of(to * 16, 16), 16), :], back_buf.at[zh], back_sem.at[0], back_sem.at[1],
                     zdev(to))

    def returned():
        @pl.when(n == 3)
        def _():
            settle(back_buf.at[0], back_sem.at[1])

        @pl.when(n != 3)
        def _():
            settle(back_buf, back_sem.at[1])
        return back_buf[0] + back_buf[1]

    def pass_on(point):
        for what, *args in PLAN[point]:
            {"f": forward_factor, "r": relay_factor, "m": multiply_first, "i": forward_inverse, "j": relay_inverse,
             "a": arrived_inverse, "s": start_inverse, "d": direct_inverse}[what](*args)

    pass_on("enter")

    settle(p0_buf.at[pl.ds(0, 7)], p0_sem.at[1])
    own = p0_buf[0]
    for k in range(1, 8):
        own = own + p0_buf[k]
    p1_src[...] = own
    p1_buf[yc] = own
    for d, e in ring:
        send(p1_src, p1_buf.at[yc], p1_sem.at[0], p1_sem.at[1], dev(zh, x, lax.rem(y + d, 4), lax.rem(c + e, 2), n))

    pass_on("gather")

    def split(v):
        hi = v.astype(BF16)
        return hi, (v - hi.astype(F32)).astype(BF16)

    def prepare_inverse(i):
        if i in WHOLE:
            settle(inv_buf.at[i, :, pl.ds(0, 4)], i2_r.at[i])
        else:
            @pl.when(jnp.logical_and(n != 0, n != 3))
            def _():
                settle(inv_buf.at[i, :, pl.ds(0, 4)], i2_r.at[i])
        for h in range(2):
            hi, lo = split(inv_buf[i, h].reshape(128, 128))
            w_inv[i, 0:128, h * 128:(h + 1) * 128] = hi
            w_inv[i, 128:256, h * 128:(h + 1) * 128] = lo

    def prepare_factor(i, k):
        pair = i * (i - 1) // 2 + k

        passes_on = -1 if i == 1 else (i + 2) % 4

        @pl.when(n == i)
        def _():
            settle(l_buf.at[pair, :, 0], l2_r.at[pair])

        @pl.when(jnp.logical_and(n != i, n != passes_on))
        def _():
            settle(l_buf.at[pair], l2_r.at[pair])
        hi, lo = split(l_buf[pair].reshape(256, 128))
        w_l[pair, :, 0:128] = hi
        w_l[pair, :, 128:256] = lo

    def fold(d):
        return (d[0:16, 0:128] + d[16:32, 128:256]) + (d[0:16, 128:256] + d[16:32, 0:128])

    def stacked(v):
        hi, lo = split(v)
        return jnp.concatenate([hi, lo], axis=0)

    def apply_inverse(i, r):
        return fold(lax.dot_general(stacked(r), w_inv[i], (((1,), (1,)), ((), ())), preferred_element_type=F32))

    def apply_factor(i, k):
        pair = i * (i - 1) // 2 + k
        return fold(jnp.dot(y_hl[k], w_l[pair], preferred_element_type=F32))

    def spread_cases(piece):
        at = pl.ds(pl.multiple_of(z * 16, 16), 16)
        spread[at, :] = piece
        return spread[...].T

    def send_x(i, partial):
        x_src[i] = partial
        x_buf[i, c * 4 + x] = partial
        for d, e in ring:
            send(x_src.at[i], x_buf.at[i, c * 4 + x], x_sem.at[0, i], x_sem.at[1, i],
                 dev(zh, lax.rem(x + d, 4), y, lax.rem(c + e, 2), n))

    def send_y(i, partial):
        y_src[i] = partial
        y_buf[i, c * 4 + y] = partial
        for d, e in ring:
            send(y_src.at[i], y_buf.at[i, c * 4 + y], y_sem.at[0, i], y_sem.at[1, i],
                 dev(zh, x, lax.rem(y + d, 4), lax.rem(c + e, 2), n))

    def halves(buf, i):
        return [(buf[i, 4 * h] + buf[i, 4 * h + 1]) + (buf[i, 4 * h + 2] + buf[i, 4 * h + 3]) for h in range(2)]

    def solved_parts(i):
        settle(x_buf.at[i, pl.ds(0, 7)], x_sem.at[1, i])
        parts = halves(x_buf, i)
        y_hl[i] = stacked(jnp.concatenate(parts, axis=1))
        return parts

    def send_out(i, parts):
        o_src[i] = spread_cases(jnp.where(c == 0, parts[0], parts[1]))
        for g in range(2):
            rows = o_src.at[i, pl.ds(pl.multiple_of((g * 4 + x) * 16, 16), 16), :]
            own_place = jnp.logical_and(n == i, zh == g)

            @pl.when(own_place)
            def _():
                o_buf[z] = o_src[i, pl.ds(pl.multiple_of((g * 4 + x) * 16, 16), 16), :]

            @pl.when(jnp.logical_not(own_place))
            def _():
                send(rows, o_buf.at[z], o_s.at[i], o_r.at[0], dev(g, x, y, c, i))

    prepare_inverse(0)
    pass_on("gather end")
    settle(p1_buf.at[pl.ds(0, 7)], p1_sem.at[1])
    lane_window = lax.broadcasted_iota(jnp.int32, (16, 128), 1) // 16

    def gathered(i):
        for h in range(2):
            first = h * 4 + i
            v = p1_buf[0]
            for k in range(1, 8):
                v = jnp.where(lane_window == (first + k) % 8, p1_buf[k], v)
            if first:
                v = pltpu.roll(v, 128 - first * 16, 1)
            g_all[i, :, h * 128:(h + 1) * 128] = v

    gathered(0)
    send_x(0, apply_inverse(0, g_all[0]))
    pass_on("x0")
    for i in range(1, 4):
        gathered(i)
    pass_on("x0 end")
    prepare_factor(1, 0)
    ahead = None
    parts = solved_parts(0)

    for i in range(1, 4):
        total = apply_factor(i, i - 1)
        if i > 1:
            total = ahead + total
        if i == 3:
            total = returned() + total
        send_y(i - 1, total)
        if i == 1:
            send_first(parts)
        send_out(i - 1, parts)
        pass_on(f"y{i - 1}")
        pass_on(f"y{i - 1} end")
        prepare_inverse(i)
        settle(y_buf.at[i - 1, pl.ds(0, 7)], y_sem.at[1, i - 1])
        sums = halves(y_buf, i - 1)
        partial = apply_inverse(i, g_all[i] - jnp.concatenate(sums, axis=1))
        if i < 3:
            send_x(i, partial)
            pass_on(f"x{i}")
            pass_on(f"x{i} end")
            for k in range(1 if i == 2 else 0, i + 1):
                prepare_factor(i + 1, k)
            ahead = apply_factor(i + 1, i - 1)
            parts = solved_parts(i)

    quad = lax.rem(lax.broadcasted_iota(jnp.int32, (16, 128), 1) // 4, 4)
    for j in range(4):
        spread[pl.ds(pl.multiple_of(lax.rem(z + 2 * j, 8) * 16, 16), 16), :] = jnp.where(quad == j, partial, 0.0)
    eights = spread[...].T.reshape(8, 2, 8, 128)
    eights = eights[:, 0] + eights[:, 1]
    f_src[...] = eights[:, 0:4] + eights[:, 4:8]
    far = jnp.where(n < 2, zh, 1 - zh)
    for d, g in [(d, far) for d in (2, 1, 3, 0)] + [(d, 1 - far) for d in (2, 1, 3, 0)]:
        xt = lax.rem(x + d, 4)
        at = g * 4 + xt
        if d:
            send(f_src.at[at], f_buf.at[z * 4 + x], o_s.at[3], o_r.at[1], dev(g, xt, y, c, 3))
        else:
            own_place = jnp.logical_and(n == 3, zh == g)

            @pl.when(own_place)
            def _(at=at):
                f_buf[z * 4 + x] = f_src[at]

            @pl.when(jnp.logical_not(own_place))
            def _(at=at, xt=xt, g=g):
                send(f_src.at[at], f_buf.at[z * 4 + x], o_s.at[3], o_r.at[1], dev(g, xt, y, c, 3))

    def drain_weights():
        settle(inv_buf.at[0, :, pl.ds(0, 3)], i1_sem.at[0, 0])
        settle(inv_buf.at[pl.ds(1, 3), :, pl.ds(0, 3)], i1_sem.at[0, 1])

        @pl.when(jnp.logical_or(n == 0, n == 3))
        def _():
            settle(inv_buf, i2_s)

        for k in range(3):
            @pl.when(k < n)
            def _(k=k):
                settle(y_buf.at[0, pl.ds(0, 7)], l1_s.at[k])

        @pl.when(n == 1)
        def _():
            settle(inv_buf.at[:, :, pl.ds(0, 7)], l2_s.at[0])

        for i in range(2, 4):
            own = range(1, 3) if i == 3 else range(i)

            @pl.when(n == i)
            def _(own=own):
                for k in own:
                    settle(l_buf.at[pl.ds(0, 2)], l2_s.at[k])

            @pl.when(n == (i + 2) % 4)
            def _(own=own):
                for k in own:
                    settle(inv_buf.at[:, :, pl.ds(0, 3)], l3_s.at[k])

        @pl.when(n == 3)
        def _():
            settle(away_src.at[0], away_sem.at[0])
            settle(away_buf.at[pl.ds(0, 7)], back_sem.at[0])

        @pl.when(n != 3)
        def _():
            settle(away_src, away_sem.at[0])

    drain_weights()
    settle(p0_buf.at[pl.ds(0, 7)], p0_sem.at[0])
    settle(p1_buf.at[pl.ds(0, 7)], p1_sem.at[0])
    for i in range(3):
        settle(x_buf.at[i, pl.ds(0, 7)], x_sem.at[0, i])
        settle(y_buf.at[i, pl.ds(0, 7)], y_sem.at[0, i])

    for i in range(4):
        count = 2 if i < 3 else 8
        sized = o_buf if i < 3 else f_buf

        @pl.when(n == i)
        def _(i=i, count=count, sized=sized):
            settle(sized.at[pl.ds(0, count - 1)], o_s.at[i])

        @pl.when(n != i)
        def _(i=i, count=count, sized=sized):
            settle(sized.at[pl.ds(0, count)], o_s.at[i])

    @pl.when(n < 3)
    def _():
        settle(o_buf.at[pl.ds(0, 7)], o_r.at[0])
        total = o_buf[0]
        for k in range(1, 8):
            total = total + o_buf[k]
        out_ref[...] = total

    @pl.when(n == 3)
    def _():
        settle(f_buf.at[pl.ds(0, 31)], o_r.at[1])
        groups = []
        for q in range(4):
            total = f_buf[8 * q]
            for k in range(1, 8):
                total = total + f_buf[8 * q + k]
            groups.append(total)
        pair = lax.broadcasted_iota(jnp.int32, (4, 128), 1) // 32
        for j in range(4):
            rows = groups[0]
            for q in range(1, 4):
                rows = jnp.where(pair == (q + j) % 4, groups[q], rows)
            out_ref[4 * j:4 * j + 4, :] = pltpu.roll(rows, (128 - 32 * j) % 128, 1) if j else rows


def body(factor_rows, load_vectors, child_updates, block_inverses):
    dma = pltpu.SemaphoreType.DMA
    out = pl.pallas_call(
        kernel,
        out_shape=pltpu.VMEM((16, 128), F32),
        in_specs=[pl.BlockSpec(memory_space=pltpu.HBM)] * 4,
        out_specs=pl.BlockSpec(memory_space=pltpu.VMEM),
        scratch_shapes=[
            pltpu.VMEM((4, 16, 128), F32), pltpu.VMEM((16, 128), F32),
            pltpu.VMEM((128, 128), F32), pltpu.VMEM((128, 128), F32),
            pltpu.VMEM((8, 16, 128), F32), pltpu.VMEM((16, 128), F32), pltpu.VMEM((8, 16, 128), F32),
            pltpu.VMEM((4, 16, 256), F32),
            pltpu.VMEM((3, 16, 128), F32), pltpu.VMEM((3, 8, 16, 128), F32),
            pltpu.VMEM((3, 16, 128), F32), pltpu.VMEM((3, 8, 16, 128), F32),
            pltpu.VMEM((4, 2, 8, 16, 128), F32), pltpu.VMEM((4, 256, 256), BF16),
            pltpu.VMEM((6, 2, 2, 4, 16, 128), F32), pltpu.VMEM((6, 256, 256), BF16),
            pltpu.VMEM((3, 32, 256), BF16),
            pltpu.VMEM((128, 128), F32), pltpu.VMEM((3, 128, 128), F32),
            pltpu.VMEM((8, 16, 128), F32), pltpu.VMEM((32, 4, 128), F32), pltpu.VMEM((8, 4, 128), F32),
            pltpu.VMEM((2, 16, 128), F32), pltpu.VMEM((8, 16, 128), F32),
            pltpu.VMEM((128, 128), F32), pltpu.VMEM((2, 16, 128), F32),
            dma((7,)), dma((2,)), dma((2,)), dma((2, 3)), dma((2, 3)), dma((2, 2)),
            dma, dma((4,)), dma((3,)), dma((3,)), dma((3,)), dma((6,)), dma((3,)), dma((2,)), dma((2,)), dma((4,)), dma((2,)),
        ],
        compiler_params=pltpu.CompilerParams(collective_id=0, has_side_effects=True, vmem_limit_bytes=60 << 20),
        name="substitution",
    )(
        block_inverses,
        factor_rows.reshape(4, 16, 1024),
        load_vectors.reshape(16, 128),
        child_updates.reshape(4, 16, 128),
    )
    return out.reshape(1, 1, 16, 128)


def solution(mesh):
    placed = (
        P(None, "narrow", None, "wide", None, None),
        P(None, "narrow", "wide", None),
        P("narrow", None, None, "wide", None),
        P(None, "wide", None),
    )
    return jax.shard_map(
        body, mesh=mesh, in_specs=placed, out_specs=P(None, "narrow", "wide", None), check_vma=False
    )
```

```python
import jax
import jax.numpy as jnp
from jax import lax
from jax.experimental import pallas as pl
from jax.experimental.pallas import tpu as pltpu
from jax.sharding import PartitionSpec as P

MESH = pl.DeviceIdType.MESH
F32, BF16 = jnp.float32, jnp.bfloat16

PLAN = {
    "enter": [("f", 1), ("f", 2)],
    "gather": [("s", 1), ("d", 1, True)],
    "gather end": [],
    "x0": [],
    "x0 end": [("a", 1), ("f", 3), ("r", 2)],
    "y0": [("i", 2, False)],
    "y0 end": [],
    "x1": [],
    "x1 end": [("j", 2)],
    "y1": [("m",), ("r", 3), ("i", 3, False)],
    "y1 end": [],
    "x2": [],
    "x2 end": [("j", 3)],
    "y2": [],
    "y2 end": [],
}
WHOLE = (0, 1)


def kernel(inv_ref, fac_ref, load_ref, child_ref, out_ref,
           kid_v, load_v, stage, staged, p0_buf, p1_src, p1_buf, g_all,
           x_src, x_buf, y_src, y_buf, inv_buf, w_inv, l_buf, w_l, y_hl,
           spread, o_src, o_buf, f_buf, f_src, away_src, away_buf, back_src, back_buf,
           loc_sem, p0_sem, p1_sem, x_sem, y_sem, i1_sem, i2_s, i2_r, l1_s, l1_r, l2_s, l2_r, l3_s, away_sem, back_sem,
           o_s, o_r):
    w = lax.axis_index("wide")
    n = lax.axis_index("narrow")
    c = lax.rem(w, 2)
    y = lax.rem(w // 2, 4)
    x = lax.rem(w // 8, 4)
    zh = w // 32
    z = zh * 4 + n
    yc = y * 2 + c

    def dev(zh_, x_, y_, c_, n_):
        return {"wide": ((zh_ * 4 + x_) * 4 + y_) * 2 + c_, "narrow": n_}

    def zdev(z_):
        return dev(z_ // 4, x, y, c, lax.rem(z_, 4))

    def send(src, dst, s_sem, r_sem, to):
        pltpu.make_async_remote_copy(src_ref=src, dst_ref=dst, send_sem=s_sem, recv_sem=r_sem,
                                     device_id=to, device_id_type=MESH).start()

    def settle(like, sem):
        pltpu.make_async_copy(like, like, sem).wait()

    ring = [(2, 0), (2, 1), (1, 0), (1, 1), (3, 0), (3, 1), (0, 1)]

    barrier = pltpu.get_barrier_semaphore()
    for d in (4, 3, 5, 2, 6, 1, 7):
        pl.semaphore_signal(barrier, inc=1, device_id=zdev(lax.rem(z + d, 8)), device_id_type=MESH)
    for d, e in ring:
        pl.semaphore_signal(barrier, inc=1, device_id=dev(zh, x, lax.rem(y + d, 4), lax.rem(c + e, 2), n),
                            device_id_type=MESH)
    for d, e in ring[:-1]:
        pl.semaphore_signal(barrier, inc=1, device_id=dev(zh, lax.rem(x + d, 4), y, lax.rem(c + e, 2), n),
                            device_id_type=MESH)

    near = jnp.where(n < 2, 3, 0)
    for d in (2, 1, 3):
        pl.semaphore_signal(barrier, inc=1, device_id=dev(1 - zh, lax.rem(x + d, 4), y, c, near), device_id_type=MESH)
    at_end = jnp.logical_or(n == 0, n == 3)

    kid_in = pltpu.make_async_copy(child_ref, kid_v, loc_sem.at[0])
    load_in = pltpu.make_async_copy(load_ref, load_v, loc_sem.at[1])
    kid_in.start()
    load_in.start()
    own_inv = [pltpu.make_async_copy(inv_ref.at[:, :, pl.ds(pl.multiple_of(h * 512 + x * 128, 128), 128)],
                                     inv_buf.at[:, h, zh * 4 + x], loc_sem.at[2 + h]) for h in range(2)]
    for cp in own_inv:
        cp.start()

    def own_pair(k):
        return (n * (n - 1)) // 2 + k

    def fac_slice(k, x_, c_):
        return fac_ref.at[k, :, pl.ds(pl.multiple_of(c_ * 512 + x_ * 128, 128), 128)]

    def own_fac(k):
        return pltpu.make_async_copy(fac_slice(k, x, c), l_buf.at[own_pair(k), c, zh, x], loc_sem.at[4 + k])

    for k in range(3):
        @pl.when(k < n)
        def _(k=k):
            own_fac(k).start()

    stage[...] = jnp.zeros_like(stage)
    spread[...] = jnp.zeros_like(spread)
    kid_in.wait()
    load_in.wait()

    def window(i):
        return pl.ds(pl.multiple_of(lax.rem(zh * 4 + i + yc, 8) * 16, 16), 16)

    for i in range(4):
        stage[window(i), :] = -kid_v[i]
    stage[window(n), :] = stage[window(n), :] + load_v[...]
    staged[...] = stage[...].T
    p0_buf[z] = staged[pl.ds(pl.multiple_of(z * 16, 16), 16), :]

    @pl.when(at_end)
    def _():
        pl.semaphore_wait(barrier, 26)

    @pl.when(jnp.logical_not(at_end))
    def _():
        pl.semaphore_wait(barrier, 20)

    for d in (4, 3, 5, 2, 6, 1, 7):
        to = lax.rem(z + d, 8)
        send(staged.at[pl.ds(pl.multiple_of(to * 16, 16), 16), :], p0_buf.at[z], p0_sem.at[0], p0_sem.at[1], zdev(to))

    def start_inverse(part):
        for d in (2, 1, 3):
            xt = lax.rem(x + d, 4)
            for h in range(2):
                cols = pl.ds(pl.multiple_of(h * 512 + xt * 128, 128), 128)
                rows = pl.ds(0, 1) if part == 0 else pl.ds(1, 3)
                send(inv_ref.at[rows, :, cols], inv_buf.at[rows, h, zh * 4 + x], i1_sem.at[0, part], i1_sem.at[1, part],
                     dev(zh, xt, y, c, n))

    def start_factor():
        for k in range(3):
            @pl.when(k < n)
            def _(k=k):
                for d, e in ring:
                    xt, ct = lax.rem(x + d, 4), lax.rem(c + e, 2)
                    send(fac_slice(k, xt, ct), l_buf.at[own_pair(k), c, zh, x], l1_s.at[k], l1_r.at[k],
                         dev(zh, xt, y, ct, n))

    def direct_inverse(i, both):
        for side in range(2):
            @pl.when(n == 3 * side)
            def _(side=side):
                for d in (2, 1, 3, 0):
                    xt = lax.rem(x + d, 4)
                    for h in range(2):
                        cols = pl.ds(pl.multiple_of(h * 512 + xt * 128, 128), 128)
                        for lane in ((3 - 3 * side, 2 - side) if both else (3 - 3 * side,)):
                            send(inv_ref.at[i, :, cols], inv_buf.at[i, h, zh * 4 + x], i2_s, i2_r.at[i],
                                 dev(1 - zh, xt, y, c, lane))

    direct_inverse(0, True)
    for part in range(2):
        @pl.when(n == 1 if part == 0 else n > 1)
        def _():
            start_factor()
        if part == 0:
            start_inverse(0)

    def arrived_inverse(part):
        settle(inv_buf.at[pl.ds(part, 1 + 2 * part), :, pl.ds(0, 3)], i1_sem.at[1, part])

    def forward_inverse(i, both):
        mine = inv_buf.at[i, :, pl.ds(pl.multiple_of(zh * 4, 4), 4)]
        for side in range(2):
            @pl.when(n == 3 * side)
            def _(side=side):
                send(mine, mine, i2_s, i2_r.at[i], dev(1 - zh, x, y, c, 3 - 3 * side))
                if both:
                    send(mine, mine, i2_s, i2_r.at[i], dev(1 - zh, x, y, c, 2 - side))

    def relay_inverse(i):
        other = inv_buf.at[i, :, pl.ds(pl.multiple_of(4 - zh * 4, 4), 4)]

        @pl.when(jnp.logical_or(n == 0, n == 3))
        def _():
            settle(inv_buf.at[i, :, pl.ds(0, 4)], i2_r.at[i])
        for side in range(2):
            @pl.when(n == 3 * side)
            def _(side=side):
                send(other, other, i2_s, i2_r.at[i], dev(zh, x, y, c, 1 + side))

    for cp in own_inv:
        cp.wait()
    arrived_inverse(0)

    def forward_factor(i):
        @pl.when(n == i)
        def _():
            own = range(1, 3) if i == 3 else range(i)
            for k in own:
                own_fac(k).wait()
                settle(y_buf.at[0, pl.ds(0, 7)], l1_r.at[k])
            for ds in (((4, 3, 5, 2, 6, 1, 7),) if i == 1 else ((2, 6), (1, 7))):
                for k in own:
                    pair = i * (i - 1) // 2 + k
                    mine = l_buf.at[pair, :, zh]
                    for d in ds:
                        send(mine, mine, l2_s.at[k], l2_r.at[pair], zdev(lax.rem(z + d, 8)))

    def relay_factor(i):
        @pl.when(n == (i + 2) % 4)
        def _():
            own = range(1, 3) if i == 3 else range(i)
            for k in own:
                pair = i * (i - 1) // 2 + k
                settle(l_buf.at[pair], l2_r.at[pair])
            for far in range(2):
                for k in own:
                    pair = i * (i - 1) // 2 + k
                    for side in range(2):
                        held = l_buf.at[pair, :, lax.rem(z + (2 if side else 6), 8) // 4]
                        hops = 1 + far

                        @pl.when(c == side if far else c < 2)
                        def _(held=held, hops=hops, side=side, k=k, pair=pair):
                            send(held, held, l3_s.at[k], l2_r.at[pair], zdev(lax.rem(z + (8 - hops if side else hops), 8)))

    def send_first(parts):
        for g in range(2):
            piece = jnp.concatenate([p[:, g * 64:(g + 1) * 64] for p in parts], axis=1)
            away_src[g] = piece
            here = jnp.logical_and(n == 3, zh == g)

            @pl.when(here)
            def _(piece=piece):
                away_buf[z] = piece

            @pl.when(jnp.logical_not(here))
            def _(g=g):
                send(away_src.at[g], away_buf.at[z], away_sem.at[0], away_sem.at[1], dev(g, x, y, c, 3))

    def multiply_first():
        @pl.when(n == 3)
        def _():
            own_fac(0).wait()
            settle(y_buf.at[0, pl.ds(0, 7)], l1_r.at[0])
            settle(away_buf.at[pl.ds(0, 7)], away_sem.at[1])
            hi, lo = split(away_buf[...].reshape(128, 128))
            w_hi, w_lo = split(l_buf[3, :, zh].reshape(128, 128))
            d = jnp.dot(jnp.concatenate([hi, lo], axis=0), jnp.concatenate([w_hi, w_lo], axis=1), preferred_element_type=F32)
            back_src[...] = (d[0:128, 0:128] + d[128:256, 128:256]) + (d[0:128, 128:256] + d[128:256, 0:128])
            back_buf[zh] = back_src[pl.ds(pl.multiple_of(z * 16, 16), 16), :]
            for m in (4, 3, 5, 2, 6, 1, 7):
                to = lax.rem(z + m, 8)
                send(back_src.at[pl.ds(pl.multiple_of(to * 16, 16), 16), :], back_buf.at[zh], back_sem.at[0], back_sem.at[1],
                     zdev(to))

    def returned():
        @pl.when(n == 3)
        def _():
            settle(back_buf.at[0], back_sem.at[1])

        @pl.when(n != 3)
        def _():
            settle(back_buf, back_sem.at[1])
        return back_buf[0] + back_buf[1]

    def pass_on(point):
        for what, *args in PLAN[point]:
            {"f": forward_factor, "r": relay_factor, "m": multiply_first, "i": forward_inverse, "j": relay_inverse,
             "a": arrived_inverse, "s": start_inverse, "d": direct_inverse}[what](*args)

    pass_on("enter")

    settle(p0_buf.at[pl.ds(0, 7)], p0_sem.at[1])
    own = p0_buf[0]
    for k in range(1, 8):
        own = own + p0_buf[k]
    p1_src[...] = own
    p1_buf[yc] = own
    for d, e in ring:
        send(p1_src, p1_buf.at[yc], p1_sem.at[0], p1_sem.at[1], dev(zh, x, lax.rem(y + d, 4), lax.rem(c + e, 2), n))

    pass_on("gather")

    def split(v):
        hi = v.astype(BF16)
        return hi, (v - hi.astype(F32)).astype(BF16)

    def prepare_inverse(i):
        if i in WHOLE:
            settle(inv_buf.at[i, :, pl.ds(0, 4)], i2_r.at[i])
        else:
            @pl.when(jnp.logical_and(n != 0, n != 3))
            def _():
                settle(inv_buf.at[i, :, pl.ds(0, 4)], i2_r.at[i])
        for h in range(2):
            hi, lo = split(inv_buf[i, h].reshape(128, 128))
            w_inv[i, 0:128, h * 128:(h + 1) * 128] = hi
            w_inv[i, 128:256, h * 128:(h + 1) * 128] = lo

    def prepare_factor(i, k):
        pair = i * (i - 1) // 2 + k

        passes_on = -1 if i == 1 else (i + 2) % 4

        @pl.when(n == i)
        def _():
            settle(l_buf.at[pair, :, 0], l2_r.at[pair])

        @pl.when(jnp.logical_and(n != i, n != passes_on))
        def _():
            settle(l_buf.at[pair], l2_r.at[pair])
        hi, lo = split(l_buf[pair].reshape(256, 128))
        w_l[pair, :, 0:128] = hi
        w_l[pair, :, 128:256] = lo

    def fold(d):
        return (d[0:16, 0:128] + d[16:32, 128:256]) + (d[0:16, 128:256] + d[16:32, 0:128])

    def stacked(v):
        hi, lo = split(v)
        return jnp.concatenate([hi, lo], axis=0)

    def apply_inverse(i, r):
        return fold(lax.dot_general(stacked(r), w_inv[i], (((1,), (1,)), ((), ())), preferred_element_type=F32))

    def apply_factor(i, k):
        pair = i * (i - 1) // 2 + k
        return fold(jnp.dot(y_hl[k], w_l[pair], preferred_element_type=F32))

    def spread_cases(piece):
        at = pl.ds(pl.multiple_of(z * 16, 16), 16)
        spread[at, :] = piece
        return spread[...].T

    def send_x(i, partial):
        x_src[i] = partial
        x_buf[i, c * 4 + x] = partial
        for d, e in ring:
            send(x_src.at[i], x_buf.at[i, c * 4 + x], x_sem.at[0, i], x_sem.at[1, i],
                 dev(zh, lax.rem(x + d, 4), y, lax.rem(c + e, 2), n))

    def send_y(i, partial):
        y_src[i] = partial
        y_buf[i, c * 4 + y] = partial
        for d, e in ring:
            send(y_src.at[i], y_buf.at[i, c * 4 + y], y_sem.at[0, i], y_sem.at[1, i],
                 dev(zh, x, lax.rem(y + d, 4), lax.rem(c + e, 2), n))

    def halves(buf, i):
        return [(buf[i, 4 * h] + buf[i, 4 * h + 1]) + (buf[i, 4 * h + 2] + buf[i, 4 * h + 3]) for h in range(2)]

    def solved_parts(i):
        settle(x_buf.at[i, pl.ds(0, 7)], x_sem.at[1, i])
        parts = halves(x_buf, i)
        y_hl[i] = stacked(jnp.concatenate(parts, axis=1))
        return parts

    def send_out(i, parts):
        o_src[i] = spread_cases(jnp.where(c == 0, parts[0], parts[1]))
        for g in range(2):
            rows = o_src.at[i, pl.ds(pl.multiple_of((g * 4 + x) * 16, 16), 16), :]
            own_place = jnp.logical_and(n == i, zh == g)

            @pl.when(own_place)
            def _():
                o_buf[z] = o_src[i, pl.ds(pl.multiple_of((g * 4 + x) * 16, 16), 16), :]

            @pl.when(jnp.logical_not(own_place))
            def _():
                send(rows, o_buf.at[z], o_s.at[i], o_r.at[0], dev(g, x, y, c, i))

    prepare_inverse(0)
    pass_on("gather end")
    settle(p1_buf.at[pl.ds(0, 7)], p1_sem.at[1])
    lane_window = lax.broadcasted_iota(jnp.int32, (16, 128), 1) // 16

    def gathered(i):
        for h in range(2):
            first = h * 4 + i
            v = p1_buf[0]
            for k in range(1, 8):
                v = jnp.where(lane_window == (first + k) % 8, p1_buf[k], v)
            if first:
                v = pltpu.roll(v, 128 - first * 16, 1)
            g_all[i, :, h * 128:(h + 1) * 128] = v

    gathered(0)
    send_x(0, apply_inverse(0, g_all[0]))
    pass_on("x0")
    for i in range(1, 4):
        gathered(i)
    pass_on("x0 end")
    prepare_factor(1, 0)
    ahead = None
    parts = solved_parts(0)

    for i in range(1, 4):
        total = apply_factor(i, i - 1)
        if i > 1:
            total = ahead + total
        if i == 3:
            total = returned() + total
        send_y(i - 1, total)
        if i == 1:
            send_first(parts)
        send_out(i - 1, parts)
        pass_on(f"y{i - 1}")
        pass_on(f"y{i - 1} end")
        prepare_inverse(i)
        settle(y_buf.at[i - 1, pl.ds(0, 7)], y_sem.at[1, i - 1])
        sums = halves(y_buf, i - 1)
        partial = apply_inverse(i, g_all[i] - jnp.concatenate(sums, axis=1))
        if i < 3:
            send_x(i, partial)
            pass_on(f"x{i}")
            pass_on(f"x{i} end")
            for k in range(1 if i == 2 else 0, i + 1):
                prepare_factor(i + 1, k)
            ahead = apply_factor(i + 1, i - 1)
            parts = solved_parts(i)

    low = lax.rem(lax.broadcasted_iota(jnp.int32, (16, 128), 1) // 8, 2) == 0
    spread[pl.ds(pl.multiple_of(z * 16, 16), 16), :] = jnp.where(low, partial, 0.0)
    spread[pl.ds(pl.multiple_of((1 - zh) * 64 + n * 16, 16), 16), :] = jnp.where(low, 0.0, partial)
    wide_rows = spread[...].T.reshape(8, 2, 8, 128)
    f_src[...] = (wide_rows[:, 0] + wide_rows[:, 1]).reshape(64, 128)
    far = jnp.where(n < 2, zh, 1 - zh)
    for d, g in [(d, far) for d in (2, 1, 3, 0)] + [(d, 1 - far) for d in (2, 1, 3, 0)]:
        xt = lax.rem(x + d, 4)
        at = pl.ds(pl.multiple_of((g * 4 + xt) * 8, 8), 8)
        if d:
            send(f_src.at[at, :], f_buf.at[z * 4 + x], o_s.at[3], o_r.at[1], dev(g, xt, y, c, 3))
        else:
            own_place = jnp.logical_and(n == 3, zh == g)

            @pl.when(own_place)
            def _(at=at):
                f_buf[z * 4 + x] = f_src[at, :]

            @pl.when(jnp.logical_not(own_place))
            def _(at=at, xt=xt, g=g):
                send(f_src.at[at, :], f_buf.at[z * 4 + x], o_s.at[3], o_r.at[1], dev(g, xt, y, c, 3))

    def drain_weights():
        settle(inv_buf.at[0, :, pl.ds(0, 3)], i1_sem.at[0, 0])
        settle(inv_buf.at[pl.ds(1, 3), :, pl.ds(0, 3)], i1_sem.at[0, 1])

        @pl.when(jnp.logical_or(n == 0, n == 3))
        def _():
            settle(inv_buf, i2_s)

        for k in range(3):
            @pl.when(k < n)
            def _(k=k):
                settle(y_buf.at[0, pl.ds(0, 7)], l1_s.at[k])

        @pl.when(n == 1)
        def _():
            settle(inv_buf.at[:, :, pl.ds(0, 7)], l2_s.at[0])

        for i in range(2, 4):
            own = range(1, 3) if i == 3 else range(i)

            @pl.when(n == i)
            def _(own=own):
                for k in own:
                    settle(l_buf.at[pl.ds(0, 2)], l2_s.at[k])

            @pl.when(n == (i + 2) % 4)
            def _(own=own):
                for k in own:
                    settle(inv_buf.at[:, :, pl.ds(0, 3)], l3_s.at[k])

        @pl.when(n == 3)
        def _():
            settle(away_src.at[0], away_sem.at[0])
            settle(away_buf.at[pl.ds(0, 7)], back_sem.at[0])

        @pl.when(n != 3)
        def _():
            settle(away_src, away_sem.at[0])

    drain_weights()
    settle(p0_buf.at[pl.ds(0, 7)], p0_sem.at[0])
    settle(p1_buf.at[pl.ds(0, 7)], p1_sem.at[0])
    for i in range(3):
        settle(x_buf.at[i, pl.ds(0, 7)], x_sem.at[0, i])
        settle(y_buf.at[i, pl.ds(0, 7)], y_sem.at[0, i])

    for i in range(4):
        count = 2 if i < 3 else 8
        sized = o_buf if i < 3 else f_buf

        @pl.when(n == i)
        def _(i=i, count=count, sized=sized):
            settle(sized.at[pl.ds(0, count - 1)], o_s.at[i])

        @pl.when(n != i)
        def _(i=i, count=count, sized=sized):
            settle(sized.at[pl.ds(0, count)], o_s.at[i])

    @pl.when(n < 3)
    def _():
        settle(o_buf.at[pl.ds(0, 7)], o_r.at[0])
        total = o_buf[0]
        for k in range(1, 8):
            total = total + o_buf[k]
        out_ref[...] = total

    @pl.when(n == 3)
    def _():
        settle(f_buf.at[pl.ds(0, 31)], o_r.at[1])
        groups = []
        for first in (0, 16):
            total = f_buf[first]
            for k in range(1, 16):
                total = total + f_buf[first + k]
            groups.append(total)
        left = lax.broadcasted_iota(jnp.int32, (8, 128), 1) < 64
        out_ref[0:8, :] = jnp.where(left, groups[0], groups[1])
        out_ref[8:16, :] = pltpu.roll(jnp.where(left, groups[1], groups[0]), 64, 1)


def body(factor_rows, load_vectors, child_updates, block_inverses):
    dma = pltpu.SemaphoreType.DMA
    out = pl.pallas_call(
        kernel,
        out_shape=pltpu.VMEM((16, 128), F32),
        in_specs=[pl.BlockSpec(memory_space=pltpu.HBM)] * 4,
        out_specs=pl.BlockSpec(memory_space=pltpu.VMEM),
        scratch_shapes=[
            pltpu.VMEM((4, 16, 128), F32), pltpu.VMEM((16, 128), F32),
            pltpu.VMEM((128, 128), F32), pltpu.VMEM((128, 128), F32),
            pltpu.VMEM((8, 16, 128), F32), pltpu.VMEM((16, 128), F32), pltpu.VMEM((8, 16, 128), F32),
            pltpu.VMEM((4, 16, 256), F32),
            pltpu.VMEM((3, 16, 128), F32), pltpu.VMEM((3, 8, 16, 128), F32),
            pltpu.VMEM((3, 16, 128), F32), pltpu.VMEM((3, 8, 16, 128), F32),
            pltpu.VMEM((4, 2, 8, 16, 128), F32), pltpu.VMEM((4, 256, 256), BF16),
            pltpu.VMEM((6, 2, 2, 4, 16, 128), F32), pltpu.VMEM((6, 256, 256), BF16),
            pltpu.VMEM((3, 32, 256), BF16),
            pltpu.VMEM((128, 128), F32), pltpu.VMEM((3, 128, 128), F32),
            pltpu.VMEM((8, 16, 128), F32), pltpu.VMEM((32, 8, 128), F32), pltpu.VMEM((64, 128), F32),
            pltpu.VMEM((2, 16, 128), F32), pltpu.VMEM((8, 16, 128), F32),
            pltpu.VMEM((128, 128), F32), pltpu.VMEM((2, 16, 128), F32),
            dma((7,)), dma((2,)), dma((2,)), dma((2, 3)), dma((2, 3)), dma((2, 2)),
            dma, dma((4,)), dma((3,)), dma((3,)), dma((3,)), dma((6,)), dma((3,)), dma((2,)), dma((2,)), dma((4,)), dma((2,)),
        ],
        compiler_params=pltpu.CompilerParams(collective_id=0, has_side_effects=True, vmem_limit_bytes=60 << 20),
        name="substitution",
    )(
        block_inverses,
        factor_rows.reshape(4, 16, 1024),
        load_vectors.reshape(16, 128),
        child_updates.reshape(4, 16, 128),
    )
    return out.reshape(1, 1, 16, 128)


def solution(mesh):
    placed = (
        P(None, "narrow", None, "wide", None, None),
        P(None, "narrow", "wide", None),
        P("narrow", None, None, "wide", None),
        P(None, "wide", None),
    )
    return jax.shard_map(
        body, mesh=mesh, in_specs=placed, out_specs=P(None, "narrow", "wide", None), check_vma=False
    )
```
